128 devices in a mesh: batch: 32 (over z, y, core), rows: 4 (over x).
Axes of the slice: x: 4, y: 4, z: 4, core: 2. Of those that a mesh axis runs over, the one named last changes fastest.
Arguments:
- features: bfloat16 [768, 14, 14, 1024], P(('batch', 'rows')), may hold values from -12 to 12
- grads: bfloat16 [768, 14, 14, 256], P(('batch', 'rows')), may hold values from -12 to 12
- kernel: bfloat16 [3, 3, 256, 1024], replicated, may hold values from -0.125 to 0.125
- vectors: float32 [16, 64, 64], replicated, may hold values from -1 to 1, as said below
- values: float32 [16, 64], replicated, may hold values from 0.05 to 2
Outputs:
- input_grad: bfloat16 [768, 14, 14, 1024], P(('batch', 'rows'))
- kernel_grad: float32 [1024, 3, 3, 256], P(('batch', 'rows'))
The draws below stay inside these ranges and needn't reach their ends.
Inputs may be any that keep to these rules, and one draw needn't show every extreme that they name: `vectors`: each group's matrix is orthogonal.
All inputs are finite; a program needn't handle non-finite values.
Results may differ from the reference program's by a relative error of at most 0.015.
Values sent between devices are 32-bit elements; how exact they have to be, the bound alone decides.
No kernel may reach another device: no remote copies, remote signals or barrier semaphores. Data moves between devices by JAX's collectives and lax.ppermute only.
A program may use at most 128 MiB of HBM per device.

```python
import math
import jax
import jax.numpy as jnp
from jax import lax

D = 1024
GSIZE = 64
COUT = 256
WD = 14
HEIGHT = 14
IMG_DEV = 6
GROUPS = 16
IMAGES = 768
DEVICES = 128


def draw_features(key, part):
    key_offset, key_spread, key_noise = jax.random.split(jax.random.fold_in(key, 11), 3)
    offsets = 0.5 * jax.random.normal(key_offset, (D,), jnp.float32)
    spread = jnp.exp(jax.random.uniform(key_spread, (D,), jnp.float32, math.log(0.5), math.log(2.0)))
    ramp = 1.0 + 2.0 * jnp.arange(IMAGES, dtype=jnp.float32) / max(IMAGES - 1, 1)
    noise = jax.random.normal(key_noise, (IMAGES, HEIGHT, WD, D), jnp.float32)
    result = offsets * ramp[:, None, None, None] + spread * noise
    return jnp.clip(result, -12.0, 12.0).astype(jnp.bfloat16)


def draw_grads(key, part):
    key_offset, key_spread, key_noise = jax.random.split(jax.random.fold_in(key, 23), 3)
    offsets = 0.3 * jax.random.normal(key_offset, (COUT,), jnp.float32)
    spread = jnp.exp(jax.random.uniform(key_spread, (COUT,), jnp.float32, math.log(0.5), math.log(2.0)))
    ramp = 1.0 + 2.0 * jnp.arange(IMAGES, dtype=jnp.float32) / max(IMAGES - 1, 1)
    noise = jax.random.normal(key_noise, (IMAGES, HEIGHT, WD, COUT), jnp.float32)
    result = offsets * ramp[:, None, None, None] + spread * noise
    return jnp.clip(result, -12.0, 12.0).astype(jnp.bfloat16)


def draw_vectors(key, part):
    matrices = jax.random.normal(jax.random.fold_in(key, 37), (GROUPS, GSIZE, GSIZE), jnp.float32)
    basis, unused = jnp.linalg.qr(matrices)
    return basis.astype(jnp.float32)


def normal_values(rng, shape, deviation, most, kind=jnp.bfloat16):
    return jnp.clip(deviation * jax.random.normal(rng, shape, jnp.float32), -most, most).astype(kind)


def setup_inputs(seed: int = 0) -> dict:
    keys = jax.random.split(jax.random.key(seed), 6)
    features = draw_features(jax.random.fold_in(keys[5], 71), 0)
    grads = draw_grads(jax.random.fold_in(keys[5], 71), 0)
    kernel = normal_values(keys[2], (3, 3, COUT, D), (9 * COUT) ** -0.5, 0.125)
    vectors = draw_vectors(jax.random.fold_in(keys[5], 71), 0)
    values = jnp.clip(jnp.exp(jax.random.uniform(keys[4], (GROUPS, GSIZE), jnp.float32, math.log(0.05), math.log(2.0))), 0.05, 2.0)
    return {"features": features, "grads": grads, "kernel": kernel, "vectors": vectors, "values": values}


highest = lax.Precision.HIGHEST

def whitening(vectors, values):
    scales = lax.rsqrt(values)
    whiten = jnp.einsum('gij,gj,gkj->gik', vectors, scales, vectors, precision=highest)
    return (scales, whiten)

def block_matrix(blocks):
    groups, group_size = (blocks.shape[0], blocks.shape[1])
    identity = jnp.eye(groups, dtype=jnp.float32)
    full = jnp.einsum('gh,gij->gihj', identity, blocks, precision=highest)
    return full.reshape(groups * group_size, groups * group_size)

def diagonal_blocks(full, groups, group_size):
    shaped = full.reshape(groups, group_size, groups, group_size)
    index = jnp.arange(groups)
    return shaped[index, :, index, :]

def gather_columns(padded, slab_rows, columns_count):
    outputs = padded.shape[3]
    pieces = [padded[:, 2 - shift_row:2 - shift_row + slab_rows, 2 - shift_col:2 - shift_col + columns_count, :] for shift_row in range(3) for shift_col in range(3)]
    return jnp.concatenate(pieces, axis=3).reshape(-1, 9 * outputs)

def reference(features, grads, kernel, vectors, values):
    group_size = values.shape[1]
    groups = values.shape[0]
    channels = features.shape[3]
    outputs = grads.shape[3]
    pixel_total = 1.0 * features.shape[0] * features.shape[1] * features.shape[2]
    feature_blocks = features.reshape(DEVICES, IMG_DEV, HEIGHT, WD, channels)
    grad_blocks = grads.reshape(DEVICES, IMG_DEV, HEIGHT, WD, outputs)
    kernel_flat = kernel.reshape(9 * outputs, channels)
    scales, whiten = whitening(vectors, values)
    whiten_low = block_matrix(whiten).astype(jnp.bfloat16)

    def add_sums(carry, block):
        return (carry + lax.optimization_barrier(jnp.sum(block.reshape(-1, channels), axis=0, dtype=jnp.float32)), None)
    sum_feature, unused = lax.scan(add_sums, jnp.zeros((channels,), jnp.float32), feature_blocks)
    channel_mean = sum_feature / pixel_total

    def block_terms(feature_block, grad_block):
        flat = feature_block.reshape(-1, channels)
        centered_low = (flat.astype(jnp.float32) - channel_mean).astype(jnp.bfloat16)
        padded = jnp.pad(grad_block, ((0, 0), (1, 1), (1, 1), (0, 0)))
        columns = gather_columns(padded, HEIGHT, WD)
        back_grad = jnp.dot(columns.astype(jnp.float32), kernel_flat.astype(jnp.float32), preferred_element_type=jnp.float32)
        return (flat, centered_low, columns, back_grad)

    def accumulate(carry, blocks):
        cov_part, back_part, weight_part = carry
        flat, centered_low, columns, back_grad = block_terms(blocks[0], blocks[1])
        whitened = jnp.dot(centered_low.astype(jnp.float32), whiten_low.astype(jnp.float32), preferred_element_type=jnp.float32).astype(jnp.bfloat16)
        back_low = back_grad.astype(jnp.bfloat16)
        cov_part = cov_part + lax.dot_general(flat.astype(jnp.float32), back_low.astype(jnp.float32), (((0,), (0,)), ((), ())), preferred_element_type=jnp.float32)
        back_part = back_part + lax.optimization_barrier(jnp.sum(back_grad, axis=0))
        weight_part = weight_part + lax.dot_general(whitened.astype(jnp.float32), columns.astype(jnp.float32), (((0,), (0,)), ((), ())), preferred_element_type=jnp.float32)
        return ((cov_part, back_part, weight_part), None)
    start_carry = (jnp.zeros((channels, channels), jnp.float32), jnp.zeros((channels,), jnp.float32), jnp.zeros((channels, 9 * outputs), jnp.float32))
    totals, unused = lax.scan(accumulate, start_carry, (feature_blocks, grad_blocks))
    raw_full, back_total, weight_total = totals
    raw_cov = diagonal_blocks(raw_full, groups, group_size)
    cov_grad = raw_cov - channel_mean.reshape(groups, group_size)[:, :, None] * back_total.reshape(groups, group_size)[:, None, :]
    rotated = jnp.einsum('gki,gkl,glj->gij', vectors, cov_grad, vectors, precision=highest)
    symmetric = 0.5 * (rotated + jnp.swapaxes(rotated, 1, 2))
    roots = jnp.sqrt(values)
    factor = -(scales[:, :, None] * scales[:, None, :]) / (roots[:, :, None] + roots[:, None, :])
    sigma_grad = jnp.einsum('gik,gkl,gjl->gij', vectors, symmetric * factor, vectors, precision=highest)
    sigma_low = block_matrix(2.0 / pixel_total * sigma_grad).astype(jnp.bfloat16)
    stacked = jnp.concatenate([whiten_low, sigma_low], axis=0)

    def input_block(blocks):
        flat, centered_low, columns, back_grad = block_terms(blocks[0], blocks[1])
        shifted_low = (back_grad - back_total / pixel_total).astype(jnp.bfloat16)
        joined = jnp.concatenate([shifted_low, centered_low], axis=1)
        result = jnp.dot(joined.astype(jnp.float32), stacked.astype(jnp.float32), preferred_element_type=jnp.float32)
        return result.reshape(IMG_DEV, HEIGHT, WD, channels).astype(jnp.bfloat16)
    input_grad = lax.map(input_block, (feature_blocks, grad_blocks)).reshape(features.shape)
    kernel_grad = weight_total.reshape(channels, 3, 3, outputs)
    return (input_grad, kernel_grad)
```

```python
import jax
import jax.numpy as jnp
import numpy as np
from jax import lax
from jax.experimental import pallas as pl
from jax.experimental.pallas import tpu as pltpu
from jax.sharding import Mesh
from jax.sharding import PartitionSpec as P

ALL = ("z", "y", "c", "x")
SIZE = {"z": 4, "y": 4, "c": 2, "x": 4}
STRIDE = {"z": 32, "y": 8, "c": 4, "x": 1}
RING = ((0, 3, 1, 2), (0, 1, 3, 2))
F32 = jnp.float32
BF16 = jnp.bfloat16
HIGHEST = lax.Precision.HIGHEST
IMAGES, H, W, D, O = 6, 14, 14, 1024, 256
ROWS = IMAGES * H * 16
PIXELS = IMAGES * H * W
TOTAL = 128.0 * PIXELS
VMEM_LIMIT = 60 << 20


def nt(a, b, precision=None):
    return lax.dot_general(
        a, b, (((1,), (1,)), ((), ())), precision=precision, preferred_element_type=F32
    )


def tn(a, b, precision=None):
    return lax.dot_general(
        a, b, (((0,), (0,)), ((), ())), precision=precision, preferred_element_type=F32
    )


def nn(a, b, precision=None):
    return lax.dot_general(
        a, b, (((1,), (0,)), ((), ())), precision=precision, preferred_element_type=F32
    )


def same_group(shape):
    row = lax.broadcasted_iota(jnp.int32, shape, 0)
    col = lax.broadcasted_iota(jnp.int32, shape, 1)
    return lax.div(row, 64) == lax.div(col, 64)


def block_vectors(vectors_ref, z):
    four = vectors_ref[4 * z : 4 * z + 4].reshape(256, 64)
    wide = jnp.concatenate([four, four, four, four], axis=1)
    return jnp.where(same_group((256, 256)), wide, 0.0)


def as_column(row):
    return jnp.broadcast_to(row, (256, 256)).T


def prep_kernel(
    features, grads, vectors, values, cols, xc, wht, u, sums, whiten, wide, wp32
):
    for z in range(4):
        basis = block_vectors(vectors, z)
        scale = lax.rsqrt(values[0:1, 256 * z : 256 * z + 256])
        full = nt(basis * scale, basis, HIGHEST)
        whiten[z] = full.astype(BF16)
        for c in range(2):
            spot = RING[c].index(z)
            for row, (y, x) in enumerate((y, x) for y in RING[c] for x in RING[c]):
                channel = y * 64 + c * 32 + x * 8
                wp32[4 * c + spot, row * 8 : row * 8 + 8, :] = full[channel : channel + 8, :]
    wide[...] = jnp.zeros_like(wide)
    inside = lax.broadcasted_iota(jnp.int32, (H, 16, O), 1) < W
    for b in range(IMAGES):
        wide[:, 8 : 8 + W, :] = grads[b].astype(F32)
        for c in range(3):
            shifted = wide[:, 9 - c : 25 - c, :]
            if c == 2:
                shifted = jnp.where(inside, shifted, 0.0)
            shifted = shifted.astype(BF16)
            for a in range(3):
                lane = (3 * a + c) * O
                first, last = b * H + max(0, a - 1), b * H + H - max(0, 1 - a)
                start = max(0, 1 - a)
                cols[first:last, :, lane : lane + O] = shifted[start : start + last - first]
                if a == 0:
                    cols[b * H + H - 1, :, lane : lane + O] = jnp.zeros((16, O), BF16)
                if a == 2:
                    cols[b * H, :, lane : lane + O] = jnp.zeros((16, O), BF16)
    total = jnp.zeros((1, D), F32)
    for b in range(IMAGES):
        total = total + jnp.sum(
            jnp.sum(features[b].astype(F32), axis=0), axis=0, keepdims=True
        )
    sums[...] = total
    mean = total * (1.0 / PIXELS)
    xc[...] = jnp.zeros_like(xc)
    for b in range(IMAGES):
        xc[b * H : b * H + H, 0:W, :] = (features[b].astype(F32) - mean[None]).astype(BF16)
    high = mean.astype(BF16)
    rest = mean - high.astype(F32)
    middle = rest.astype(BF16)
    low = (rest - middle.astype(F32)).astype(BF16)
    pad = lax.broadcasted_iota(jnp.int32, (16, D), 0)
    head = xc[0].astype(F32)
    head = jnp.where(pad == 14, high.astype(F32), jnp.where(pad == 15, middle.astype(F32), head))
    xc[0] = head.astype(BF16)
    head = xc[1].astype(F32)
    xc[1] = jnp.where(pad == 14, low.astype(F32), head).astype(BF16)
    for k in range(8):
        c, spot = k // 4, k % 4
        z = RING[c][spot]
        chunk = xc[:, :, 256 * z : 256 * z + 256].reshape(ROWS, 256)
        part = nt(wp32[k].astype(BF16), chunk)
        wht[128 * k : 128 * k + 128, :] = part.astype(BF16)
        shift = part[:, 14:15] + part[:, 15:16] + part[:, 30:31]
        u[128 * k : 128 * k + 128, :] = jnp.broadcast_to(shift, (128, 128))
    wht[1024:1040, :] = jnp.ones((16, ROWS), BF16)


def prep(features, grads, vectors, values):
    return pl.pallas_call(
        prep_kernel,
        out_shape=(
            jax.ShapeDtypeStruct((IMAGES * H, 16, 9 * O), BF16),
            jax.ShapeDtypeStruct((IMAGES * H, 16, D), BF16),
            jax.ShapeDtypeStruct((1040, ROWS), BF16),
            jax.ShapeDtypeStruct((1024, 128), F32),
            jax.ShapeDtypeStruct((1, D), F32),
            jax.ShapeDtypeStruct((4, 256, 256), BF16),
        ),
        scratch_shapes=[pltpu.VMEM((H, 32, O), F32), pltpu.VMEM((8, 128, 256), F32)],
        compiler_params=pltpu.CompilerParams(vmem_limit_bytes=VMEM_LIMIT),
        name="prep",
    )(features, grads, vectors, values)


def weight_kernel(wht, cols, u, out, colsum):
    full = nn(wht[...], cols[...])
    ones = full[1024:1032, :]
    colsum[...] = ones
    for k in range(6):
        lanes = slice(128 * k, 128 * k + 128)
        out[:, lanes] = full[0:1024, lanes] + u[...] * ones[0:1, lanes]


def weight_part(wht, cols, u, a):
    return pl.pallas_call(
        weight_kernel,
        grid=(1,),
        in_specs=[
            pl.BlockSpec((1040, ROWS), lambda i: (0, 0)),
            pl.BlockSpec((ROWS, 768), lambda i: (0, a)),
            pl.BlockSpec((1024, 128), lambda i: (0, 0)),
        ],
        out_specs=(
            pl.BlockSpec((1024, 768), lambda i: (0, 0)),
            pl.BlockSpec((8, 768), lambda i: (0, 0)),
        ),
        out_shape=(
            jax.ShapeDtypeStruct((1024, 768), F32),
            jax.ShapeDtypeStruct((8, 768), F32),
        ),
        compiler_params=pltpu.CompilerParams(vmem_limit_bytes=VMEM_LIMIT),
        name="weight_part",
    )(wht, cols, u)


def back_kernel(cols, kernel, xc, sums, sum0, sum1, sum2, dev, payload):
    z = pl.program_id(0)
    back = nn(cols[...], kernel[...])
    total = jnp.sum(back, axis=0, keepdims=True)
    real = lax.rem(lax.broadcasted_iota(jnp.int32, (ROWS, 256), 0), 16) < W
    low = jnp.where(real, back - total * (1.0 / PIXELS), 0.0).astype(BF16)
    dev[...] = low
    cov = tn(xc[...], low) + as_column(sums[...] * (1.0 / PIXELS)) * total
    group = lax.div(lax.broadcasted_iota(jnp.int32, (64, 256), 1), 64)
    packed = cov[0:64]
    for k in range(1, 4):
        packed = jnp.where(group == k, cov[64 * k : 64 * k + 64], packed)
    payload[0:64, :] = packed
    row = lax.broadcasted_iota(jnp.int32, (8, 256), 0)
    tail = jnp.where(row == 0, total, jnp.where(row == 1, sums[...], 0.0))
    for a, part in enumerate((sum0, sum1, sum2)):
        tail = jnp.where((row == 2 + a) & (z < 3), part[0:1, :], tail)
    payload[64:72, :] = tail


def back_part(cols, kernel, xc, sums, parts):
    last = lambda z: (0, jnp.minimum(z, 2))
    column = lambda z: (0, z)
    return pl.pallas_call(
        back_kernel,
        grid=(4,),
        in_specs=[
            pl.BlockSpec((ROWS, 9 * O), lambda z: (0, 0)),
            pl.BlockSpec((9 * O, 256), column),
            pl.BlockSpec((ROWS, 256), column),
            pl.BlockSpec((1, 256), column),
            pl.BlockSpec((8, 256), last),
            pl.BlockSpec((8, 256), last),
            pl.BlockSpec((8, 256), last),
        ],
        out_specs=(pl.BlockSpec((ROWS, 256), column), pl.BlockSpec((72, 256), column)),
        out_shape=(
            jax.ShapeDtypeStruct((ROWS, D), BF16),
            jax.ShapeDtypeStruct((72, D), F32),
        ),
        compiler_params=pltpu.CompilerParams(vmem_limit_bytes=VMEM_LIMIT),
        name="back_part",
    )(cols, kernel, xc, sums, *parts)


def final_kernel(
    dev, xc, payload, own, vectors, values, whiten, out, shift, sigma, row_vector
):
    @pl.when(pl.program_id(0) == 0)
    def _():
        for z in range(4):
            lanes = slice(256 * z, 256 * z + 256)
            basis = block_vectors(vectors, z)
            total = payload[64:65, lanes]
            mean = payload[65:66, lanes] * (1.0 / TOTAL)
            same = same_group((256, 256))
            stack = payload[0:64, lanes]
            raw = jnp.concatenate([stack, stack, stack, stack], axis=0)
            cov = jnp.where(same, raw - as_column(mean) * total, 0.0)
            rotated = nn(tn(basis, cov, HIGHEST), basis, HIGHEST)
            symmetric = 0.5 * (rotated + rotated.T)
            value = values[0:1, lanes]
            scale, root = lax.rsqrt(value), jnp.sqrt(value)
            factor = -(as_column(scale) * scale) / (as_column(root) + root)
            inner = jnp.where(same, symmetric * factor, 0.0)
            grad = nt(nn(basis, inner, HIGHEST), basis, HIGHEST)
            low = (grad * (2.0 / TOTAL)).astype(BF16)
            sigma[z] = low
            whiten_z = whiten[z].astype(F32)
            own_total, own_mean = own[64:65, lanes], own[65:66, lanes] * (1.0 / PIXELS)
            eight = lambda row: jnp.broadcast_to(row, (8, 256))
            row_vector[0:8, lanes] = nn(
                eight(own_total * (1.0 / PIXELS) - total * (1.0 / TOTAL)), whiten_z, HIGHEST
            ) + nn(eight(own_mean - mean), low.astype(F32), HIGHEST)
            shift[0:8, lanes] = nn(eight(mean), whiten_z, HIGHEST)

    for z in range(4):
        lanes = slice(256 * z, 256 * z + 256)
        result = nn(dev[:, lanes], whiten[z]) + nn(xc[:, lanes], sigma[z])
        result = result + row_vector[0:1, lanes]
        out[0, :, :, lanes] = result.astype(BF16).reshape(H, 16, 256)[:, 0:W, :]


def final_part(dev, xc, payload, own, vectors, values, whiten):
    return pl.pallas_call(
        final_kernel,
        grid=(IMAGES,),
        in_specs=[
            pl.BlockSpec((H * 16, D), lambda b: (b, 0)),
            pl.BlockSpec((H * 16, D), lambda b: (b, 0)),
            pl.BlockSpec((72, D), lambda b: (0, 0)),
            pl.BlockSpec((72, D), lambda b: (0, 0)),
            pl.BlockSpec((16, 64, 64), lambda b: (0, 0, 0)),
            pl.BlockSpec((1, D), lambda b: (0, 0)),
            pl.BlockSpec((4, 256, 256), lambda b: (0, 0, 0)),
        ],
        out_specs=(
            pl.BlockSpec((1, H, W, D), lambda b: (b, 0, 0, 0)),
            pl.BlockSpec((8, D), lambda b: (0, 0)),
        ),
        out_shape=(
            jax.ShapeDtypeStruct((IMAGES, H, W, D), BF16),
            jax.ShapeDtypeStruct((8, D), F32),
        ),
        scratch_shapes=[pltpu.VMEM((4, 256, 256), BF16), pltpu.VMEM((8, D), F32)],
        compiler_params=pltpu.CompilerParams(vmem_limit_bytes=VMEM_LIMIT),
        name="final_part",
    )(dev, xc, payload, own, vectors, values, whiten)


def permutation(move):
    pairs = []
    for device in range(128):
        at = {k: (device // STRIDE[k]) % SIZE[k] for k in ALL}
        move(at)
        pairs.append((device, sum(at[k] * STRIDE[k] for k in ALL)))
    return pairs


def exchange(value, move):
    return lax.ppermute(value, ALL, permutation(move))


def other_core(at):
    at["c"] ^= 1


def ring(axis, step):
    def move(at):
        at[axis] ^= (1, 3)[(step + at["c"]) % 2]

    return move


def split(value, dim, bit):
    keep = lax.dynamic_index_in_dim(value, bit, dim, keepdims=False)
    send = lax.dynamic_index_in_dim(value, 1 - bit, dim, keepdims=False)
    return keep, send


def local(features, grads, kernel, vectors, values):
    core = lax.axis_index("c")
    bits = {}
    for axis in "xyz":
        i = lax.axis_index(axis)
        a, b = (i ^ (i >> 1)) & 1, i >> 1
        bits[axis] = (jnp.where(core == 0, a, b), jnp.where(core == 0, b, a))
    flat_values = values.reshape(1, D)
    cols, xc, wht, u, sums, whiten = prep(features, grads, vectors, flat_values)
    cols, xc = cols.reshape(ROWS, 9 * O), xc.reshape(ROWS, D)

    parts, colsums = [], []
    for a in range(3):
        part, colsum = weight_part(wht, cols, u, a)
        colsums.append(colsum)
        keep, send = split(part.reshape(2, 512, 768), 0, core)
        parts.append((keep + exchange(send, other_core)).reshape(2, 2, 2, 2, 2, 2, 8, 768))
    dev, own = back_part(cols, kernel.reshape(9 * O, D), xc, sums, colsums)

    low, high = own[:, :512], own[:, 512:]
    mine = jnp.where(core == 0, low, high) + exchange(
        jnp.where(core == 0, high, low), other_core
    )
    for axis in "xyz":
        for step in range(2):
            mine = mine + exchange(mine, ring(axis, step))
    theirs = exchange(mine, other_core)
    payload = jnp.concatenate(
        [jnp.where(core == 0, mine, theirs), jnp.where(core == 0, theirs, mine)], axis=1
    )

    names = [["z1", "z2", "y1", "y2", "x1", "x2"] for _ in range(3)]
    for turn in range(3):
        parts = list(lax.optimization_barrier(tuple(parts)))
        for a in range(3):
            axis = "xyz"[(a + turn) % 3]
            dim = names[a].index(axis + "1")
            names[a].pop(dim)
            keep, send = split(parts[a], dim, bits[axis][0])
            parts[a] = keep + exchange(send, ring(axis, 0))
    share = jnp.stack(parts, axis=3)
    order = ["z", "y", "x"]
    for axis in "xyz":
        dim = order.index(axis)
        order.pop(dim)
        keep, send = split(share, dim, bits[axis][1])
        share = keep + exchange(send, ring(axis, 1))

    input_grad, shift = final_part(dev, xc, payload, own, vectors, flat_values, whiten)
    me = lax.axis_index(ALL)
    mine8 = lax.dynamic_slice(shift, (0, me * 8), (1, 8)).reshape(1, 8, 1)
    share = share - mine8 * payload[66:69, None, :768]
    kernel_grad = share.transpose(1, 0, 2).reshape(8, 3, 3, O)
    return input_grad, kernel_grad


def solution(mesh):
    finer = Mesh(mesh.devices.reshape(4, 4, 2, 4), ALL)
    split_all = P(ALL, None, None, None)
    return jax.shard_map(
        local,
        mesh=finer,
        in_specs=(split_all, split_all, P(), P(), P()),
        out_specs=(split_all, split_all),
        check_vma=False,
    )
```

```python
import functools

import jax
import jax.numpy as jnp
import numpy as np
from jax import lax
from jax.experimental import pallas as pl
from jax.experimental.pallas import tpu as pltpu
from jax.sharding import Mesh
from jax.sharding import PartitionSpec as P

ALL = ("z", "y", "c", "x")
SIZE = {"z": 4, "y": 4, "c": 2, "x": 4}
STRIDE = {"z": 32, "y": 8, "c": 4, "x": 1}
RING = ((0, 3, 1, 2), (0, 1, 3, 2))
F32 = jnp.float32
BF16 = jnp.bfloat16
HIGHEST = lax.Precision.HIGHEST
IMAGES, H, W, D, O = 6, 14, 14, 1024, 256
ROWS = IMAGES * H * 16
PIXELS = IMAGES * H * W
TOTAL = 128.0 * PIXELS
ON_CHIP = pl.BlockSpec(memory_space=pltpu.VMEM)


def nt(a, b, precision=None):
    return lax.dot_general(
        a, b, (((1,), (1,)), ((), ())), precision=precision, preferred_element_type=F32
    )


def tn(a, b, precision=None):
    return lax.dot_general(
        a, b, (((0,), (0,)), ((), ())), precision=precision, preferred_element_type=F32
    )


def nn(a, b, precision=None):
    return lax.dot_general(
        a, b, (((1,), (0,)), ((), ())), precision=precision, preferred_element_type=F32
    )


def same_group(shape):
    row = lax.broadcasted_iota(jnp.int32, shape, 0)
    col = lax.broadcasted_iota(jnp.int32, shape, 1)
    return lax.div(row, 64) == lax.div(col, 64)


def block_vectors(vectors_ref, z):
    four = vectors_ref[4 * z : 4 * z + 4].reshape(256, 64)
    wide = jnp.concatenate([four, four, four, four], axis=1)
    return jnp.where(same_group((256, 256)), wide, 0.0)


def as_column(row):
    return jnp.broadcast_to(row, (256, 256)).T


def place():
    core = lax.axis_index("c")
    spots = ([], [])
    for axis in "zyx":
        i = lax.axis_index(axis)
        a, b = (i ^ (i >> 1)) & 1, i >> 1
        spots[0].append(2 * a + b)
        spots[1].append(2 * b + a)
    return core, spots


def prep_kernel(
    features, grads, vectors, values, cols, xc, wht, u, sums, whiten, wide, wp32
):
    core, spots = place()
    for z in range(4):
        basis = block_vectors(vectors, z)
        scale = lax.rsqrt(values[0:1, 256 * z : 256 * z + 256])
        full = nt(basis * scale, basis, HIGHEST)
        whiten[z] = full.astype(BF16)
        for c in range(2):
            at_z, at_y, at_x = spots[c]
            for row, (y, x) in enumerate((y, x) for y in RING[c] for x in RING[c]):
                channel = y * 64 + c * 32 + x * 8
                row = pl.multiple_of(8 * (row ^ (4 * at_y + at_x)), 8)
                wp32[4 * c + z, pl.ds(row, 8), :] = full[channel : channel + 8, :]
    wide[...] = jnp.zeros_like(wide)
    inside = lax.broadcasted_iota(jnp.int32, (H, 16, O), 1) < W
    for b in range(IMAGES):
        wide[:, 8 : 8 + W, :] = grads[b].astype(F32)
        for c in range(3):
            shifted = wide[:, 9 - c : 25 - c, :]
            if c == 2:
                shifted = jnp.where(inside, shifted, 0.0)
            shifted = shifted.astype(BF16)
            for a in range(3):
                lane = (3 * a + c) * O
                first, last = b * H + max(0, a - 1), b * H + H - max(0, 1 - a)
                start = max(0, 1 - a)
                cols[first:last, :, lane : lane + O] = shifted[start : start + last - first]
                if a == 0:
                    cols[b * H + H - 1, :, lane : lane + O] = jnp.zeros((16, O), BF16)
                if a == 2:
                    cols[b * H, :, lane : lane + O] = jnp.zeros((16, O), BF16)
    total = jnp.zeros((1, D), F32)
    for b in range(IMAGES):
        total = total + jnp.sum(
            jnp.sum(features[b].astype(F32), axis=0), axis=0, keepdims=True
        )
    sums[...] = total
    mean = total * (1.0 / PIXELS)
    xc[...] = jnp.zeros_like(xc)
    for b in range(IMAGES):
        xc[b * H : b * H + H, 0:W, :] = (features[b].astype(F32) - mean[None]).astype(BF16)
    high = mean.astype(BF16)
    rest = mean - high.astype(F32)
    middle = rest.astype(BF16)
    low = (rest - middle.astype(F32)).astype(BF16)
    pad = lax.broadcasted_iota(jnp.int32, (16, D), 0)
    head = xc[0].astype(F32)
    head = jnp.where(pad == 14, high.astype(F32), jnp.where(pad == 15, middle.astype(F32), head))
    xc[0] = head.astype(BF16)
    head = xc[1].astype(F32)
    xc[1] = jnp.where(pad == 14, low.astype(F32), head).astype(BF16)
    for k in range(8):
        c, z = k // 4, k % 4
        chunk = xc[:, :, 256 * z : 256 * z + 256].reshape(ROWS, 256)
        part = nt(wp32[k].astype(BF16), chunk)
        row = 4 * (c ^ core) + (RING[c].index(z) ^ spots[c][0])
        row = pl.multiple_of(128 * row, 128)
        wht[pl.ds(row, 128), :] = part.astype(BF16)
        shift = part[:, 14:15] + part[:, 15:16] + part[:, 30:31]
        u[pl.ds(row, 128), :] = jnp.broadcast_to(shift, (128, 128))
    wht[1024:1040, :] = jnp.ones((16, ROWS), BF16)


def prep(features, grads, vectors, values):
    return pl.pallas_call(
        prep_kernel,
        out_shape=(
            jax.ShapeDtypeStruct((IMAGES * H, 16, 9 * O), BF16),
            jax.ShapeDtypeStruct((IMAGES * H, 16, D), BF16),
            jax.ShapeDtypeStruct((1040, ROWS), BF16),
            jax.ShapeDtypeStruct((1024, 128), F32),
            jax.ShapeDtypeStruct((1, D), F32),
            jax.ShapeDtypeStruct((4, 256, 256), BF16),
        ),
        in_specs=[ON_CHIP] * 4,
        out_specs=(ON_CHIP,) * 6,
        scratch_shapes=[pltpu.VMEM((H, 32, O), F32), pltpu.VMEM((8, 128, 256), F32)],
        compiler_params=pltpu.CompilerParams(vmem_limit_bytes=8 << 20),
        name="prep",
    )(features, grads, vectors, values)


def weight_kernel(a, wht, cols, u, keep, send, colsum):
    full = nn(wht[...], cols[:, 768 * a : 768 * a + 768])
    ones = full[1024:1032, :]
    colsum[...] = ones
    for k in range(6):
        lanes = slice(128 * k, 128 * k + 128)
        keep[:, lanes] = full[0:512, lanes] + u[0:512] * ones[0:1, lanes]
        send[:, lanes] = full[512:1024, lanes] + u[512:1024] * ones[0:1, lanes]


def weight_part(wht, cols, u, a):
    return pl.pallas_call(
        functools.partial(weight_kernel, a),
        in_specs=[ON_CHIP] * 3,
        out_specs=(ON_CHIP,) * 3,
        out_shape=(
            jax.ShapeDtypeStruct((512, 768), F32),
            jax.ShapeDtypeStruct((512, 768), F32),
            jax.ShapeDtypeStruct((8, 768), F32),
        ),
        compiler_params=pltpu.CompilerParams(vmem_limit_bytes=6 << 20),
        name=f"weight_part_{a}",
    )(wht, cols, u)


def back_kernel(cols, kernel, xc, sums, sum0, sum1, sum2, dev, payload):
    z = pl.program_id(0)
    back = nn(cols[...], kernel[...])
    total = jnp.sum(back, axis=0, keepdims=True)
    real = lax.rem(lax.broadcasted_iota(jnp.int32, (ROWS, 256), 0), 16) < W
    low = jnp.where(real, back - total * (1.0 / PIXELS), 0.0).astype(BF16)
    dev[...] = low
    cov = tn(xc[...], low) + as_column(sums[...] * (1.0 / PIXELS)) * total
    group = lax.div(lax.broadcasted_iota(jnp.int32, (64, 256), 1), 64)
    packed = cov[0:64]
    for k in range(1, 4):
        packed = jnp.where(group == k, cov[64 * k : 64 * k + 64], packed)
    payload[0:64, :] = packed
    row = lax.broadcasted_iota(jnp.int32, (8, 256), 0)
    tail = jnp.where(row == 0, total, jnp.where(row == 1, sums[...], 0.0))
    for a, part in enumerate((sum0, sum1, sum2)):
        tail = jnp.where((row == 2 + a) & (z < 3), part[0:1, :], tail)
    payload[64:72, :] = tail


def back_part(cols, kernel, xc, sums, parts):
    last = lambda z: (0, jnp.minimum(z, 2))
    column = lambda z: (0, z)
    return pl.pallas_call(
        back_kernel,
        grid=(4,),
        in_specs=[
            ON_CHIP,
            pl.BlockSpec((9 * O, 256), column),
            pl.BlockSpec((ROWS, 256), column),
            pl.BlockSpec((1, 256), column),
            pl.BlockSpec((8, 256), last),
            pl.BlockSpec((8, 256), last),
            pl.BlockSpec((8, 256), last),
        ],
        out_specs=(pl.BlockSpec((ROWS, 256), column), pl.BlockSpec((72, 256), column)),
        out_shape=(
            jax.ShapeDtypeStruct((ROWS, D), BF16),
            jax.ShapeDtypeStruct((72, D), F32),
        ),
        compiler_params=pltpu.CompilerParams(vmem_limit_bytes=14 << 20),
        name="back_part",
    )(cols, kernel, xc, sums, *parts)


def final_kernel(
    dev, xc, payload, own, vectors, values, whiten, out, shift, sigma, row_vector
):
    @pl.when(pl.program_id(0) == 0)
    def _():
        for z in range(4):
            lanes = slice(256 * z, 256 * z + 256)
            basis = block_vectors(vectors, z)
            total = payload[64:65, lanes]
            mean = payload[65:66, lanes] * (1.0 / TOTAL)
            same = same_group((256, 256))
            stack = payload[0:64, lanes]
            raw = jnp.concatenate([stack, stack, stack, stack], axis=0)
            cov = jnp.where(same, raw - as_column(mean) * total, 0.0)
            rotated = nn(tn(basis, cov, HIGHEST), basis, HIGHEST)
            symmetric = 0.5 * (rotated + rotated.T)
            value = values[0:1, lanes]
            scale, root = lax.rsqrt(value), jnp.sqrt(value)
            factor = -(as_column(scale) * scale) / (as_column(root) + root)
            inner = jnp.where(same, symmetric * factor, 0.0)
            grad = nt(nn(basis, inner, HIGHEST), basis, HIGHEST)
            low = (grad * (2.0 / TOTAL)).astype(BF16)
            sigma[z] = low
            whiten_z = whiten[z].astype(F32)
            own_total, own_mean = own[64:65, lanes], own[65:66, lanes] * (1.0 / PIXELS)
            eight = lambda row: jnp.broadcast_to(row, (8, 256))
            row_vector[0:8, lanes] = nn(
                eight(own_total * (1.0 / PIXELS) - total * (1.0 / TOTAL)), whiten_z, HIGHEST
            ) + nn(eight(own_mean - mean), low.astype(F32), HIGHEST)
            shift[0:8, lanes] = nn(eight(mean), whiten_z, HIGHEST)

    for z in range(4):
        lanes = slice(256 * z, 256 * z + 256)
        result = nn(dev[:, lanes], whiten[z]) + nn(xc[:, lanes], sigma[z])
        result = result + row_vector[0:1, lanes]
        out[0, :, :, lanes] = result.astype(BF16).reshape(H, 16, 256)[:, 0:W, :]


def final_part(dev, xc, payload, own, vectors, values, whiten):
    return pl.pallas_call(
        final_kernel,
        grid=(IMAGES,),
        in_specs=[
            pl.BlockSpec((H * 16, D), lambda b: (b, 0)),
            pl.BlockSpec((H * 16, D), lambda b: (b, 0)),
            pl.BlockSpec((72, D), lambda b: (0, 0)),
            pl.BlockSpec((72, D), lambda b: (0, 0)),
            pl.BlockSpec((16, 64, 64), lambda b: (0, 0, 0)),
            pl.BlockSpec((1, D), lambda b: (0, 0)),
            pl.BlockSpec((4, 256, 256), lambda b: (0, 0, 0)),
        ],
        out_specs=(
            pl.BlockSpec((1, H, W, D), lambda b: (b, 0, 0, 0)),
            pl.BlockSpec((8, D), lambda b: (0, 0)),
        ),
        out_shape=(
            jax.ShapeDtypeStruct((IMAGES, H, W, D), BF16),
            jax.ShapeDtypeStruct((8, D), F32),
        ),
        scratch_shapes=[pltpu.VMEM((4, 256, 256), BF16), pltpu.VMEM((8, D), F32)],
        compiler_params=pltpu.CompilerParams(vmem_limit_bytes=10 << 20),
        name="final_part",
    )(dev, xc, payload, own, vectors, values, whiten)


def permutation(move):
    pairs = []
    for device in range(128):
        at = {k: (device // STRIDE[k]) % SIZE[k] for k in ALL}
        move(at)
        pairs.append((device, sum(at[k] * STRIDE[k] for k in ALL)))
    return pairs


def exchange(value, move):
    return lax.ppermute(value, ALL, permutation(move))


def other_core(at):
    at["c"] ^= 1


def ring(axis, step):
    def move(at):
        at[axis] ^= (1, 3)[(step + at["c"]) % 2]

    return move


def halves(value, dim):
    pick = lambda k: lax.index_in_dim(value, k, dim, keepdims=False)
    return pick(0), pick(1)


def local(features, grads, kernel, vectors, values):
    core = lax.axis_index("c")
    flat_values = values.reshape(1, D)
    cols, xc, wht, u, sums, whiten = prep(features, grads, vectors, flat_values)
    cols, xc = cols.reshape(ROWS, 9 * O), xc.reshape(ROWS, D)

    parts, colsums = [], []
    for a in range(3):
        keep, send, colsum = weight_part(wht, cols, u, a)
        colsums.append(colsum)
        parts.append((keep + exchange(send, other_core)).reshape(2, 2, 2, 2, 2, 2, 8, 768))
    dev, own = back_part(cols, kernel.reshape(9 * O, D), xc, sums, colsums)

    low, high = own[:, :512], own[:, 512:]
    mine = jnp.where(core == 0, low, high) + exchange(
        jnp.where(core == 0, high, low), other_core
    )
    for axis in "xyz":
        for step in range(2):
            mine = mine + exchange(mine, ring(axis, step))
    theirs = exchange(mine, other_core)
    payload = jnp.concatenate(
        [jnp.where(core == 0, mine, theirs), jnp.where(core == 0, theirs, mine)], axis=1
    )

    names = [["z1", "z2", "y1", "y2", "x1", "x2"] for _ in range(3)]
    for turn in range(3):
        parts = list(lax.optimization_barrier(tuple(parts)))
        for a in range(3):
            axis = "xyz"[(a + turn) % 3]
            dim = names[a].index(axis + "1")
            names[a].pop(dim)
            keep, send = halves(parts[a], dim)
            parts[a] = keep + exchange(send, ring(axis, 0))
    share = jnp.stack(parts, axis=3)
    order = ["z", "y", "x"]
    for axis in "xyz":
        dim = order.index(axis)
        order.pop(dim)
        keep, send = halves(share, dim)
        share = keep + exchange(send, ring(axis, 1))

    input_grad, shift = final_part(dev, xc, payload, own, vectors, flat_values, whiten)
    me = lax.axis_index(ALL)
    mine8 = lax.dynamic_slice(shift, (0, me * 8), (1, 8)).reshape(1, 8, 1)
    share = share - mine8 * payload[66:69, None, :768]
    kernel_grad = share.transpose(1, 0, 2).reshape(8, 3, 3, O)
    return input_grad, kernel_grad


def solution(mesh):
    finer = Mesh(mesh.devices.reshape(4, 4, 2, 4), ALL)
    split_all = P(ALL, None, None, None)
    return jax.shard_map(
        local,
        mesh=finer,
        in_specs=(split_all, split_all, P(), P(), P()),
        out_specs=(split_all, split_all),
        check_vma=False,
    )
```

```python
import functools

import jax
import jax.numpy as jnp
import numpy as np
from jax import lax
from jax.experimental import pallas as pl
from jax.experimental.pallas import tpu as pltpu
from jax.sharding import Mesh
from jax.sharding import PartitionSpec as P

ALL = ("z", "y", "c", "x")
SIZE = {"z": 4, "y": 4, "c": 2, "x": 4}
STRIDE = {"z": 32, "y": 8, "c": 4, "x": 1}
RING = ((0, 3, 1, 2), (0, 1, 3, 2))
F32 = jnp.float32
BF16 = jnp.bfloat16
IMAGES, H, W, D, O = 6, 14, 14, 1024, 256
ROWS = IMAGES * H * 16
PIXELS = IMAGES * H * W
TOTAL = 128.0 * PIXELS
ON_CHIP = pl.BlockSpec(memory_space=pltpu.VMEM)
IN_HBM = pl.BlockSpec(memory_space=pltpu.HBM)


def nt(a, b):
    return lax.dot_general(
        a, b, (((1,), (1,)), ((), ())), preferred_element_type=F32
    )


def tn(a, b):
    return lax.dot_general(
        a, b, (((0,), (0,)), ((), ())), preferred_element_type=F32
    )


def nn(a, b):
    return lax.dot_general(
        a, b, (((1,), (0,)), ((), ())), preferred_element_type=F32
    )


def same_group():
    row = lax.broadcasted_iota(jnp.int32, (256, 256), 0)
    col = lax.broadcasted_iota(jnp.int32, (256, 256), 1)
    return (row >> 6) == (col >> 6)


def block_vectors(vectors, z, same):
    four = vectors[4 * z : 4 * z + 4].reshape(256, 64)
    return jnp.where(same, jnp.concatenate([four, four, four, four], axis=1), 0.0)


def value_row(values, z):
    return jnp.concatenate([values[4 * z + g : 4 * z + g + 1, :] for g in range(4)], axis=1)


def columns_of(rows):
    rows = rows + [jnp.zeros((1, 256), F32)] * (8 - len(rows))
    return jnp.concatenate(rows, axis=0).T


def pieces(a, n):
    out = []
    for _ in range(n):
        out.append(a.astype(BF16))
        a = a - out[-1].astype(F32)
    return out


def fine(dot, a, b):
    a_high, a_low = pieces(a, 2)
    b_high, b_low = pieces(b, 2)
    return dot(a_high, b_high) + (dot(a_high, b_low) + dot(a_low, b_high))


def place():
    core = lax.axis_index("c")
    spots = ([], [])
    for axis in "zyx":
        i = lax.axis_index(axis)
        a, b = (i ^ (i >> 1)) & 1, i >> 1
        spots[0].append(2 * a + b)
        spots[1].append(2 * b + a)
    return core, spots


def prep_kernel(
    features_hbm,
    grads_hbm,
    vectors_hbm,
    values,
    cols,
    xc,
    wht,
    u,
    sums,
    whiten,
    wide,
    wp32,
    features,
    grads,
    vectors,
    arrived,
):
    copies = [
        pltpu.make_async_copy(source, target, arrived.at[k])
        for k, (source, target) in enumerate(
            ((vectors_hbm, vectors), (grads_hbm, grads), (features_hbm, features))
        )
    ]
    for copy in copies:
        copy.start()
    core, spots = place()
    same = same_group()
    wide[...] = jnp.zeros_like(wide)
    xc[...] = jnp.zeros_like(xc)
    wht[1024:1040, :] = jnp.ones((16, ROWS), BF16)
    copies[0].wait()
    for z in range(4):
        basis = block_vectors(vectors, z, same)
        scale = lax.rsqrt(value_row(values, z))
        full = fine(nt, basis * scale, basis)
        whiten[z] = full.astype(BF16)
        for c in range(2):
            at_z, at_y, at_x = spots[c]
            for row, (y, x) in enumerate((y, x) for y in RING[c] for x in RING[c]):
                channel = y * 64 + c * 32 + x * 8
                row = pl.multiple_of(8 * (row ^ (4 * at_y + at_x)), 8)
                wp32[4 * c + z, pl.ds(row, 8), :] = full[channel : channel + 8, :]
    copies[1].wait()
    inside = lax.broadcasted_iota(jnp.int32, (H, 16, O), 1) < W
    for b in range(IMAGES):
        wide[:, 8 : 8 + W, :] = grads[b].astype(F32)
        for c in range(3):
            shifted = wide[:, 9 - c : 25 - c, :]
            if c == 2:
                shifted = jnp.where(inside, shifted, 0.0)
            shifted = shifted.astype(BF16)
            for a in range(3):
                lane = (3 * a + c) * O
                first, last = b * H + max(0, a - 1), b * H + H - max(0, 1 - a)
                start = max(0, 1 - a)
                cols[first:last, :, lane : lane + O] = shifted[start : start + last - first]
                if a == 0:
                    cols[b * H + H - 1, :, lane : lane + O] = jnp.zeros((16, O), BF16)
                if a == 2:
                    cols[b * H, :, lane : lane + O] = jnp.zeros((16, O), BF16)
    copies[2].wait()
    total = jnp.zeros((1, D), F32)
    for b in range(IMAGES):
        total = total + jnp.sum(
            jnp.sum(features[b].astype(F32), axis=0), axis=0, keepdims=True
        )
    sums[...] = total
    mean = total * (1.0 / PIXELS)
    for b in range(IMAGES):
        xc[b * H : b * H + H, 0:W, :] = (features[b].astype(F32) - mean[None]).astype(BF16)
    high, middle, low = pieces(mean, 3)
    pad = lax.broadcasted_iota(jnp.int32, (16, D), 0)
    head = xc[0].astype(F32)
    head = jnp.where(pad == 14, high.astype(F32), jnp.where(pad == 15, middle.astype(F32), head))
    xc[0] = head.astype(BF16)
    head = xc[1].astype(F32)
    xc[1] = jnp.where(pad == 14, low.astype(F32), head).astype(BF16)
    for k in range(8):
        c, z = k // 4, k % 4
        chunk = xc[:, :, 256 * z : 256 * z + 256].reshape(ROWS, 256)
        part = nt(wp32[k].astype(BF16), chunk)
        row = 4 * (c ^ core) + (RING[c].index(z) ^ spots[c][0])
        row = pl.multiple_of(128 * row, 128)
        wht[pl.ds(row, 128), :] = part.astype(BF16)
        shift = part[:, 14:15] + part[:, 15:16] + part[:, 30:31]
        u[pl.ds(row, 128), :] = jnp.broadcast_to(shift, (128, 128))


def prep(features, grads, vectors, values):
    return pl.pallas_call(
        prep_kernel,
        out_shape=(
            jax.ShapeDtypeStruct((IMAGES * H, 16, 9 * O), BF16),
            jax.ShapeDtypeStruct((IMAGES * H, 16, D), BF16),
            jax.ShapeDtypeStruct((1040, ROWS), BF16),
            jax.ShapeDtypeStruct((1024, 128), F32),
            jax.ShapeDtypeStruct((1, D), F32),
            jax.ShapeDtypeStruct((4, 256, 256), BF16),
        ),
        in_specs=[IN_HBM] * 3 + [ON_CHIP],
        out_specs=(ON_CHIP,) * 6,
        scratch_shapes=[
            pltpu.VMEM((H, 32, O), F32),
            pltpu.VMEM((8, 128, 256), F32),
            pltpu.VMEM((IMAGES, H, W, D), BF16),
            pltpu.VMEM((IMAGES, H, W, O), BF16),
            pltpu.VMEM((16, 64, 64), F32),
            pltpu.SemaphoreType.DMA((3,)),
        ],
        compiler_params=pltpu.CompilerParams(vmem_limit_bytes=10 << 20),
        name="prep",
    )(features, grads, vectors, values)


def weight_kernel(a, wht, cols, u, keep, send, colsum):
    for n in range(3):
        start = 768 * a + 256 * n
        full = nn(wht[...], cols[:, start : start + 256])
        colsum[:, 256 * n : 256 * n + 256] = full[1024:1032, :]
        for k in range(2):
            ones = full[1024:1025, 128 * k : 128 * k + 128]
            lanes = slice(256 * n + 128 * k, 256 * n + 128 * k + 128)
            part = full[0:1024, 128 * k : 128 * k + 128] + u[...] * ones
            keep[:, lanes] = part[0:512]
            send[:, lanes] = part[512:1024]


def weight_part(wht, cols, u, a):
    return pl.pallas_call(
        functools.partial(weight_kernel, a),
        in_specs=[ON_CHIP] * 3,
        out_specs=(ON_CHIP,) * 3,
        out_shape=(
            jax.ShapeDtypeStruct((512, 768), F32),
            jax.ShapeDtypeStruct((512, 768), F32),
            jax.ShapeDtypeStruct((8, 768), F32),
        ),
        compiler_params=pltpu.CompilerParams(vmem_limit_bytes=6 << 20),
        name=f"weight_part_{a}",
    )(wht, cols, u)


def back_kernel(
    cols,
    kernel_hbm,
    xc,
    sums,
    sum0,
    sum1,
    sum2,
    vectors,
    values,
    dev,
    payload,
    mine,
    theirs,
    bases,
    factors,
    kernel,
    arrived,
):
    copies = [
        pltpu.make_async_copy(
            kernel_hbm.at[:, pl.ds(256 * z, 256)], kernel.at[z], arrived.at[z]
        )
        for z in range(4)
    ]
    for copy in copies:
        copy.start()
    same = same_group()
    real = (lax.broadcasted_iota(jnp.int32, (ROWS, 256), 0) & 15) < W
    group = lax.broadcasted_iota(jnp.int32, (64, 256), 1) >> 6
    row = lax.broadcasted_iota(jnp.int32, (8, 256), 0)
    for z in range(4):
        lanes = slice(256 * z, 256 * z + 256)
        copies[z].wait()
        back = nn(cols[...], kernel[z])
        total = jnp.sum(back, axis=0, keepdims=True)
        low = jnp.where(real, back - total * (1.0 / PIXELS), 0.0).astype(BF16)
        dev[:, lanes] = low
        value = value_row(values, z)
        scale, root = lax.rsqrt(value), jnp.sqrt(value)
        tall = columns_of([sums[:, lanes] * (1.0 / PIXELS), scale, root])
        cov = tn(xc[:, lanes], low) + tall[:, 0:1] * total
        packed = cov[0:64]
        for k in range(1, 4):
            packed = jnp.where(group == k, cov[64 * k : 64 * k + 64], packed)
        payload[0:64, lanes] = packed
        tail = jnp.where(row == 0, total, jnp.where(row == 1, sums[:, lanes], 0.0))
        if z < 3:
            for a, part in enumerate((sum0, sum1, sum2)):
                tail = jnp.where(row == 2 + a, part[0:1, lanes], tail)
        payload[64:72, lanes] = tail
        bases[z] = block_vectors(vectors, z, same)
        factor = -(tall[:, 1:2] * scale) / (tall[:, 2:3] + root)
        factors[z] = jnp.where(same, factor, 0.0)
    for c in range(2):

        @pl.when(lax.axis_index("c") == c)
        def _():
            mine[...] = payload[:, 512 * c : 512 * c + 512]
            theirs[...] = payload[:, 512 - 512 * c : 1024 - 512 * c]


def back_part(cols, kernel, xc, sums, colsums, vectors, values):
    return pl.pallas_call(
        back_kernel,
        in_specs=[ON_CHIP, IN_HBM] + [ON_CHIP] * 7,
        out_specs=(ON_CHIP,) * 6,
        out_shape=(
            jax.ShapeDtypeStruct((ROWS, D), BF16),
            jax.ShapeDtypeStruct((72, D), F32),
            jax.ShapeDtypeStruct((72, 512), F32),
            jax.ShapeDtypeStruct((72, 512), F32),
            jax.ShapeDtypeStruct((4, 256, 256), F32),
            jax.ShapeDtypeStruct((4, 256, 256), F32),
        ),
        scratch_shapes=[
            pltpu.VMEM((4, 9 * O, 256), BF16),
            pltpu.SemaphoreType.DMA((4,)),
        ],
        compiler_params=pltpu.CompilerParams(vmem_limit_bytes=14 << 20),
        name="back_part",
    )(cols, kernel, xc, sums, *colsums, vectors, values)


def final_kernel(
    dev,
    xc,
    mine,
    theirs,
    own,
    bases,
    factors,
    whiten,
    out,
    fix,
    payload,
    shift,
    sigma,
    row_vector,
):
    image = pl.program_id(0)

    @pl.when(image == 0)
    def _():
        for c in range(2):

            @pl.when(lax.axis_index("c") == c)
            def _():
                payload[:, 512 * c : 512 * c + 512] = mine[...]
                payload[:, 512 - 512 * c : 1024 - 512 * c] = theirs[...]

        for z in range(4):
            lanes = slice(256 * z, 256 * z + 256)
            basis = bases[z]
            total = payload[64:65, lanes]
            mean = payload[65:66, lanes] * (1.0 / TOTAL)
            stack = payload[0:64, lanes]
            raw = jnp.concatenate([stack, stack, stack, stack], axis=0)
            cov = raw - columns_of([mean])[:, 0:1] * total
            rotated = fine(nn, fine(tn, basis, cov), basis)
            inner = 0.5 * (rotated + rotated.T) * factors[z]
            grad = fine(nt, fine(nn, basis, inner), basis)
            sigma[z] = (grad * (2.0 / TOTAL)).astype(BF16)
            moved = own[64:65, lanes] * (1.0 / PIXELS) - total * (1.0 / TOTAL)
            offset = own[65:66, lanes] * (1.0 / PIXELS) - mean
            empty = [jnp.zeros((1, 256), BF16)]
            stacked = jnp.concatenate(pieces(moved, 3) + pieces(mean, 3) + empty * 2, axis=0)
            through = nn(stacked, whiten[z])
            stacked = jnp.concatenate(pieces(offset, 3) + empty * 5, axis=0)
            other = nn(stacked, sigma[z])
            row_vector[0:1, lanes] = (
                jnp.sum(through[0:3], axis=0, keepdims=True)
                + jnp.sum(other[0:3], axis=0, keepdims=True)
            )
            shift[0:1, lanes] = jnp.sum(through[3:6], axis=0, keepdims=True)
        first = 8 * sum(STRIDE[axis] * lax.axis_index(axis) for axis in ALL)
        lane = lax.broadcasted_iota(jnp.int32, (8, D), 1)
        row = lax.broadcasted_iota(jnp.int32, (8, D), 0)
        chosen = jnp.where(lane == row + first, shift[...], 0.0)
        chosen = jnp.sum(chosen, axis=1, keepdims=True)
        for a in range(3):
            fix[a] = chosen * payload[66 + a : 67 + a, 0:768]

    rows = pl.ds(pl.multiple_of(image * (H * 16), H * 16), H * 16)
    for z in range(4):
        lanes = slice(256 * z, 256 * z + 256)
        result = nn(dev[rows, lanes], whiten[z]) + nn(xc[rows, lanes], sigma[z])
        result = result + row_vector[0:1, lanes]
        out[0, :, :, lanes] = result.astype(BF16).reshape(H, 16, 256)[:, 0:W, :]


def final_part(dev, xc, mine, theirs, own, bases, factors, whiten):
    return pl.pallas_call(
        final_kernel,
        grid=(IMAGES,),
        in_specs=[ON_CHIP] * 8,
        out_specs=(pl.BlockSpec((1, H, W, D), lambda b: (b, 0, 0, 0)), ON_CHIP),
        out_shape=(
            jax.ShapeDtypeStruct((IMAGES, H, W, D), BF16),
            jax.ShapeDtypeStruct((3, 8, 768), F32),
        ),
        scratch_shapes=[
            pltpu.VMEM((72, D), F32),
            pltpu.VMEM((1, D), F32),
            pltpu.VMEM((4, 256, 256), BF16),
            pltpu.VMEM((1, D), F32),
        ],
        compiler_params=pltpu.CompilerParams(vmem_limit_bytes=10 << 20),
        name="final_part",
    )(dev, xc, mine, theirs, own, bases, factors, whiten)


def permutation(move):
    pairs = []
    for device in range(128):
        at = {k: (device // STRIDE[k]) % SIZE[k] for k in ALL}
        move(at)
        pairs.append((device, sum(at[k] * STRIDE[k] for k in ALL)))
    return pairs


def exchange(value, move):
    return lax.ppermute(value, ALL, permutation(move))


def other_core(at):
    at["c"] ^= 1


def ring(axis, step):
    def move(at):
        at[axis] ^= (1, 3)[(step + at["c"]) % 2]

    return move


def halves(value, dim):
    pick = lambda k: lax.index_in_dim(value, k, dim, keepdims=False)
    return pick(0), pick(1)


def local(features, grads, kernel, vectors, values):
    stay = lambda array: pltpu.with_memory_space_constraint(array, pltpu.HBM)
    cols, xc, wht, u, sums, whiten = prep(stay(features), stay(grads), stay(vectors), values)
    cols, xc = cols.reshape(ROWS, 9 * O), xc.reshape(ROWS, D)

    parts, colsums = [], []
    for a in range(3):
        keep, send, colsum = weight_part(wht, cols, u, a)
        colsums.append(colsum)
        parts.append((keep + exchange(send, other_core)).reshape(2, 2, 2, 2, 2, 2, 8, 768))
    cols, *parts = lax.optimization_barrier((cols, *parts))
    dev, own, mine, theirs, bases, factors = back_part(
        cols, stay(kernel.reshape(9 * O, D)), xc, sums, colsums, vectors, values
    )
    mine = mine + exchange(theirs, other_core)

    names = [["z1", "z2", "y1", "y2", "x1", "x2"] for _ in range(3)]
    for turn in range(3):
        for a in range(3):
            axis = "xyz"[(a + turn) % 3]
            dim = names[a].index(axis + "1")
            names[a].pop(dim)
            keep, send = halves(parts[a], dim)
            parts[a] = keep + exchange(send, ring(axis, 0))
        if turn == 0:
            mine, *parts = lax.optimization_barrier((mine, *parts))
            for axis in "xyz":
                for step in range(2):
                    mine = mine + exchange(mine, ring(axis, step))
            theirs = exchange(mine, other_core)
    share = jnp.stack(parts, axis=3)
    order = ["z", "y", "x"]
    for axis in "xyz":
        dim = order.index(axis)
        order.pop(dim)
        keep, send = halves(share, dim)
        share = keep + exchange(send, ring(axis, 1))

    input_grad, fix = final_part(dev, xc, mine, theirs, own, bases, factors, whiten)
    kernel_grad = (share - fix).transpose(1, 0, 2).reshape(8, 3, 3, O)
    return input_grad, kernel_grad


def solution(mesh):
    finer = Mesh(mesh.devices.reshape(4, 4, 2, 4), ALL)
    split_all = P(ALL, None, None, None)
    return jax.shard_map(
        local,
        mesh=finer,
        in_specs=(split_all, split_all, P(), P(), P()),
        out_specs=(split_all, split_all),
        check_vma=False,
    )
```

```python
import functools

import jax
import jax.numpy as jnp
import numpy as np
from jax import lax
from jax.experimental import pallas as pl
from jax.experimental.pallas import tpu as pltpu
from jax.sharding import Mesh
from jax.sharding import PartitionSpec as P

ALL = ("z", "y", "c", "x")
SIZE = {"z": 4, "y": 4, "c": 2, "x": 4}
STRIDE = {"z": 32, "y": 8, "c": 4, "x": 1}
RING = ((0, 3, 1, 2), (0, 1, 3, 2))
F32 = jnp.float32
BF16 = jnp.bfloat16
IMAGES, H, W, D, O = 6, 14, 14, 1024, 256
ROWS = IMAGES * H * 16
PIXELS = IMAGES * H * W
TOTAL = 128.0 * PIXELS
ON_CHIP = pl.BlockSpec(memory_space=pltpu.VMEM)
IN_HBM = pl.BlockSpec(memory_space=pltpu.HBM)


def nt(a, b):
    return lax.dot_general(
        a, b, (((1,), (1,)), ((), ())), preferred_element_type=F32
    )


def tn(a, b):
    return lax.dot_general(
        a, b, (((0,), (0,)), ((), ())), preferred_element_type=F32
    )


def nn(a, b):
    return lax.dot_general(
        a, b, (((1,), (0,)), ((), ())), preferred_element_type=F32
    )


def same_group():
    row = lax.broadcasted_iota(jnp.int32, (256, 256), 0)
    col = lax.broadcasted_iota(jnp.int32, (256, 256), 1)
    return (row >> 6) == (col >> 6)


def block_vectors(vectors, z, same):
    four = vectors[4 * z : 4 * z + 4].reshape(256, 64)
    return jnp.where(same, jnp.concatenate([four, four, four, four], axis=1), 0.0)


def value_row(values, z):
    return jnp.concatenate([values[4 * z + g : 4 * z + g + 1, :] for g in range(4)], axis=1)


def columns_of(rows):
    rows = rows + [jnp.zeros((1, 256), F32)] * (8 - len(rows))
    return jnp.concatenate(rows, axis=0).T


def pieces(a, n):
    out = []
    for _ in range(n):
        out.append(a.astype(BF16))
        a = a - out[-1].astype(F32)
    return out


def fine(dot, a, b):
    a_high, a_low = pieces(a, 2)
    b_high, b_low = pieces(b, 2)
    return dot(a_high, b_high) + (dot(a_high, b_low) + dot(a_low, b_high))


def place():
    core = lax.axis_index("c")
    spots = ([], [])
    for axis in "zyx":
        i = lax.axis_index(axis)
        a, b = (i ^ (i >> 1)) & 1, i >> 1
        spots[0].append(2 * a + b)
        spots[1].append(2 * b + a)
    return core, spots


def prep_kernel(
    features_hbm,
    grads_hbm,
    vectors_hbm,
    values,
    cols,
    xc,
    wht,
    u,
    sums,
    whiten,
    wide,
    wp32,
    features,
    grads,
    vectors,
    arrived,
):
    copies = [
        pltpu.make_async_copy(source, target, arrived.at[k])
        for k, (source, target) in enumerate(
            ((vectors_hbm, vectors), (grads_hbm, grads), (features_hbm, features))
        )
    ]
    for copy in copies:
        copy.start()
    core, spots = place()
    same = same_group()
    wide[...] = jnp.zeros_like(wide)
    xc[...] = jnp.zeros_like(xc)
    wht[1024:1040, :] = jnp.ones((16, ROWS), BF16)
    copies[0].wait()
    for z in range(4):
        basis = block_vectors(vectors, z, same)
        scale = lax.rsqrt(value_row(values, z))
        full = fine(nt, basis * scale, basis)
        whiten[z] = full.astype(BF16)
        for c in range(2):
            at_z, at_y, at_x = spots[c]
            for row, (y, x) in enumerate((y, x) for y in RING[c] for x in RING[c]):
                channel = y * 64 + c * 32 + x * 8
                row = pl.multiple_of(8 * (row ^ (4 * at_y + at_x)), 8)
                wp32[4 * c + z, pl.ds(row, 8), :] = full[channel : channel + 8, :]
    copies[1].wait()
    inside = lax.broadcasted_iota(jnp.int32, (H, 16, O), 1) < W
    for b in range(IMAGES):
        wide[:, 8 : 8 + W, :] = grads[b].astype(F32)
        for c in range(3):
            shifted = wide[:, 9 - c : 25 - c, :]
            if c == 2:
                shifted = jnp.where(inside, shifted, 0.0)
            shifted = shifted.astype(BF16)
            for a in range(3):
                lane = (3 * a + c) * O
                first, last = b * H + max(0, a - 1), b * H + H - max(0, 1 - a)
                start = max(0, 1 - a)
                cols[first:last, :, lane : lane + O] = shifted[start : start + last - first]
                if a == 0:
                    cols[b * H + H - 1, :, lane : lane + O] = jnp.zeros((16, O), BF16)
                if a == 2:
                    cols[b * H, :, lane : lane + O] = jnp.zeros((16, O), BF16)
    copies[2].wait()
    total = jnp.zeros((1, D), F32)
    for b in range(IMAGES):
        total = total + jnp.sum(
            jnp.sum(features[b].astype(F32), axis=0), axis=0, keepdims=True
        )
    sums[...] = total
    mean = total * (1.0 / PIXELS)
    for b in range(IMAGES):
        xc[b * H : b * H + H, 0:W, :] = (features[b].astype(F32) - mean[None]).astype(BF16)
    high, middle, low = pieces(mean, 3)
    pad = lax.broadcasted_iota(jnp.int32, (16, D), 0)
    head = xc[0].astype(F32)
    head = jnp.where(pad == 14, high.astype(F32), jnp.where(pad == 15, middle.astype(F32), head))
    xc[0] = head.astype(BF16)
    head = xc[1].astype(F32)
    xc[1] = jnp.where(pad == 14, low.astype(F32), head).astype(BF16)
    for k in range(8):
        c, z = k // 4, k % 4
        chunk = xc[:, :, 256 * z : 256 * z + 256].reshape(ROWS, 256)
        part = nt(wp32[k].astype(BF16), chunk)
        row = 4 * (c ^ core) + (RING[c].index(z) ^ spots[c][0])
        row = pl.multiple_of(128 * row, 128)
        wht[pl.ds(row, 128), :] = part.astype(BF16)
        shift = part[:, 14:15] + part[:, 15:16] + part[:, 30:31]
        u[pl.ds(row, 128), :] = jnp.broadcast_to(shift, (128, 128))


def prep(features, grads, vectors, values):
    return pl.pallas_call(
        prep_kernel,
        out_shape=(
            jax.ShapeDtypeStruct((IMAGES * H, 16, 9 * O), BF16),
            jax.ShapeDtypeStruct((IMAGES * H, 16, D), BF16),
            jax.ShapeDtypeStruct((1040, ROWS), BF16),
            jax.ShapeDtypeStruct((1024, 128), F32),
            jax.ShapeDtypeStruct((1, D), F32),
            jax.ShapeDtypeStruct((4, 256, 256), BF16),
        ),
        in_specs=[IN_HBM] * 3 + [ON_CHIP],
        out_specs=(ON_CHIP,) * 6,
        scratch_shapes=[
            pltpu.VMEM((H, 32, O), F32),
            pltpu.VMEM((8, 128, 256), F32),
            pltpu.VMEM((IMAGES, H, W, D), BF16),
            pltpu.VMEM((IMAGES, H, W, O), BF16),
            pltpu.VMEM((16, 64, 64), F32),
            pltpu.SemaphoreType.DMA((3,)),
        ],
        compiler_params=pltpu.CompilerParams(vmem_limit_bytes=10 << 20),
        name="prep",
    )(features, grads, vectors, values)


def weight_kernel(a, wht, cols, u, kernel_hbm, keep, send, colsum, slab, arrived):
    copy = pltpu.make_async_copy(kernel_hbm.at[pl.ds(768 * a, 768)], slab, arrived)
    copy.start()
    for n in range(3):
        start = 768 * a + 256 * n
        full = nn(wht[...], cols[:, start : start + 256])
        colsum[:, 256 * n : 256 * n + 256] = full[1024:1032, :]
        for k in range(2):
            ones = full[1024:1025, 128 * k : 128 * k + 128]
            lanes = slice(256 * n + 128 * k, 256 * n + 128 * k + 128)
            part = full[0:1024, 128 * k : 128 * k + 128] + u[...] * ones
            keep[:, lanes] = part[0:512]
            send[:, lanes] = part[512:1024]
    copy.wait()


def weight_part(wht, cols, u, kernel, a):
    return pl.pallas_call(
        functools.partial(weight_kernel, a),
        in_specs=[ON_CHIP] * 3 + [IN_HBM],
        out_specs=(ON_CHIP,) * 4,
        out_shape=(
            jax.ShapeDtypeStruct((512, 768), F32),
            jax.ShapeDtypeStruct((512, 768), F32),
            jax.ShapeDtypeStruct((8, 768), F32),
            jax.ShapeDtypeStruct((768, D), BF16),
        ),
        scratch_shapes=[pltpu.SemaphoreType.DMA],
        compiler_params=pltpu.CompilerParams(vmem_limit_bytes=6 << 20),
        name=f"weight_part_{a}",
    )(wht, cols, u, kernel)


def pack(block, payload, first):
    block[:, 0:256] = payload[0:48, first : first + 256]
    block[:, 256:512] = payload[0:48, first + 256 : first + 512]
    block[0:24, 512:768] = payload[48:72, first : first + 256]
    block[24:48, 512:768] = payload[48:72, first + 256 : first + 512]


def unpack(block, payload, first):
    payload[0:48, first : first + 256] = block[:, 0:256]
    payload[0:48, first + 256 : first + 512] = block[:, 256:512]
    payload[48:72, first : first + 256] = block[0:24, 512:768]
    payload[48:72, first + 256 : first + 512] = block[24:48, 512:768]


def back_kernel(
    cols,
    slab0,
    slab1,
    slab2,
    xc,
    sums,
    sum0,
    sum1,
    sum2,
    vectors,
    values,
    dev,
    own,
    mine,
    theirs,
    bases,
    factors,
    payload,
):
    same = same_group()
    real = (lax.broadcasted_iota(jnp.int32, (ROWS, 256), 0) & 15) < W
    group = lax.broadcasted_iota(jnp.int32, (64, 256), 1) >> 6
    row = lax.broadcasted_iota(jnp.int32, (8, 256), 0)
    for z in range(4):
        lanes = slice(256 * z, 256 * z + 256)
        back = nn(cols[:, 0:768], slab0[:, lanes])
        back = back + nn(cols[:, 768:1536], slab1[:, lanes])
        back = back + nn(cols[:, 1536:2304], slab2[:, lanes])
        total = jnp.sum(back, axis=0, keepdims=True)
        low = jnp.where(real, back - total * (1.0 / PIXELS), 0.0).astype(BF16)
        dev[:, lanes] = low
        value = value_row(values, z)
        scale, root = lax.rsqrt(value), jnp.sqrt(value)
        tall = columns_of([sums[:, lanes] * (1.0 / PIXELS), scale, root])
        cov = tn(xc[:, lanes], low) + tall[:, 0:1] * total
        packed = cov[0:64]
        for k in range(1, 4):
            packed = jnp.where(group == k, cov[64 * k : 64 * k + 64], packed)
        payload[0:64, lanes] = packed
        tail = jnp.where(row == 0, total, jnp.where(row == 1, sums[:, lanes], 0.0))
        if z < 3:
            for a, part in enumerate((sum0, sum1, sum2)):
                tail = jnp.where(row == 2 + a, part[0:1, lanes], tail)
        payload[64:72, lanes] = tail
        own[:, lanes] = tail
        bases[z] = block_vectors(vectors, z, same)
        factor = -(tall[:, 1:2] * scale) / (tall[:, 2:3] + root)
        factors[z] = jnp.where(same, factor, 0.0)
    for c in range(2):

        @pl.when(lax.axis_index("c") == c)
        def _():
            pack(mine, payload, 512 * c)
            pack(theirs, payload, 512 - 512 * c)


def back_part(cols, slabs, xc, sums, colsums, vectors, values):
    return pl.pallas_call(
        back_kernel,
        in_specs=[ON_CHIP] * 11,
        out_specs=(ON_CHIP,) * 6,
        out_shape=(
            jax.ShapeDtypeStruct((ROWS, D), BF16),
            jax.ShapeDtypeStruct((8, D), F32),
            jax.ShapeDtypeStruct((48, 768), F32),
            jax.ShapeDtypeStruct((48, 768), F32),
            jax.ShapeDtypeStruct((4, 256, 256), F32),
            jax.ShapeDtypeStruct((4, 256, 256), F32),
        ),
        scratch_shapes=[pltpu.VMEM((72, D), F32)],
        compiler_params=pltpu.CompilerParams(vmem_limit_bytes=14 << 20),
        name="back_part",
    )(cols, *slabs, xc, sums, *colsums, vectors, values)


def final_kernel(
    dev,
    xc,
    mine,
    theirs,
    own,
    bases,
    factors,
    whiten,
    out,
    fix,
    payload,
    shift,
    sigma,
    row_vector,
    done,
    sent,
):
    for c in range(2):

        @pl.when(lax.axis_index("c") == c)
        def _():
            unpack(mine, payload, 512 * c)
            unpack(theirs, payload, 512 - 512 * c)

    for z in range(4):
        lanes = slice(256 * z, 256 * z + 256)
        basis = bases[z]
        total = payload[64:65, lanes]
        mean = payload[65:66, lanes] * (1.0 / TOTAL)
        stack = payload[0:64, lanes]
        raw = jnp.concatenate([stack, stack, stack, stack], axis=0)
        cov = raw - columns_of([mean])[:, 0:1] * total
        rotated = fine(nn, fine(tn, basis, cov), basis)
        inner = 0.5 * (rotated + rotated.T) * factors[z]
        grad = fine(nt, fine(nn, basis, inner), basis)
        sigma[z] = (grad * (2.0 / TOTAL)).astype(BF16)
        moved = own[0:1, lanes] * (1.0 / PIXELS) - total * (1.0 / TOTAL)
        offset = own[1:2, lanes] * (1.0 / PIXELS) - mean
        empty = [jnp.zeros((1, 256), BF16)]
        stacked = jnp.concatenate(pieces(moved, 3) + pieces(mean, 3) + empty * 2, axis=0)
        through = nn(stacked, whiten[z])
        stacked = jnp.concatenate(pieces(offset, 3) + empty * 5, axis=0)
        other = nn(stacked, sigma[z])
        row_vector[0:1, lanes] = (
            jnp.sum(through[0:3], axis=0, keepdims=True)
            + jnp.sum(other[0:3], axis=0, keepdims=True)
        )
        shift[0:1, lanes] = jnp.sum(through[3:6], axis=0, keepdims=True)
    first = 8 * sum(STRIDE[axis] * lax.axis_index(axis) for axis in ALL)
    lane = lax.broadcasted_iota(jnp.int32, (8, D), 1)
    row = lax.broadcasted_iota(jnp.int32, (8, D), 0)
    chosen = jnp.where(lane == row + first, shift[...], 0.0)
    chosen = jnp.sum(chosen, axis=1, keepdims=True)
    for a in range(3):
        fix[a] = chosen * payload[66 + a : 67 + a, 0:768]
    copies = []
    for b in range(IMAGES):
        rows = slice(H * 16 * b, H * 16 * b + H * 16)
        for z in range(4):
            lanes = slice(256 * z, 256 * z + 256)
            result = nn(dev[rows, lanes], whiten[z]) + nn(xc[rows, lanes], sigma[z])
            result = result + row_vector[0:1, lanes]
            done[b, :, :, lanes] = result.astype(BF16).reshape(H, 16, 256)[:, 0:W, :]
        copies.append(pltpu.make_async_copy(done.at[b], out.at[b], sent.at[b]))
        copies[-1].start()
    for copy in copies:
        copy.wait()


def final_part(dev, xc, mine, theirs, own, bases, factors, whiten):
    return pl.pallas_call(
        final_kernel,
        in_specs=[ON_CHIP] * 8,
        out_specs=(IN_HBM, ON_CHIP),
        out_shape=(
            jax.ShapeDtypeStruct((IMAGES, H, W, D), BF16),
            jax.ShapeDtypeStruct((3, 8, 768), F32),
        ),
        scratch_shapes=[
            pltpu.VMEM((72, D), F32),
            pltpu.VMEM((1, D), F32),
            pltpu.VMEM((4, 256, 256), BF16),
            pltpu.VMEM((1, D), F32),
            pltpu.VMEM((IMAGES, H, W, D), BF16),
            pltpu.SemaphoreType.DMA((IMAGES,)),
        ],
        compiler_params=pltpu.CompilerParams(vmem_limit_bytes=12 << 20),
        name="final_part",
    )(dev, xc, mine, theirs, own, bases, factors, whiten)


def permutation(move):
    pairs = []
    for device in range(128):
        at = {k: (device // STRIDE[k]) % SIZE[k] for k in ALL}
        move(at)
        pairs.append((device, sum(at[k] * STRIDE[k] for k in ALL)))
    return pairs


def exchange(value, move):
    return lax.ppermute(value, ALL, permutation(move))


def other_core(at):
    at["c"] ^= 1


def ring(axis, step):
    def move(at):
        at[axis] ^= (1, 3)[(step + at["c"]) % 2]

    return move


def halves(value, dim):
    pick = lambda k: lax.index_in_dim(value, k, dim, keepdims=False)
    return pick(0), pick(1)


def joint(part, send, mine, move):
    rows = send.size // 768
    message = jnp.concatenate([send.reshape(rows, 768), mine], axis=0)
    message = exchange(message, move)
    return part + message[:rows].reshape(part.shape), mine + message[rows:]


def local(features, grads, kernel, vectors, values):
    stay = lambda array: pltpu.with_memory_space_constraint(array, pltpu.HBM)
    cols, xc, wht, u, sums, whiten = prep(stay(features), stay(grads), stay(vectors), values)
    cols, xc = cols.reshape(ROWS, 9 * O), xc.reshape(ROWS, D)
    kernel = stay(kernel.reshape(9 * O, D))

    parts, colsums, slabs = [], [], []
    for a in range(3):
        keep, send, colsum, slab = weight_part(wht, cols, u, kernel, a)
        colsums.append(colsum)
        slabs.append(slab)
        parts.append((keep + exchange(send, other_core)).reshape(2, 2, 2, 2, 2, 2, 8, 768))
    cols = lax.optimization_barrier((cols, *parts))[0]
    dev, own, mine, theirs, bases, factors = back_part(
        cols, slabs, xc, sums, colsums, vectors, values
    )
    mine = mine + exchange(theirs, other_core)

    names = [["z1", "z2", "y1", "y2", "x1", "x2"] for _ in range(3)]
    for turn in range(3):
        for a in range(3):
            axis = "xyz"[(a + turn) % 3]
            dim = names[a].index(axis + "1")
            names[a].pop(dim)
            keep, send = halves(parts[a], dim)
            if turn > 0 and a == 0:
                parts[a], mine = joint(keep, send, mine, ring(axis, 0))
            else:
                parts[a] = keep + exchange(send, ring(axis, 0))
        if turn == 0:
            mine, *parts = lax.optimization_barrier((mine, *parts))
            mine = mine + exchange(mine, ring("x", 0))
    share = jnp.stack(parts, axis=0)
    order = ["a", "z", "y", "x"]
    for axis in "xyz":
        dim = order.index(axis)
        order.pop(dim)
        keep, send = halves(share, dim)
        share, mine = joint(keep, send, mine, ring(axis, 1))
    theirs = exchange(mine, other_core)

    input_grad, fix = final_part(dev, xc, mine, theirs, own, bases, factors, whiten)
    kernel_grad = (share - fix).transpose(1, 0, 2).reshape(8, 3, 3, O)
    return input_grad, kernel_grad


def solution(mesh):
    finer = Mesh(mesh.devices.reshape(4, 4, 2, 4), ALL)
    split_all = P(ALL, None, None, None)
    return jax.shard_map(
        local,
        mesh=finer,
        in_specs=(split_all, split_all, P(), P(), P()),
        out_specs=(split_all, split_all),
        check_vma=False,
    )
```

```python
import functools

import jax
import jax.numpy as jnp
import numpy as np
from jax import lax
from jax.experimental import pallas as pl
from jax.experimental.pallas import tpu as pltpu
from jax.sharding import Mesh
from jax.sharding import PartitionSpec as P

ALL = ("z", "y", "c", "x")
SIZE = {"z": 4, "y": 4, "c": 2, "x": 4}
STRIDE = {"z": 32, "y": 8, "c": 4, "x": 1}
RING = ((0, 3, 1, 2), (0, 1, 3, 2))
F32 = jnp.float32
BF16 = jnp.bfloat16
IMAGES, H, W, D, O = 6, 14, 14, 1024, 256
ROWS = IMAGES * H * 16
PIXELS = IMAGES * H * W
TOTAL = 128.0 * PIXELS
ON_CHIP = pl.BlockSpec(memory_space=pltpu.VMEM)
IN_HBM = pl.BlockSpec(memory_space=pltpu.HBM)


def nt(a, b):
    return lax.dot_general(
        a, b, (((1,), (1,)), ((), ())), preferred_element_type=F32
    )


def tn(a, b):
    return lax.dot_general(
        a, b, (((0,), (0,)), ((), ())), preferred_element_type=F32
    )


def nn(a, b):
    return lax.dot_general(
        a, b, (((1,), (0,)), ((), ())), preferred_element_type=F32
    )


def same_group():
    row = lax.broadcasted_iota(jnp.int32, (256, 256), 0)
    col = lax.broadcasted_iota(jnp.int32, (256, 256), 1)
    return (row >> 6) == (col >> 6)


def block_vectors(vectors, z, same):
    four = vectors[4 * z : 4 * z + 4].reshape(256, 64)
    return jnp.where(same, jnp.concatenate([four, four, four, four], axis=1), 0.0)


def value_row(values, z):
    return jnp.concatenate([values[4 * z + g : 4 * z + g + 1, :] for g in range(4)], axis=1)


def columns_of(rows):
    rows = rows + [jnp.zeros((1, 256), F32)] * (8 - len(rows))
    return jnp.concatenate(rows, axis=0).T


def pieces(a, n):
    out = []
    for _ in range(n):
        out.append(a.astype(BF16))
        a = a - out[-1].astype(F32)
    return out


def fine(dot, a, b):
    a_high, a_low = a if isinstance(a, tuple) else pieces(a, 2)
    b_high, b_low = b if isinstance(b, tuple) else pieces(b, 2)
    return dot(a_high, b_high) + (dot(a_high, b_low) + dot(a_low, b_high))


def place():
    core = lax.axis_index("c")
    spots = ([], [])
    for axis in "zyx":
        i = lax.axis_index(axis)
        a, b = (i ^ (i >> 1)) & 1, i >> 1
        spots[0].append(2 * a + b)
        spots[1].append(2 * b + a)
    return core, spots


def prep_kernel(
    features_hbm,
    grads_hbm,
    vectors_hbm,
    values,
    cols,
    xc,
    wht,
    u,
    sums,
    whiten,
    wide,
    wp32,
    features,
    grads,
    vectors,
    arrived,
):
    copies = [
        pltpu.make_async_copy(source, target, arrived.at[k])
        for k, (source, target) in enumerate(
            ((vectors_hbm, vectors), (grads_hbm, grads), (features_hbm, features))
        )
    ]
    for copy in copies:
        copy.start()
    core, spots = place()
    same = same_group()
    wide[...] = jnp.zeros_like(wide)
    xc[...] = jnp.zeros_like(xc)
    wht[1024:1040, :] = jnp.ones((16, ROWS), BF16)
    copies[0].wait()
    for z in range(4):
        basis = block_vectors(vectors, z, same)
        scale = lax.rsqrt(value_row(values, z))
        full = fine(nt, basis * scale, basis)
        whiten[z] = full.astype(BF16)
        for c in range(2):
            at_z, at_y, at_x = spots[c]
            for row, (y, x) in enumerate((y, x) for y in RING[c] for x in RING[c]):
                channel = y * 64 + c * 32 + x * 8
                row = pl.multiple_of(8 * (row ^ (4 * at_y + at_x)), 8)
                wp32[4 * c + z, pl.ds(row, 8), :] = full[channel : channel + 8, :]
    copies[1].wait()
    inside = lax.broadcasted_iota(jnp.int32, (H, 16, O), 1) < W
    for b in range(IMAGES):
        wide[:, 8 : 8 + W, :] = grads[b].astype(F32)
        for c in range(3):
            shifted = wide[:, 9 - c : 25 - c, :]
            if c == 2:
                shifted = jnp.where(inside, shifted, 0.0)
            shifted = shifted.astype(BF16)
            for a in range(3):
                lane = (3 * a + c) * O
                first, last = b * H + max(0, a - 1), b * H + H - max(0, 1 - a)
                start = max(0, 1 - a)
                cols[first:last, :, lane : lane + O] = shifted[start : start + last - first]
                if a == 0:
                    cols[b * H + H - 1, :, lane : lane + O] = jnp.zeros((16, O), BF16)
                if a == 2:
                    cols[b * H, :, lane : lane + O] = jnp.zeros((16, O), BF16)
    copies[2].wait()
    total = jnp.zeros((1, D), F32)
    for b in range(IMAGES):
        total = total + jnp.sum(
            jnp.sum(features[b].astype(F32), axis=0), axis=0, keepdims=True
        )
    sums[...] = total
    mean = total * (1.0 / PIXELS)
    for b in range(IMAGES):
        xc[b * H : b * H + H, 0:W, :] = (features[b].astype(F32) - mean[None]).astype(BF16)
    high, middle, low = pieces(mean, 3)
    pad = lax.broadcasted_iota(jnp.int32, (16, D), 0)
    head = xc[0].astype(F32)
    head = jnp.where(pad == 14, high.astype(F32), jnp.where(pad == 15, middle.astype(F32), head))
    xc[0] = head.astype(BF16)
    head = xc[1].astype(F32)
    xc[1] = jnp.where(pad == 14, low.astype(F32), head).astype(BF16)
    for k in range(8):
        c, z = k // 4, k % 4
        chunk = xc[:, :, 256 * z : 256 * z + 256].reshape(ROWS, 256)
        part = nt(wp32[k].astype(BF16), chunk)
        row = 4 * (c ^ core) + (RING[c].index(z) ^ spots[c][0])
        row = pl.multiple_of(128 * row, 128)
        wht[pl.ds(row, 128), :] = part.astype(BF16)
        shift = part[:, 14:15] + part[:, 15:16] + part[:, 30:31]
        u[pl.ds(row, 128), :] = jnp.broadcast_to(shift, (128, 128))


def prep(features, grads, vectors, values):
    return pl.pallas_call(
        prep_kernel,
        out_shape=(
            jax.ShapeDtypeStruct((IMAGES * H, 16, 9 * O), BF16),
            jax.ShapeDtypeStruct((IMAGES * H, 16, D), BF16),
            jax.ShapeDtypeStruct((1040, ROWS), BF16),
            jax.ShapeDtypeStruct((1024, 128), F32),
            jax.ShapeDtypeStruct((1, D), F32),
            jax.ShapeDtypeStruct((4, 256, 256), BF16),
        ),
        in_specs=[IN_HBM] * 3 + [ON_CHIP],
        out_specs=(ON_CHIP,) * 6,
        scratch_shapes=[
            pltpu.VMEM((H, 32, O), F32),
            pltpu.VMEM((8, 128, 256), F32),
            pltpu.VMEM((IMAGES, H, W, D), BF16),
            pltpu.VMEM((IMAGES, H, W, O), BF16),
            pltpu.VMEM((16, 64, 64), F32),
            pltpu.SemaphoreType.DMA((3,)),
        ],
        compiler_params=pltpu.CompilerParams(vmem_limit_bytes=10 << 20),
        name="prep",
    )(features, grads, vectors, values)


def weight_kernel(a, wht, cols, u, kernel_hbm, keep, send, colsum, slab, arrived):
    copy = pltpu.make_async_copy(kernel_hbm.at[pl.ds(768 * a, 768)], slab, arrived)
    copy.start()
    for n in range(3):
        start = 768 * a + 256 * n
        full = nn(wht[...], cols[:, start : start + 256])
        colsum[:, 256 * n : 256 * n + 256] = full[1024:1032, :]
        for k in range(2):
            ones = full[1024:1025, 128 * k : 128 * k + 128]
            lanes = slice(256 * n + 128 * k, 256 * n + 128 * k + 128)
            part = full[0:1024, 128 * k : 128 * k + 128] + u[...] * ones
            keep[:, lanes] = part[0:512]
            send[:, lanes] = part[512:1024]
    copy.wait()


def weight_part(wht, cols, u, kernel, a):
    return pl.pallas_call(
        functools.partial(weight_kernel, a),
        in_specs=[ON_CHIP] * 3 + [IN_HBM],
        out_specs=(ON_CHIP,) * 4,
        out_shape=(
            jax.ShapeDtypeStruct((512, 768), F32),
            jax.ShapeDtypeStruct((512, 768), F32),
            jax.ShapeDtypeStruct((8, 768), F32),
            jax.ShapeDtypeStruct((768, D), BF16),
        ),
        scratch_shapes=[pltpu.SemaphoreType.DMA],
        compiler_params=pltpu.CompilerParams(vmem_limit_bytes=6 << 20),
        name=f"weight_part_{a}",
    )(wht, cols, u, kernel)


def back_kernel(
    cols,
    slab0,
    slab1,
    slab2,
    xc,
    sums,
    sum0,
    sum1,
    sum2,
    vectors,
    values,
    dev,
    own,
    mine,
    theirs,
    bases,
    factors,
    blocks,
):
    same = same_group()
    eye = lax.broadcasted_iota(jnp.int32, (256, 256), 0) == lax.broadcasted_iota(
        jnp.int32, (256, 256), 1
    )
    eye = jnp.where(eye, 1.0, 0.0).astype(BF16)
    real = (lax.broadcasted_iota(jnp.int32, (ROWS, 256), 0) & 15) < W
    group = lax.broadcasted_iota(jnp.int32, (64, 256), 1) >> 6
    below = lax.broadcasted_iota(jnp.int32, (64, 256), 0) - (
        lax.broadcasted_iota(jnp.int32, (64, 256), 1) & 63
    )
    row = lax.broadcasted_iota(jnp.int32, (8, 256), 0)
    upper = None
    for z in range(4):
        lanes = slice(256 * z, 256 * z + 256)
        back = nn(cols[:, 0:768], slab0[:, lanes])
        back = back + nn(cols[:, 768:1536], slab1[:, lanes])
        back = back + nn(cols[:, 1536:2304], slab2[:, lanes])
        total = jnp.sum(back, axis=0, keepdims=True)
        low = jnp.where(real, back - total * (1.0 / PIXELS), 0.0).astype(BF16)
        dev[:, lanes] = low
        value = value_row(values, z)
        scale, root = lax.rsqrt(value), jnp.sqrt(value)
        tall = columns_of([sums[:, lanes] * (1.0 / PIXELS), scale, root])
        turned = nt(eye, xc[:, lanes]).astype(BF16)
        cov = nn(turned, low) + tall[:, 0:1] * total
        cov = 0.5 * (cov + cov.T)
        packed = cov[0:64]
        for k in range(1, 4):
            packed = jnp.where(group == k, cov[64 * k : 64 * k + 64], packed)
        if z % 2 == 0:
            upper = packed
        else:
            blocks[z // 2, 0:64, :] = jnp.where(below <= 0, upper, packed)
        diagonal = jnp.sum(jnp.where(below == 0, packed, 0.0), axis=0, keepdims=True)
        tail = jnp.where(row == 0, total, jnp.where(row == 1, sums[:, lanes], 0.0))
        tail = jnp.where(row == 5, diagonal, tail)
        if z < 3:
            for a, part in enumerate((sum0, sum1, sum2)):
                tail = jnp.where(row == 2 + a, part[0:1, lanes], tail)
        own[:, lanes] = tail
        blocks[z // 2, 64 + 8 * (z % 2) : 72 + 8 * (z % 2), :] = tail
        basis = block_vectors(vectors, z, same)
        for k, piece in enumerate(pieces(basis, 2) + pieces(basis.T, 2)):
            bases[z, k] = piece
        factor = -(tall[:, 1:2] * scale) / (tall[:, 2:3] + root)
        factors[z] = jnp.where(same, factor, 0.0)
    core = lax.axis_index("c")
    mine[...] = blocks[core]
    theirs[...] = blocks[1 - core]


def back_part(cols, slabs, xc, sums, colsums, vectors, values):
    return pl.pallas_call(
        back_kernel,
        in_specs=[ON_CHIP] * 11,
        out_specs=(ON_CHIP,) * 6,
        out_shape=(
            jax.ShapeDtypeStruct((ROWS, D), BF16),
            jax.ShapeDtypeStruct((8, D), F32),
            jax.ShapeDtypeStruct((80, 256), F32),
            jax.ShapeDtypeStruct((80, 256), F32),
            jax.ShapeDtypeStruct((4, 4, 256, 256), BF16),
            jax.ShapeDtypeStruct((4, 256, 256), F32),
        ),
        scratch_shapes=[pltpu.VMEM((2, 80, 256), F32)],
        compiler_params=pltpu.CompilerParams(vmem_limit_bytes=14 << 20),
        name="back_part",
    )(cols, *slabs, xc, sums, *colsums, vectors, values)


def final_kernel(
    dev,
    xc,
    mine,
    theirs,
    own,
    bases,
    factors,
    whiten,
    out,
    fix,
    blocks,
    shift,
    sigma,
    row_vector,
    done,
    sent,
):
    core = lax.axis_index("c")
    blocks[core] = mine[...]
    blocks[1 - core] = theirs[...]
    below = (lax.broadcasted_iota(jnp.int32, (256, 256), 0) & 63) - (
        lax.broadcasted_iota(jnp.int32, (256, 256), 1) & 63
    )
    for z in range(4):
        lanes = slice(256 * z, 256 * z + 256)
        start = 64 + 8 * (z % 2)
        tail = blocks[z // 2, start : start + 8, :]
        total, mean = tail[0:1], tail[1:2] * (1.0 / TOTAL)
        packed = blocks[z // 2, 0:64, :]
        square = jnp.concatenate([packed, packed, packed, packed], axis=0)
        if z % 2 == 0:
            raw = jnp.where(below <= 0, square, square.T)
        else:
            raw = jnp.where(below > 0, square, square.T)
            raw = jnp.where(below == 0, tail[5:6], raw)
        tall = columns_of([total, mean])
        cov = raw - 0.5 * (tall[:, 1:2] * total + tall[:, 0:1] * mean)
        basis, turned = (bases[z, 0], bases[z, 1]), (bases[z, 2], bases[z, 3])
        rotated = fine(nn, turned, fine(nn, cov, basis))
        grad = fine(nn, basis, fine(nn, rotated * factors[z], turned))
        sigma[z] = (grad * (2.0 / TOTAL)).astype(BF16)
        moved = own[0:1, lanes] * (1.0 / PIXELS) - total * (1.0 / TOTAL)
        offset = own[1:2, lanes] * (1.0 / PIXELS) - mean
        empty = [jnp.zeros((1, 256), BF16)]
        stacked = jnp.concatenate(pieces(moved, 3) + pieces(mean, 3) + empty * 2, axis=0)
        through = nn(stacked, whiten[z])
        stacked = jnp.concatenate(pieces(offset, 3) + empty * 5, axis=0)
        other = nn(stacked, sigma[z])
        row_vector[0:1, lanes] = (
            jnp.sum(through[0:3], axis=0, keepdims=True)
            + jnp.sum(other[0:3], axis=0, keepdims=True)
        )
        shift[0:1, lanes] = jnp.sum(through[3:6], axis=0, keepdims=True)
    first = 8 * sum(STRIDE[axis] * lax.axis_index(axis) for axis in ALL)
    lane = lax.broadcasted_iota(jnp.int32, (8, D), 1)
    row = lax.broadcasted_iota(jnp.int32, (8, D), 0)
    chosen = jnp.where(lane == row + first, shift[...], 0.0)
    chosen = jnp.sum(chosen, axis=1, keepdims=True)
    for a in range(3):
        for z in range(3):
            start = 66 + 8 * (z % 2) + a
            fix[a, :, 256 * z : 256 * z + 256] = chosen * blocks[z // 2, start : start + 1, :]
    copies = []
    for b in range(IMAGES):
        rows = slice(H * 16 * b, H * 16 * b + H * 16)
        for z in range(4):
            lanes = slice(256 * z, 256 * z + 256)
            result = nn(dev[rows, lanes], whiten[z]) + nn(xc[rows, lanes], sigma[z])
            result = result + row_vector[0:1, lanes]
            done[b, :, :, lanes] = result.astype(BF16).reshape(H, 16, 256)[:, 0:W, :]
        copies.append(pltpu.make_async_copy(done.at[b], out.at[b], sent.at[b]))
        copies[-1].start()
    for copy in copies:
        copy.wait()


def final_part(dev, xc, mine, theirs, own, bases, factors, whiten):
    return pl.pallas_call(
        final_kernel,
        in_specs=[ON_CHIP] * 8,
        out_specs=(IN_HBM, ON_CHIP),
        out_shape=(
            jax.ShapeDtypeStruct((IMAGES, H, W, D), BF16),
            jax.ShapeDtypeStruct((3, 8, 768), F32),
        ),
        scratch_shapes=[
            pltpu.VMEM((2, 80, 256), F32),
            pltpu.VMEM((1, D), F32),
            pltpu.VMEM((4, 256, 256), BF16),
            pltpu.VMEM((1, D), F32),
            pltpu.VMEM((IMAGES, H, W, D), BF16),
            pltpu.SemaphoreType.DMA((IMAGES,)),
        ],
        compiler_params=pltpu.CompilerParams(vmem_limit_bytes=12 << 20),
        name="final_part",
    )(dev, xc, mine, theirs, own, bases, factors, whiten)


def permutation(move):
    pairs = []
    for device in range(128):
        at = {k: (device // STRIDE[k]) % SIZE[k] for k in ALL}
        move(at)
        pairs.append((device, sum(at[k] * STRIDE[k] for k in ALL)))
    return pairs


def exchange(value, move):
    return lax.ppermute(value, ALL, permutation(move))


def other_core(at):
    at["c"] ^= 1


def ring(axis, step):
    def move(at):
        at[axis] ^= (1, 3)[(step + at["c"]) % 2]

    return move


def halves(value, dim):
    pick = lambda k: lax.index_in_dim(value, k, dim, keepdims=False)
    return pick(0), pick(1)


def local(features, grads, kernel, vectors, values):
    stay = lambda array: pltpu.with_memory_space_constraint(array, pltpu.HBM)
    cols, xc, wht, u, sums, whiten = prep(stay(features), stay(grads), stay(vectors), values)
    cols, xc = cols.reshape(ROWS, 9 * O), xc.reshape(ROWS, D)
    kernel = stay(kernel.reshape(9 * O, D))

    parts, colsums, slabs = [], [], []
    for a in range(3):
        keep, send, colsum, slab = weight_part(wht, cols, u, kernel, a)
        colsums.append(colsum)
        slabs.append(slab)
        parts.append((keep + exchange(send, other_core)).reshape(2, 2, 2, 2, 2, 2, 8, 768))
    cols = lax.optimization_barrier((cols, *parts))[0]
    dev, own, mine, theirs, bases, factors = back_part(
        cols, slabs, xc, sums, colsums, vectors, values
    )
    mine = mine + exchange(theirs, other_core)

    names = [["z1", "z2", "y1", "y2", "x1", "x2"] for _ in range(3)]

    def turn(k):
        for a in range(3):
            axis = "xyz"[(a + k) % 3]
            dim = names[a].index(axis + "1")
            names[a].pop(dim)
            keep, send = halves(parts[a], dim)
            parts[a] = keep + exchange(send, ring(axis, 0))

    moves = [ring(axis, step) for axis in "xyz" for step in range(2)]

    def after(value, *others):
        return lax.optimization_barrier((value, *others))[0]

    turn(0)
    mine, *parts = lax.optimization_barrier((mine, *parts))
    one = mine + exchange(mine, moves[0])
    two = one + exchange(one, moves[1])
    turn(1)
    two, *parts = lax.optimization_barrier((two, *parts))
    three = two + exchange(two, moves[2])
    four = three + exchange(three, moves[3])
    turn(2)
    share = after(jnp.stack(parts, axis=3), three)
    four = after(four, share)
    five = four + exchange(four, moves[4])
    order = ["z", "y", "x"]
    for axis, ahead in (("x", None), ("y", four), ("z", five)):
        if ahead is not None:
            share = after(share, ahead)
        dim = order.index(axis)
        order.pop(dim)
        keep, send = halves(share, dim)
        share = keep + exchange(send, ring(axis, 1))
        if axis == "x":
            five = after(five, share)
            six = five + exchange(five, moves[5])
    mine, theirs = six, exchange(six, other_core)

    input_grad, fix = final_part(dev, xc, mine, theirs, own, bases, factors, whiten)
    kernel_grad = (share - fix).transpose(1, 0, 2).reshape(8, 3, 3, O)
    return input_grad, kernel_grad


def solution(mesh):
    finer = Mesh(mesh.devices.reshape(4, 4, 2, 4), ALL)
    split_all = P(ALL, None, None, None)
    return jax.shard_map(
        local,
        mesh=finer,
        in_specs=(split_all, split_all, P(), P(), P()),
        out_specs=(split_all, split_all),
        check_vma=False,
    )
```

```python
import functools

import jax
import jax.numpy as jnp
import numpy as np
from jax import lax
from jax.experimental import pallas as pl
from jax.experimental.pallas import tpu as pltpu
from jax.sharding import Mesh
from jax.sharding import PartitionSpec as P

ALL = ("z", "y", "c", "x")
SIZE = {"z": 4, "y": 4, "c": 2, "x": 4}
STRIDE = {"z": 32, "y": 8, "c": 4, "x": 1}
RING = ((0, 3, 1, 2), (0, 1, 3, 2))
F32 = jnp.float32
BF16 = jnp.bfloat16
IMAGES, H, W, D, O = 6, 14, 14, 1024, 256
ROWS = IMAGES * H * 16
PIXELS = IMAGES * H * W
TOTAL = 128.0 * PIXELS
ON_CHIP = pl.BlockSpec(memory_space=pltpu.VMEM)
IN_HBM = pl.BlockSpec(memory_space=pltpu.HBM)


def nt(a, b):
    return lax.dot_general(
        a, b, (((1,), (1,)), ((), ())), preferred_element_type=F32
    )


def tn(a, b):
    return lax.dot_general(
        a, b, (((0,), (0,)), ((), ())), preferred_element_type=F32
    )


def nn(a, b):
    return lax.dot_general(
        a, b, (((1,), (0,)), ((), ())), preferred_element_type=F32
    )


def same_group():
    row = lax.broadcasted_iota(jnp.int32, (256, 256), 0)
    col = lax.broadcasted_iota(jnp.int32, (256, 256), 1)
    return (row >> 6) == (col >> 6)


def block_vectors(vectors, z, same):
    four = vectors[4 * z : 4 * z + 4].reshape(256, 64)
    return jnp.where(same, jnp.concatenate([four, four, four, four], axis=1), 0.0)


def value_row(values, z):
    return jnp.concatenate([values[4 * z + g : 4 * z + g + 1, :] for g in range(4)], axis=1)


def columns_of(rows):
    rows = rows + [jnp.zeros((1, 256), F32)] * (8 - len(rows))
    return jnp.concatenate(rows, axis=0).T


def pieces(a, n):
    out = []
    for _ in range(n):
        out.append(a.astype(BF16))
        a = a - out[-1].astype(F32)
    return out


def fine(dot, a, b):
    a_high, a_low = a if isinstance(a, tuple) else pieces(a, 2)
    b_high, b_low = b if isinstance(b, tuple) else pieces(b, 2)
    return dot(a_high, b_high) + (dot(a_high, b_low) + dot(a_low, b_high))


def place():
    core = lax.axis_index("c")
    spots = ([], [])
    for axis in "zyx":
        i = lax.axis_index(axis)
        a, b = (i ^ (i >> 1)) & 1, i >> 1
        spots[0].append(2 * a + b)
        spots[1].append(2 * b + a)
    return core, spots


def prep_kernel(
    features_hbm,
    grads_hbm,
    vectors_hbm,
    values,
    cols,
    xc,
    wht,
    u,
    sums,
    whiten,
    wide,
    wp32,
    features,
    grads,
    vectors,
    arrived,
):
    copies = [
        pltpu.make_async_copy(source, target, arrived.at[k])
        for k, (source, target) in enumerate(
            ((vectors_hbm, vectors), (grads_hbm, grads), (features_hbm, features))
        )
    ]
    for copy in copies:
        copy.start()
    core, spots = place()
    same = same_group()
    wide[...] = jnp.zeros_like(wide)
    xc[...] = jnp.zeros_like(xc)
    wht[1024:1040, :] = jnp.ones((16, ROWS), BF16)
    copies[0].wait()
    for z in range(4):
        basis = block_vectors(vectors, z, same)
        scale = lax.rsqrt(value_row(values, z))
        full = fine(nt, basis * scale, basis)
        whiten[z] = full.astype(BF16)
        for c in range(2):
            at_z, at_y, at_x = spots[c]
            for row, (y, x) in enumerate((y, x) for y in RING[c] for x in RING[c]):
                channel = y * 64 + c * 32 + x * 8
                row = pl.multiple_of(8 * (row ^ (4 * at_y + at_x)), 8)
                wp32[4 * c + z, pl.ds(row, 8), :] = full[channel : channel + 8, :]
    copies[1].wait()
    inside = lax.broadcasted_iota(jnp.int32, (H, 16, O), 1) < W
    for b in range(IMAGES):
        wide[:, 8 : 8 + W, :] = grads[b].astype(F32)
        for c in range(3):
            shifted = wide[:, 9 - c : 25 - c, :]
            if c == 2:
                shifted = jnp.where(inside, shifted, 0.0)
            shifted = shifted.astype(BF16)
            for a in range(3):
                lane = (3 * a + c) * O
                first, last = b * H + max(0, a - 1), b * H + H - max(0, 1 - a)
                start = max(0, 1 - a)
                cols[first:last, :, lane : lane + O] = shifted[start : start + last - first]
                if a == 0:
                    cols[b * H + H - 1, :, lane : lane + O] = jnp.zeros((16, O), BF16)
                if a == 2:
                    cols[b * H, :, lane : lane + O] = jnp.zeros((16, O), BF16)
    copies[2].wait()
    total = jnp.zeros((1, D), F32)
    for b in range(IMAGES):
        total = total + jnp.sum(
            jnp.sum(features[b].astype(F32), axis=0), axis=0, keepdims=True
        )
    sums[...] = total
    mean = total * (1.0 / PIXELS)
    for b in range(IMAGES):
        xc[b * H : b * H + H, 0:W, :] = (features[b].astype(F32) - mean[None]).astype(BF16)
    high, middle, low = pieces(mean, 3)
    pad = lax.broadcasted_iota(jnp.int32, (16, D), 0)
    head = xc[0].astype(F32)
    head = jnp.where(pad == 14, high.astype(F32), jnp.where(pad == 15, middle.astype(F32), head))
    xc[0] = head.astype(BF16)
    head = xc[1].astype(F32)
    xc[1] = jnp.where(pad == 14, low.astype(F32), head).astype(BF16)
    for k in range(8):
        c, z = k // 4, k % 4
        chunk = xc[:, :, 256 * z : 256 * z + 256].reshape(ROWS, 256)
        part = nt(wp32[k].astype(BF16), chunk)
        row = 4 * (c ^ core) + (RING[c].index(z) ^ spots[c][0])
        row = pl.multiple_of(128 * row, 128)
        wht[pl.ds(row, 128), :] = part.astype(BF16)
        shift = part[:, 14:15] + part[:, 15:16] + part[:, 30:31]
        u[pl.ds(row, 128), :] = jnp.broadcast_to(shift, (128, 128))


def prep(features, grads, vectors, values):
    return pl.pallas_call(
        prep_kernel,
        out_shape=(
            jax.ShapeDtypeStruct((IMAGES * H, 16, 9 * O), BF16),
            jax.ShapeDtypeStruct((IMAGES * H, 16, D), BF16),
            jax.ShapeDtypeStruct((1040, ROWS), BF16),
            jax.ShapeDtypeStruct((1024, 128), F32),
            jax.ShapeDtypeStruct((1, D), F32),
            jax.ShapeDtypeStruct((4, 256, 256), BF16),
        ),
        in_specs=[IN_HBM] * 3 + [ON_CHIP],
        out_specs=(ON_CHIP,) * 6,
        scratch_shapes=[
            pltpu.VMEM((H, 32, O), F32),
            pltpu.VMEM((8, 128, 256), F32),
            pltpu.VMEM((IMAGES, H, W, D), BF16),
            pltpu.VMEM((IMAGES, H, W, O), BF16),
            pltpu.VMEM((16, 64, 64), F32),
            pltpu.SemaphoreType.DMA((3,)),
        ],
        compiler_params=pltpu.CompilerParams(vmem_limit_bytes=10 << 20),
        name="prep",
    )(features, grads, vectors, values)


def weight_kernel(a, wht, cols, u, kernel_hbm, keep, send, colsum, slab, arrived):
    copy = pltpu.make_async_copy(kernel_hbm.at[pl.ds(768 * a, 768)], slab, arrived)
    copy.start()
    for n in range(3):
        start = 768 * a + 256 * n
        full = nn(wht[...], cols[:, start : start + 256])
        colsum[:, 256 * n : 256 * n + 256] = full[1024:1032, :]
        for k in range(2):
            ones = full[1024:1025, 128 * k : 128 * k + 128]
            lanes = slice(256 * n + 128 * k, 256 * n + 128 * k + 128)
            part = full[0:1024, 128 * k : 128 * k + 128] + u[...] * ones
            keep[:, lanes] = part[0:512]
            send[:, lanes] = part[512:1024]
    copy.wait()


def weight_part(wht, cols, u, kernel, a):
    return pl.pallas_call(
        functools.partial(weight_kernel, a),
        in_specs=[ON_CHIP] * 3 + [IN_HBM],
        out_specs=(ON_CHIP,) * 4,
        out_shape=(
            jax.ShapeDtypeStruct((512, 768), F32),
            jax.ShapeDtypeStruct((512, 768), F32),
            jax.ShapeDtypeStruct((8, 768), F32),
            jax.ShapeDtypeStruct((768, D), BF16),
        ),
        scratch_shapes=[pltpu.SemaphoreType.DMA],
        compiler_params=pltpu.CompilerParams(vmem_limit_bytes=6 << 20),
        name=f"weight_part_{a}",
    )(wht, cols, u, kernel)


def back_kernel(
    cols,
    slab0,
    slab1,
    slab2,
    xc,
    sums,
    sum0,
    sum1,
    sum2,
    vectors,
    values,
    dev,
    own,
    mine,
    theirs,
    bases,
    factors,
    blocks,
    tails,
):
    same = same_group()
    real = (lax.broadcasted_iota(jnp.int32, (ROWS, 256), 0) & 15) < W
    group = lax.broadcasted_iota(jnp.int32, (64, 256), 1) >> 6
    below = lax.broadcasted_iota(jnp.int32, (64, 256), 0) - (
        lax.broadcasted_iota(jnp.int32, (64, 256), 1) & 63
    )
    row = lax.broadcasted_iota(jnp.int32, (8, 256), 0)
    upper = None
    for z in range(4):
        lanes = slice(256 * z, 256 * z + 256)
        back = nn(cols[:, 0:768], slab0[:, lanes])
        back = back + nn(cols[:, 768:1536], slab1[:, lanes])
        back = back + nn(cols[:, 1536:2304], slab2[:, lanes])
        total = jnp.sum(back, axis=0, keepdims=True)
        low = jnp.where(real, back - total * (1.0 / PIXELS), 0.0).astype(BF16)
        dev[:, lanes] = low
        tails[z : z + 1, :] = total
    for z in range(4):
        lanes = slice(256 * z, 256 * z + 256)
        total = tails[z : z + 1, :]
        value = value_row(values, z)
        scale, root = lax.rsqrt(value), jnp.sqrt(value)
        tall = columns_of([sums[:, lanes] * (1.0 / PIXELS), scale, root])
        cov = tn(xc[:, lanes], dev[:, lanes]) + tall[:, 0:1] * total
        cov = 0.5 * (cov + cov.T)
        packed = cov[0:64]
        for k in range(1, 4):
            packed = jnp.where(group == k, cov[64 * k : 64 * k + 64], packed)
        if z % 2 == 0:
            upper = packed
        else:
            blocks[z // 2, 0:64, :] = jnp.where(below <= 0, upper, packed)
        diagonal = jnp.sum(jnp.where(below == 0, packed, 0.0), axis=0, keepdims=True)
        tail = jnp.where(row == 0, total, jnp.where(row == 1, sums[:, lanes], 0.0))
        tail = jnp.where(row == 5, diagonal, tail)
        if z < 3:
            for a, part in enumerate((sum0, sum1, sum2)):
                tail = jnp.where(row == 2 + a, part[0:1, lanes], tail)
        own[:, lanes] = tail
        blocks[z // 2, 64 + 8 * (z % 2) : 72 + 8 * (z % 2), :] = tail
        basis = block_vectors(vectors, z, same)
        for k, piece in enumerate(pieces(basis, 2) + pieces(basis.T, 2)):
            bases[z, k] = piece
        factor = -(tall[:, 1:2] * scale) / (tall[:, 2:3] + root)
        factors[z] = jnp.where(same, factor, 0.0)
    core = lax.axis_index("c")
    mine[...] = blocks[core]
    theirs[...] = blocks[1 - core]


def back_part(cols, slabs, xc, sums, colsums, vectors, values):
    return pl.pallas_call(
        back_kernel,
        in_specs=[ON_CHIP] * 11,
        out_specs=(ON_CHIP,) * 6,
        out_shape=(
            jax.ShapeDtypeStruct((ROWS, D), BF16),
            jax.ShapeDtypeStruct((8, D), F32),
            jax.ShapeDtypeStruct((80, 256), F32),
            jax.ShapeDtypeStruct((80, 256), F32),
            jax.ShapeDtypeStruct((4, 4, 256, 256), BF16),
            jax.ShapeDtypeStruct((4, 256, 256), F32),
        ),
        scratch_shapes=[pltpu.VMEM((2, 80, 256), F32), pltpu.VMEM((8, 256), F32)],
        compiler_params=pltpu.CompilerParams(vmem_limit_bytes=14 << 20),
        name="back_part",
    )(cols, *slabs, xc, sums, *colsums, vectors, values)


def final_kernel(
    dev,
    xc,
    mine,
    theirs,
    own,
    bases,
    factors,
    whiten,
    out,
    fix,
    blocks,
    shift,
    sigma,
    row_vector,
    done,
    sent,
):
    core = lax.axis_index("c")
    blocks[core] = mine[...]
    blocks[1 - core] = theirs[...]
    below = (lax.broadcasted_iota(jnp.int32, (256, 256), 0) & 63) - (
        lax.broadcasted_iota(jnp.int32, (256, 256), 1) & 63
    )
    for z in range(4):
        lanes = slice(256 * z, 256 * z + 256)
        start = 64 + 8 * (z % 2)
        tail = blocks[z // 2, start : start + 8, :]
        total, mean = tail[0:1], tail[1:2] * (1.0 / TOTAL)
        packed = blocks[z // 2, 0:64, :]
        square = jnp.concatenate([packed, packed, packed, packed], axis=0)
        if z % 2 == 0:
            raw = jnp.where(below <= 0, square, square.T)
        else:
            raw = jnp.where(below > 0, square, square.T)
            raw = jnp.where(below == 0, tail[5:6], raw)
        tall = columns_of([total, mean])
        cov = raw - 0.5 * (tall[:, 1:2] * total + tall[:, 0:1] * mean)
        basis, turned = (bases[z, 0], bases[z, 1]), (bases[z, 2], bases[z, 3])
        rotated = fine(nn, turned, fine(nn, cov, basis))
        grad = fine(nn, basis, fine(nn, rotated * factors[z], turned))
        sigma[z] = (grad * (2.0 / TOTAL)).astype(BF16)
        moved = own[0:1, lanes] * (1.0 / PIXELS) - total * (1.0 / TOTAL)
        offset = own[1:2, lanes] * (1.0 / PIXELS) - mean
        empty = [jnp.zeros((1, 256), BF16)]
        stacked = jnp.concatenate(pieces(moved, 3) + pieces(mean, 3) + empty * 2, axis=0)
        through = nn(stacked, whiten[z])
        stacked = jnp.concatenate(pieces(offset, 3) + empty * 5, axis=0)
        other = nn(stacked, sigma[z])
        row_vector[0:1, lanes] = (
            jnp.sum(through[0:3], axis=0, keepdims=True)
            + jnp.sum(other[0:3], axis=0, keepdims=True)
        )
        shift[0:1, lanes] = jnp.sum(through[3:6], axis=0, keepdims=True)
    first = 8 * sum(STRIDE[axis] * lax.axis_index(axis) for axis in ALL)
    lane = lax.broadcasted_iota(jnp.int32, (8, D), 1)
    row = lax.broadcasted_iota(jnp.int32, (8, D), 0)
    chosen = jnp.where(lane == row + first, shift[...], 0.0)
    chosen = jnp.sum(chosen, axis=1, keepdims=True)
    for a in range(3):
        for z in range(3):
            start = 66 + 8 * (z % 2) + a
            fix[a, :, 256 * z : 256 * z + 256] = chosen * blocks[z // 2, start : start + 1, :]
    copies = []
    for b in range(IMAGES):
        rows = slice(H * 16 * b, H * 16 * b + H * 16)
        for z in range(4):
            lanes = slice(256 * z, 256 * z + 256)
            result = nn(dev[rows, lanes], whiten[z]) + nn(xc[rows, lanes], sigma[z])
            result = result + row_vector[0:1, lanes]
            done[b, :, :, lanes] = result.astype(BF16).reshape(H, 16, 256)[:, 0:W, :]
        copies.append(pltpu.make_async_copy(done.at[b], out.at[b], sent.at[b]))
        copies[-1].start()
    for copy in copies:
        copy.wait()


def final_part(dev, xc, mine, theirs, own, bases, factors, whiten):
    return pl.pallas_call(
        final_kernel,
        in_specs=[ON_CHIP] * 8,
        out_specs=(IN_HBM, ON_CHIP),
        out_shape=(
            jax.ShapeDtypeStruct((IMAGES, H, W, D), BF16),
            jax.ShapeDtypeStruct((3, 8, 768), F32),
        ),
        scratch_shapes=[
            pltpu.VMEM((2, 80, 256), F32),
            pltpu.VMEM((1, D), F32),
            pltpu.VMEM((4, 256, 256), BF16),
            pltpu.VMEM((1, D), F32),
            pltpu.VMEM((IMAGES, H, W, D), BF16),
            pltpu.SemaphoreType.DMA((IMAGES,)),
        ],
        compiler_params=pltpu.CompilerParams(vmem_limit_bytes=12 << 20),
        name="final_part",
    )(dev, xc, mine, theirs, own, bases, factors, whiten)


def permutation(move):
    pairs = []
    for device in range(128):
        at = {k: (device // STRIDE[k]) % SIZE[k] for k in ALL}
        move(at)
        pairs.append((device, sum(at[k] * STRIDE[k] for k in ALL)))
    return pairs


def exchange(value, move):
    return lax.ppermute(value, ALL, permutation(move))


def other_core(at):
    at["c"] ^= 1


def ring(axis, step):
    def move(at):
        at[axis] ^= (1, 3)[(step + at["c"]) % 2]

    return move


def halves(value, dim):
    pick = lambda k: lax.index_in_dim(value, k, dim, keepdims=False)
    return pick(0), pick(1)


def local(features, grads, kernel, vectors, values):
    stay = lambda array: pltpu.with_memory_space_constraint(array, pltpu.HBM)
    cols, xc, wht, u, sums, whiten = prep(stay(features), stay(grads), stay(vectors), values)
    cols, xc = cols.reshape(ROWS, 9 * O), xc.reshape(ROWS, D)
    kernel = stay(kernel.reshape(9 * O, D))

    parts, colsums, slabs = [], [], []
    for a in range(3):
        keep, send, colsum, slab = weight_part(wht, cols, u, kernel, a)
        colsums.append(colsum)
        slabs.append(slab)
        parts.append((keep + exchange(send, other_core)).reshape(2, 2, 2, 2, 2, 2, 8, 768))
    cols = lax.optimization_barrier((cols, *parts))[0]
    dev, own, mine, theirs, bases, factors = back_part(
        cols, slabs, xc, sums, colsums, vectors, values
    )
    mine = mine + exchange(theirs, other_core)

    names = [["z1", "z2", "y1", "y2", "x1", "x2"] for _ in range(3)]

    def turn(k):
        for a in range(3):
            axis = "xyz"[(a + k) % 3]
            dim = names[a].index(axis + "1")
            names[a].pop(dim)
            keep, send = halves(parts[a], dim)
            parts[a] = keep + exchange(send, ring(axis, 0))

    moves = [ring(axis, step) for axis in "xyz" for step in range(2)]

    def after(value, *others):
        return lax.optimization_barrier((value, *others))[0]

    turn(0)
    mine, *parts = lax.optimization_barrier((mine, *parts))
    one = mine + exchange(mine, moves[0])
    two = one + exchange(one, moves[1])
    turn(1)
    two, *parts = lax.optimization_barrier((two, *parts))
    three = two + exchange(two, moves[2])
    four = three + exchange(three, moves[3])
    turn(2)
    share = after(jnp.stack(parts, axis=3), four)
    five = four + exchange(four, moves[4])
    order = ["z", "y", "x"]
    for axis in "xyz":
        if axis == "y":
            share = after(share, five)
            six = after(five, share)
            six = six + exchange(six, moves[5])
        dim = order.index(axis)
        order.pop(dim)
        keep, send = halves(share, dim)
        share = keep + exchange(send, ring(axis, 1))
    mine, theirs = six, exchange(six, other_core)

    input_grad, fix = final_part(dev, xc, mine, theirs, own, bases, factors, whiten)
    kernel_grad = (share - fix).transpose(1, 0, 2).reshape(8, 3, 3, O)
    return input_grad, kernel_grad


def solution(mesh):
    finer = Mesh(mesh.devices.reshape(4, 4, 2, 4), ALL)
    split_all = P(ALL, None, None, None)
    return jax.shard_map(
        local,
        mesh=finer,
        in_specs=(split_all, split_all, P(), P(), P()),
        out_specs=(split_all, split_all),
        check_vma=False,
    )
```

```python
import functools

import jax
import jax.numpy as jnp
import numpy as np
from jax import lax
from jax.experimental import pallas as pl
from jax.experimental.pallas import tpu as pltpu
from jax.sharding import Mesh
from jax.sharding import PartitionSpec as P

ALL = ("z", "y", "c", "x")
SIZE = {"z": 4, "y": 4, "c": 2, "x": 4}
STRIDE = {"z": 32, "y": 8, "c": 4, "x": 1}
ORDERS = ((0, 3, 1, 2), (0, 1, 3, 2))
FLIP = {"z": 0, "y": 1, "x": 0}
RING = [{axis: ORDERS[(c + FLIP[axis]) % 2] for axis in "zyx"} for c in range(2)]
F32 = jnp.float32
BF16 = jnp.bfloat16
IMAGES, H, W, D, O = 6, 14, 14, 1024, 256
ROWS = IMAGES * H * 16
WIDE = 9 * O // 2
PIXELS = IMAGES * H * W
TOTAL = 128.0 * PIXELS
ON_CHIP = pl.BlockSpec(memory_space=pltpu.VMEM)
IN_HBM = pl.BlockSpec(memory_space=pltpu.HBM)


def nt(a, b):
    return lax.dot_general(
        a, b, (((1,), (1,)), ((), ())), preferred_element_type=F32
    )


def tn(a, b):
    return lax.dot_general(
        a, b, (((0,), (0,)), ((), ())), preferred_element_type=F32
    )


def nn(a, b):
    return lax.dot_general(
        a, b, (((1,), (0,)), ((), ())), preferred_element_type=F32
    )


def same_group():
    row = lax.broadcasted_iota(jnp.int32, (256, 256), 0)
    col = lax.broadcasted_iota(jnp.int32, (256, 256), 1)
    return (row >> 6) == (col >> 6)


def block_vectors(vectors, z, same):
    four = vectors[4 * z : 4 * z + 4].reshape(256, 64)
    return jnp.where(same, jnp.concatenate([four, four, four, four], axis=1), 0.0)


def value_row(values, z):
    return jnp.concatenate([values[4 * z + g : 4 * z + g + 1, :] for g in range(4)], axis=1)


def columns_of(rows):
    rows = rows + [jnp.zeros((1, 256), F32)] * (8 - len(rows))
    return jnp.concatenate(rows, axis=0).T


def pieces(a, n):
    out = []
    for _ in range(n):
        out.append(a.astype(BF16))
        a = a - out[-1].astype(F32)
    return out


def fine(dot, a, b):
    a_high, a_low = a if isinstance(a, tuple) else pieces(a, 2)
    b_high, b_low = b if isinstance(b, tuple) else pieces(b, 2)
    return dot(a_high, b_high) + (dot(a_high, b_low) + dot(a_low, b_high))


def place():
    core = lax.axis_index("c")
    spots = ([], [])
    for axis in "zyx":
        i = lax.axis_index(axis)
        a, b = (i ^ (i >> 1)) & 1, i >> 1
        for c in range(2):
            spots[c].append(2 * a + b if (c + FLIP[axis]) % 2 == 0 else 2 * b + a)
    return core, spots


def prep_kernel(
    features_hbm,
    grads_hbm,
    vectors_hbm,
    values,
    cols,
    xc,
    wht,
    u,
    sums,
    whiten,
    wide,
    wp32,
    features,
    grads,
    vectors,
    arrived,
):
    copies = [
        pltpu.make_async_copy(source, target, arrived.at[k])
        for k, (source, target) in enumerate(
            ((vectors_hbm, vectors), (grads_hbm, grads), (features_hbm, features))
        )
    ]
    for copy in copies:
        copy.start()
    core, spots = place()
    same = same_group()
    wide[...] = jnp.zeros_like(wide)
    xc[...] = jnp.zeros_like(xc)
    wht[1024:1040, :] = jnp.ones((16, ROWS), BF16)
    copies[0].wait()
    for z in range(4):
        basis = block_vectors(vectors, z, same)
        scale = lax.rsqrt(value_row(values, z))
        full = fine(nt, basis * scale, basis)
        whiten[z] = full.astype(BF16)
        for c in range(2):
            at_z, at_y, at_x = spots[c]
            order = [(y, x) for y in RING[c]["y"] for x in RING[c]["x"]]
            for row, (y, x) in enumerate(order):
                channel = y * 64 + c * 32 + x * 8
                row = pl.multiple_of(8 * (row ^ (4 * at_y + at_x)), 8)
                wp32[4 * c + z, pl.ds(row, 8), :] = full[channel : channel + 8, :]
    copies[1].wait()
    inside = lax.broadcasted_iota(jnp.int32, (H, 16, O), 1) < W
    for b in range(IMAGES):
        wide[:, 8 : 8 + W, :] = grads[b].astype(F32)
        for c in range(3):
            shifted = wide[:, 9 - c : 25 - c, :]
            if c == 2:
                shifted = jnp.where(inside, shifted, 0.0)
            shifted = shifted.astype(BF16)
            for a in range(3):
                lane = (3 * a + c) * O
                first, last = b * H + max(0, a - 1), b * H + H - max(0, 1 - a)
                start = max(0, 1 - a)
                cols[first:last, :, lane : lane + O] = shifted[start : start + last - first]
                if a == 0:
                    cols[b * H + H - 1, :, lane : lane + O] = jnp.zeros((16, O), BF16)
                if a == 2:
                    cols[b * H, :, lane : lane + O] = jnp.zeros((16, O), BF16)
    copies[2].wait()
    total = jnp.zeros((1, D), F32)
    for b in range(IMAGES):
        total = total + jnp.sum(
            jnp.sum(features[b].astype(F32), axis=0), axis=0, keepdims=True
        )
    sums[...] = total
    mean = total * (1.0 / PIXELS)
    for b in range(IMAGES):
        xc[b * H : b * H + H, 0:W, :] = (features[b].astype(F32) - mean[None]).astype(BF16)
    high, middle, low = pieces(mean, 3)
    pad = lax.broadcasted_iota(jnp.int32, (16, D), 0)
    head = xc[0].astype(F32)
    head = jnp.where(pad == 14, high.astype(F32), jnp.where(pad == 15, middle.astype(F32), head))
    xc[0] = head.astype(BF16)
    head = xc[1].astype(F32)
    xc[1] = jnp.where(pad == 14, low.astype(F32), head).astype(BF16)
    for k in range(8):
        c, z = k // 4, k % 4
        chunk = xc[:, :, 256 * z : 256 * z + 256].reshape(ROWS, 256)
        part = nt(wp32[k].astype(BF16), chunk)
        row = 4 * (c ^ core) + (RING[c]["z"].index(z) ^ spots[c][0])
        row = pl.multiple_of(128 * row, 128)
        wht[pl.ds(row, 128), :] = part.astype(BF16)
        shift = part[:, 14:15] + part[:, 15:16] + part[:, 30:31]
        u[pl.ds(row, 128), :] = jnp.broadcast_to(shift, (128, 128))


def prep(features, grads, vectors, values):
    return pl.pallas_call(
        prep_kernel,
        out_shape=(
            jax.ShapeDtypeStruct((IMAGES * H, 16, 9 * O), BF16),
            jax.ShapeDtypeStruct((IMAGES * H, 16, D), BF16),
            jax.ShapeDtypeStruct((1040, ROWS), BF16),
            jax.ShapeDtypeStruct((1024, 128), F32),
            jax.ShapeDtypeStruct((1, D), F32),
            jax.ShapeDtypeStruct((4, 256, 256), BF16),
        ),
        in_specs=[IN_HBM] * 3 + [ON_CHIP],
        out_specs=(ON_CHIP,) * 6,
        scratch_shapes=[
            pltpu.VMEM((H, 32, O), F32),
            pltpu.VMEM((8, 128, 256), F32),
            pltpu.VMEM((IMAGES, H, W, D), BF16),
            pltpu.VMEM((IMAGES, H, W, O), BF16),
            pltpu.VMEM((16, 64, 64), F32),
            pltpu.SemaphoreType.DMA((3,)),
        ],
        compiler_params=pltpu.CompilerParams(vmem_limit_bytes=10 << 20),
        name="prep",
    )(features, grads, vectors, values)


def weight_kernel(a, wht, cols, u, kernel_hbm, keep, send, colsum, slab, arrived):
    copy = pltpu.make_async_copy(kernel_hbm.at[pl.ds(WIDE * a, WIDE)], slab, arrived)
    copy.start()
    for start, size in ((0, 256), (256, 256), (512, 256), (768, 384)):
        full = nn(wht[...], cols[:, WIDE * a + start : WIDE * a + start + size])
        colsum[:, start : start + size] = full[1024:1032, :]
        for k in range(size // 128):
            ones = full[1024:1025, 128 * k : 128 * k + 128]
            lanes = slice(start + 128 * k, start + 128 * k + 128)
            part = full[0:1024, 128 * k : 128 * k + 128] + u[...] * ones
            keep[:, lanes] = part[0:512]
            send[:, lanes] = part[512:1024]
    copy.wait()


def weight_part(wht, cols, u, kernel, a):
    return pl.pallas_call(
        functools.partial(weight_kernel, a),
        in_specs=[ON_CHIP] * 3 + [IN_HBM],
        out_specs=(ON_CHIP,) * 4,
        out_shape=(
            jax.ShapeDtypeStruct((512, WIDE), F32),
            jax.ShapeDtypeStruct((512, WIDE), F32),
            jax.ShapeDtypeStruct((8, WIDE), F32),
            jax.ShapeDtypeStruct((WIDE, D), BF16),
        ),
        scratch_shapes=[pltpu.SemaphoreType.DMA],
        compiler_params=pltpu.CompilerParams(vmem_limit_bytes=8 << 20),
        name=f"weight_part_{a}",
    )(wht, cols, u, kernel)


def pair_of_lanes(sums, a, c):
    first = (3 * a + c) * 2
    row = [
        sums[q // 9][0:1, 128 * (q % 9) : 128 * (q % 9) + 128] for q in (first, first + 1)
    ]
    return jnp.concatenate(row, axis=1)


def back_kernel(
    cols,
    slab0,
    slab1,
    xc,
    sums,
    sum0,
    sum1,
    vectors,
    values,
    dev,
    own,
    mine,
    theirs,
    bases,
    factors,
    blocks,
    tails,
):
    same = same_group()
    real = (lax.broadcasted_iota(jnp.int32, (ROWS, 256), 0) & 15) < W
    group = lax.broadcasted_iota(jnp.int32, (64, 256), 1) >> 6
    below = lax.broadcasted_iota(jnp.int32, (64, 256), 0) - (
        lax.broadcasted_iota(jnp.int32, (64, 256), 1) & 63
    )
    row = lax.broadcasted_iota(jnp.int32, (8, 256), 0)
    upper = None
    for z in range(4):
        lanes = slice(256 * z, 256 * z + 256)
        back = nn(cols[:, 0:WIDE], slab0[:, lanes])
        back = back + nn(cols[:, WIDE : 2 * WIDE], slab1[:, lanes])
        total = jnp.sum(back, axis=0, keepdims=True)
        low = jnp.where(real, back - total * (1.0 / PIXELS), 0.0).astype(BF16)
        dev[:, lanes] = low
        tails[z : z + 1, :] = total
    for z in range(4):
        lanes = slice(256 * z, 256 * z + 256)
        total = tails[z : z + 1, :]
        value = value_row(values, z)
        scale, root = lax.rsqrt(value), jnp.sqrt(value)
        tall = columns_of([sums[:, lanes] * (1.0 / PIXELS), scale, root])
        cov = tn(xc[:, lanes], dev[:, lanes]) + tall[:, 0:1] * total
        cov = 0.5 * (cov + cov.T)
        packed = cov[0:64]
        for k in range(1, 4):
            packed = jnp.where(group == k, cov[64 * k : 64 * k + 64], packed)
        if z % 2 == 0:
            upper = packed
        else:
            blocks[z // 2, 0:64, :] = jnp.where(below <= 0, upper, packed)
        diagonal = jnp.sum(jnp.where(below == 0, packed, 0.0), axis=0, keepdims=True)
        tail = jnp.where(row == 0, total, jnp.where(row == 1, sums[:, lanes], 0.0))
        tail = jnp.where(row == 5, diagonal, tail)
        if z < 3:
            for a in range(3):
                tail = jnp.where(row == 2 + a, pair_of_lanes((sum0, sum1), a, z), tail)
        own[:, lanes] = tail
        blocks[z // 2, 64 + 8 * (z % 2) : 72 + 8 * (z % 2), :] = tail
        basis = block_vectors(vectors, z, same)
        for k, piece in enumerate(pieces(basis, 2) + pieces(basis.T, 2)):
            bases[z, k] = piece
        factor = -(tall[:, 1:2] * scale) / (tall[:, 2:3] + root)
        factors[z] = jnp.where(same, factor, 0.0)
    core = lax.axis_index("c")
    mine[...] = blocks[core]
    theirs[...] = blocks[1 - core]


def back_part(cols, slabs, xc, sums, colsums, vectors, values):
    return pl.pallas_call(
        back_kernel,
        in_specs=[ON_CHIP] * 9,
        out_specs=(ON_CHIP,) * 6,
        out_shape=(
            jax.ShapeDtypeStruct((ROWS, D), BF16),
            jax.ShapeDtypeStruct((8, D), F32),
            jax.ShapeDtypeStruct((80, 256), F32),
            jax.ShapeDtypeStruct((80, 256), F32),
            jax.ShapeDtypeStruct((4, 4, 256, 256), BF16),
            jax.ShapeDtypeStruct((4, 256, 256), F32),
        ),
        scratch_shapes=[pltpu.VMEM((2, 80, 256), F32), pltpu.VMEM((8, 256), F32)],
        compiler_params=pltpu.CompilerParams(vmem_limit_bytes=14 << 20),
        name="back_part",
    )(cols, *slabs, xc, sums, *colsums, vectors, values)


def final_kernel(
    dev,
    xc,
    mine,
    theirs,
    own,
    bases,
    factors,
    whiten,
    out,
    fix,
    blocks,
    shift,
    sigma,
    row_vector,
    done,
    sent,
):
    core = lax.axis_index("c")
    blocks[core] = mine[...]
    blocks[1 - core] = theirs[...]
    below = (lax.broadcasted_iota(jnp.int32, (256, 256), 0) & 63) - (
        lax.broadcasted_iota(jnp.int32, (256, 256), 1) & 63
    )
    every = range(4)
    chunk = [slice(256 * z, 256 * z + 256) for z in every]
    total, mean, covs = [], [], []
    for z in every:
        start = 64 + 8 * (z % 2)
        tail = blocks[z // 2, start : start + 8, :]
        total.append(tail[0:1])
        mean.append(tail[1:2] * (1.0 / TOTAL))
        packed = blocks[z // 2, 0:64, :]
        square = jnp.concatenate([packed, packed, packed, packed], axis=0)
        if z % 2 == 0:
            raw = jnp.where(below <= 0, square, square.T)
        else:
            raw = jnp.where(below > 0, square, square.T)
            raw = jnp.where(below == 0, blocks[z // 2, start + 5 : start + 6, :], raw)
        tall = columns_of([total[z], mean[z]])
        covs.append(raw - 0.5 * (tall[:, 1:2] * total[z] + tall[:, 0:1] * mean[z]))
    basis = [(bases[z, 0], bases[z, 1]) for z in every]
    turned = [(bases[z, 2], bases[z, 3]) for z in every]
    grads = [fine(nn, covs[z], basis[z]) for z in every]
    grads = [fine(nn, turned[z], grads[z]) * factors[z] for z in every]
    grads = [fine(nn, grads[z], turned[z]) for z in every]
    grads = [fine(nn, basis[z], grads[z]) for z in every]
    for z in every:
        sigma[z] = (grads[z] * (2.0 / TOTAL)).astype(BF16)
    for z in every:
        lanes = chunk[z]
        moved = own[0:1, lanes] * (1.0 / PIXELS) - total[z] * (1.0 / TOTAL)
        offset = own[1:2, lanes] * (1.0 / PIXELS) - mean[z]
        empty = [jnp.zeros((1, 256), BF16)]
        stacked = jnp.concatenate(pieces(moved, 3) + pieces(mean[z], 3) + empty * 2, axis=0)
        through = nn(stacked, whiten[z])
        stacked = jnp.concatenate(pieces(offset, 3) + empty * 5, axis=0)
        other = nn(stacked, sigma[z])
        row_vector[0:1, lanes] = jnp.sum(through[0:3], axis=0, keepdims=True) + jnp.sum(
            other[0:3], axis=0, keepdims=True
        )
        shift[0:1, lanes] = jnp.sum(through[3:6], axis=0, keepdims=True)
    first = 8 * sum(STRIDE[axis] * lax.axis_index(axis) for axis in ALL)
    lane = lax.broadcasted_iota(jnp.int32, (8, D), 1)
    row = lax.broadcasted_iota(jnp.int32, (8, D), 0)
    chosen = jnp.where(lane == row + first, shift[...], 0.0)
    chosen = jnp.sum(chosen, axis=1, keepdims=True)
    for a in range(3):
        for z in range(3):
            start = 66 + 8 * (z % 2) + a
            both = chosen * blocks[z // 2, start : start + 1, :]
            for k in range(2):
                q = (3 * a + z) * 2 + k
                lanes = slice(128 * (q % 9), 128 * (q % 9) + 128)
                fix[q // 9, :, lanes] = both[:, 128 * k : 128 * k + 128]
    copies = []
    for b in range(IMAGES):
        rows = slice(H * 16 * b, H * 16 * b + H * 16)
        for z in range(4):
            lanes = slice(256 * z, 256 * z + 256)
            result = nn(dev[rows, lanes], whiten[z]) + nn(xc[rows, lanes], sigma[z])
            result = result + row_vector[0:1, lanes]
            done[b, :, :, lanes] = result.astype(BF16).reshape(H, 16, 256)[:, 0:W, :]
        copies.append(pltpu.make_async_copy(done.at[b], out.at[b], sent.at[b]))
        copies[-1].start()
    for copy in copies:
        copy.wait()


def final_part(dev, xc, mine, theirs, own, bases, factors, whiten):
    return pl.pallas_call(
        final_kernel,
        in_specs=[ON_CHIP] * 8,
        out_specs=(IN_HBM, ON_CHIP),
        out_shape=(
            jax.ShapeDtypeStruct((IMAGES, H, W, D), BF16),
            jax.ShapeDtypeStruct((2, 8, WIDE), F32),
        ),
        scratch_shapes=[
            pltpu.VMEM((2, 80, 256), F32),
            pltpu.VMEM((1, D), F32),
            pltpu.VMEM((4, 256, 256), BF16),
            pltpu.VMEM((1, D), F32),
            pltpu.VMEM((IMAGES, H, W, D), BF16),
            pltpu.SemaphoreType.DMA((IMAGES,)),
        ],
        compiler_params=pltpu.CompilerParams(vmem_limit_bytes=12 << 20),
        name="final_part",
    )(dev, xc, mine, theirs, own, bases, factors, whiten)


def permutation(move):
    pairs = []
    for device in range(128):
        at = {k: (device // STRIDE[k]) % SIZE[k] for k in ALL}
        move(at)
        pairs.append((device, sum(at[k] * STRIDE[k] for k in ALL)))
    return pairs


def exchange(value, move):
    return lax.ppermute(value, ALL, permutation(move))


def other_core(at):
    at["c"] ^= 1


def ring(axis, step):
    def move(at):
        at[axis] ^= (1, 3)[(step + at["c"] + FLIP[axis]) % 2]

    return move


def halves(value, dim):
    pick = lambda k: lax.index_in_dim(value, k, dim, keepdims=False)
    return pick(0), pick(1)


def local(features, grads, kernel, vectors, values):
    stay = lambda array: pltpu.with_memory_space_constraint(array, pltpu.HBM)
    cols, xc, wht, u, sums, whiten = prep(stay(features), stay(grads), stay(vectors), values)
    cols, xc = cols.reshape(ROWS, 9 * O), xc.reshape(ROWS, D)
    kernel = stay(kernel.reshape(9 * O, D))

    parts, colsums, slabs = [], [], []
    for a in range(2):
        keep, send, colsum, slab = weight_part(wht, cols, u, kernel, a)
        colsums.append(colsum)
        slabs.append(slab)
        parts.append((keep + exchange(send, other_core)).reshape(2, 2, 2, 2, 2, 2, 8, WIDE))
    cols = lax.optimization_barrier((cols, *parts))[0]
    dev, own, mine, theirs, bases, factors = back_part(
        cols, slabs, xc, sums, colsums, vectors, values
    )
    mine = mine + exchange(theirs, other_core)

    names = [["z1", "z2", "y1", "y2", "x1", "x2"] for _ in range(2)]

    def turn(k):
        for a in range(2):
            axis = "xyz"[(a + k) % 3]
            dim = names[a].index(axis + "1")
            names[a].pop(dim)
            keep, send = halves(parts[a], dim)
            parts[a] = keep + exchange(send, ring(axis, 0))

    moves = [ring(axis, step) for axis in "xyz" for step in range(2)]

    def after(value, *others):
        return lax.optimization_barrier((value, *others))[0]

    turn(0)
    one = mine + exchange(mine, moves[0])
    one, *parts = lax.optimization_barrier((one, *parts))
    two = one + exchange(one, moves[1])
    turn(1)
    two, *parts = lax.optimization_barrier((two, *parts))
    three = two + exchange(two, moves[2])
    four = three + exchange(three, moves[3])
    turn(2)
    share = after(jnp.stack(parts, axis=3), four)
    five = four + exchange(four, moves[4])
    order = ["z", "y", "x"]
    for axis in "xyz":
        if axis == "y":
            share = after(share, five)
            six = after(five, share)
            six = six + exchange(six, moves[5])
        dim = order.index(axis)
        order.pop(dim)
        keep, send = halves(share, dim)
        share = keep + exchange(send, ring(axis, 1))
    mine, theirs = six, exchange(six, other_core)

    input_grad, fix = final_part(dev, xc, mine, theirs, own, bases, factors, whiten)
    kernel_grad = (share - fix).transpose(1, 0, 2).reshape(8, 9 * O).reshape(8, 3, 3, O)
    return input_grad, kernel_grad


def solution(mesh):
    finer = Mesh(mesh.devices.reshape(4, 4, 2, 4), ALL)
    split_all = P(ALL, None, None, None)
    return jax.shard_map(
        local,
        mesh=finer,
        in_specs=(split_all, split_all, P(), P(), P()),
        out_specs=(split_all, split_all),
        check_vma=False,
    )
```

```python
import functools

import jax
import jax.numpy as jnp
import numpy as np
from jax import lax
from jax.experimental import pallas as pl
from jax.experimental.pallas import tpu as pltpu
from jax.sharding import Mesh
from jax.sharding import PartitionSpec as P

ALL = ("z", "y", "c", "x")
SIZE = {"z": 4, "y": 4, "c": 2, "x": 4}
STRIDE = {"z": 32, "y": 8, "c": 4, "x": 1}
ORDERS = ((0, 3, 1, 2), (0, 1, 3, 2))
FLIP = {"z": 0, "y": 1, "x": 0}
RING = [{axis: ORDERS[(c + FLIP[axis]) % 2] for axis in "zyx"} for c in range(2)]
F32 = jnp.float32
BF16 = jnp.bfloat16
IMAGES, H, W, D, O = 6, 14, 14, 1024, 256
ROWS = IMAGES * H * 16
PIXELS = IMAGES * H * W
TOTAL = 128.0 * PIXELS
ON_CHIP = pl.BlockSpec(memory_space=pltpu.VMEM)
IN_HBM = pl.BlockSpec(memory_space=pltpu.HBM)


def nt(a, b):
    return lax.dot_general(
        a, b, (((1,), (1,)), ((), ())), preferred_element_type=F32
    )


def tn(a, b):
    return lax.dot_general(
        a, b, (((0,), (0,)), ((), ())), preferred_element_type=F32
    )


def nn(a, b):
    return lax.dot_general(
        a, b, (((1,), (0,)), ((), ())), preferred_element_type=F32
    )


def same_group():
    row = lax.broadcasted_iota(jnp.int32, (256, 256), 0)
    col = lax.broadcasted_iota(jnp.int32, (256, 256), 1)
    return (row >> 6) == (col >> 6)


def block_vectors(vectors, z, same):
    four = vectors[4 * z : 4 * z + 4].reshape(256, 64)
    return jnp.where(same, jnp.concatenate([four, four, four, four], axis=1), 0.0)


def value_row(values, z):
    return jnp.concatenate([values[4 * z + g : 4 * z + g + 1, :] for g in range(4)], axis=1)


def columns_of(rows):
    rows = rows + [jnp.zeros((1, 256), F32)] * (8 - len(rows))
    return jnp.concatenate(rows, axis=0).T


def pieces(a, n):
    out = []
    for _ in range(n):
        out.append(a.astype(BF16))
        a = a - out[-1].astype(F32)
    return out


def fine(dot, a, b):
    a_high, a_low = a if isinstance(a, tuple) else pieces(a, 2)
    b_high, b_low = b if isinstance(b, tuple) else pieces(b, 2)
    return dot(a_high, b_high) + (dot(a_high, b_low) + dot(a_low, b_high))


def place():
    core = lax.axis_index("c")
    spots = ([], [])
    for axis in "zyx":
        i = lax.axis_index(axis)
        a, b = (i ^ (i >> 1)) & 1, i >> 1
        for c in range(2):
            spots[c].append(2 * a + b if (c + FLIP[axis]) % 2 == 0 else 2 * b + a)
    return core, spots


def prep_kernel(
    features_hbm,
    grads_hbm,
    vectors_hbm,
    values_hbm,
    cols,
    xc,
    wht,
    u,
    sums,
    whiten,
    wide,
    wp32,
    features,
    grads,
    vectors,
    values,
    arrived,
):
    moves = [(values_hbm, values), (vectors_hbm, vectors), (grads_hbm, grads)]
    moves += [(features_hbm.at[b], features.at[b]) for b in range(IMAGES)]
    copies = [
        pltpu.make_async_copy(source, target, arrived.at[k])
        for k, (source, target) in enumerate(moves)
    ]
    for copy in copies:
        copy.start()
    core, spots = place()
    same = same_group()
    wide[...] = jnp.zeros_like(wide)
    xc[...] = jnp.zeros_like(xc)
    wht[1024:1040, :] = jnp.ones((16, ROWS), BF16)
    copies[0].wait()
    copies[1].wait()
    for z in range(4):
        basis = block_vectors(vectors, z, same)
        scale = lax.rsqrt(value_row(values, z))
        full = fine(nt, basis * scale, basis)
        whiten[z] = full.astype(BF16)
        for c in range(2):
            at_z, at_y, at_x = spots[c]
            order = [(y, x) for y in RING[c]["y"] for x in RING[c]["x"]]
            for row, (y, x) in enumerate(order):
                channel = y * 64 + c * 32 + x * 8
                row = pl.multiple_of(8 * (row ^ (4 * at_y + at_x)), 8)
                wp32[4 * c + z, pl.ds(row, 8), :] = full[channel : channel + 8, :]
    copies[2].wait()
    inside = lax.broadcasted_iota(jnp.int32, (H, 16, O), 1) < W
    for b in range(IMAGES):
        wide[:, 8 : 8 + W, :] = grads[b].astype(F32)
        for c in range(3):
            shifted = wide[:, 9 - c : 25 - c, :]
            if c == 2:
                shifted = jnp.where(inside, shifted, 0.0)
            shifted = shifted.astype(BF16)
            for a in range(3):
                lane = (3 * a + c) * O
                first, last = b * H + max(0, a - 1), b * H + H - max(0, 1 - a)
                start = max(0, 1 - a)
                cols[first:last, :, lane : lane + O] = shifted[start : start + last - first]
                if a == 0:
                    cols[b * H + H - 1, :, lane : lane + O] = jnp.zeros((16, O), BF16)
                if a == 2:
                    cols[b * H, :, lane : lane + O] = jnp.zeros((16, O), BF16)
    total = jnp.zeros((1, D), F32)
    for b in range(IMAGES):
        copies[3 + b].wait()
        total = total + jnp.sum(
            jnp.sum(features[b].astype(F32), axis=0), axis=0, keepdims=True
        )
    sums[...] = total
    mean = total * (1.0 / PIXELS)
    for b in range(IMAGES):
        xc[b * H : b * H + H, 0:W, :] = (features[b].astype(F32) - mean[None]).astype(BF16)
    high, middle, low = pieces(mean, 3)
    pad = lax.broadcasted_iota(jnp.int32, (16, D), 0)
    head = xc[0].astype(F32)
    head = jnp.where(pad == 14, high.astype(F32), jnp.where(pad == 15, middle.astype(F32), head))
    xc[0] = head.astype(BF16)
    head = xc[1].astype(F32)
    xc[1] = jnp.where(pad == 14, low.astype(F32), head).astype(BF16)
    for k in range(8):
        c, z = k // 4, k % 4
        chunk = xc[:, :, 256 * z : 256 * z + 256].reshape(ROWS, 256)
        part = nt(wp32[k].astype(BF16), chunk)
        row = 4 * (c ^ core) + (RING[c]["z"].index(z) ^ spots[c][0])
        row = pl.multiple_of(128 * row, 128)
        wht[pl.ds(row, 128), :] = part.astype(BF16)
        shift = part[:, 14:15] + part[:, 15:16] + part[:, 30:31]
        u[pl.ds(row, 128), :] = jnp.broadcast_to(shift, (128, 128))


def prep(features, grads, vectors, values):
    return pl.pallas_call(
        prep_kernel,
        out_shape=(
            jax.ShapeDtypeStruct((IMAGES * H, 16, 9 * O), BF16),
            jax.ShapeDtypeStruct((IMAGES * H, 16, D), BF16),
            jax.ShapeDtypeStruct((1040, ROWS), BF16),
            jax.ShapeDtypeStruct((1024, 128), F32),
            jax.ShapeDtypeStruct((1, D), F32),
            jax.ShapeDtypeStruct((4, 256, 256), BF16),
        ),
        in_specs=[IN_HBM] * 4,
        out_specs=(ON_CHIP,) * 6,
        scratch_shapes=[
            pltpu.VMEM((H, 32, O), F32),
            pltpu.VMEM((8, 128, 256), F32),
            pltpu.VMEM((IMAGES, H, W, D), BF16),
            pltpu.VMEM((IMAGES, H, W, O), BF16),
            pltpu.VMEM((16, 64, 64), F32),
            pltpu.VMEM((16, 64), F32),
            pltpu.SemaphoreType.DMA((3 + IMAGES,)),
        ],
        compiler_params=pltpu.CompilerParams(vmem_limit_bytes=10 << 20),
        name="prep",
    )(features, grads, vectors, values)


def weight_kernel(a, wht, cols, u, kernel_hbm, keep, send, colsum, slab, arrived):
    copy = pltpu.make_async_copy(kernel_hbm.at[pl.ds(768 * a, 768)], slab, arrived)
    copy.start()
    for n in range(3):
        start = 768 * a + 256 * n
        full = nn(wht[...], cols[:, start : start + 256])
        colsum[:, 256 * n : 256 * n + 256] = full[1024:1032, :]
        for k in range(2):
            ones = full[1024:1025, 128 * k : 128 * k + 128]
            lanes = slice(256 * n + 128 * k, 256 * n + 128 * k + 128)
            part = full[0:1024, 128 * k : 128 * k + 128] + u[...] * ones
            keep[:, lanes] = part[0:512]
            send[:, lanes] = part[512:1024]
    copy.wait()


def weight_part(wht, cols, u, kernel, a):
    return pl.pallas_call(
        functools.partial(weight_kernel, a),
        in_specs=[ON_CHIP] * 3 + [IN_HBM],
        out_specs=(ON_CHIP,) * 4,
        out_shape=(
            jax.ShapeDtypeStruct((512, 768), F32),
            jax.ShapeDtypeStruct((512, 768), F32),
            jax.ShapeDtypeStruct((8, 768), F32),
            jax.ShapeDtypeStruct((768, D), BF16),
        ),
        scratch_shapes=[pltpu.SemaphoreType.DMA],
        compiler_params=pltpu.CompilerParams(vmem_limit_bytes=6 << 20),
        name=f"weight_part_{a}",
    )(wht, cols, u, kernel)


def back_kernel(
    cols,
    slab0,
    slab1,
    slab2,
    xc,
    sums,
    sum0,
    sum1,
    sum2,
    vectors,
    values,
    dev,
    own,
    mine,
    theirs,
    bases,
    factors,
    blocks,
    tails,
):
    same = same_group()
    real = (lax.broadcasted_iota(jnp.int32, (ROWS, 256), 0) & 15) < W
    group = lax.broadcasted_iota(jnp.int32, (64, 256), 1) >> 6
    below = lax.broadcasted_iota(jnp.int32, (64, 256), 0) - (
        lax.broadcasted_iota(jnp.int32, (64, 256), 1) & 63
    )
    row = lax.broadcasted_iota(jnp.int32, (8, 256), 0)
    upper = None
    for z in range(4):
        lanes = slice(256 * z, 256 * z + 256)
        back = nn(cols[:, 0:768], slab0[:, lanes])
        back = back + nn(cols[:, 768:1536], slab1[:, lanes])
        back = back + nn(cols[:, 1536:2304], slab2[:, lanes])
        total = jnp.sum(back, axis=0, keepdims=True)
        low = jnp.where(real, back - total * (1.0 / PIXELS), 0.0).astype(BF16)
        dev[:, lanes] = low
        tails[z : z + 1, :] = total
    for z in range(4):
        lanes = slice(256 * z, 256 * z + 256)
        total = tails[z : z + 1, :]
        value = value_row(values, z)
        scale, root = lax.rsqrt(value), jnp.sqrt(value)
        tall = columns_of([sums[:, lanes] * (1.0 / PIXELS), scale, root])
        cov = tn(xc[:, lanes], dev[:, lanes]) + tall[:, 0:1] * total
        cov = 0.5 * (cov + cov.T)
        packed = cov[0:64]
        for k in range(1, 4):
            packed = jnp.where(group == k, cov[64 * k : 64 * k + 64], packed)
        if z % 2 == 0:
            upper = packed
        else:
            blocks[z // 2, 0:64, :] = jnp.where(below <= 0, upper, packed)
        diagonal = jnp.sum(jnp.where(below == 0, packed, 0.0), axis=0, keepdims=True)
        tail = jnp.where(row == 0, total, jnp.where(row == 1, sums[:, lanes], 0.0))
        tail = jnp.where(row == 5, diagonal, tail)
        if z < 3:
            for a, part in enumerate((sum0, sum1, sum2)):
                tail = jnp.where(row == 2 + a, part[0:1, lanes], tail)
        own[:, lanes] = tail
        blocks[z // 2, 64 + 8 * (z % 2) : 72 + 8 * (z % 2), :] = tail
        basis = block_vectors(vectors, z, same)
        for k, piece in enumerate(pieces(basis, 2) + pieces(basis.T, 2)):
            bases[z, k] = piece
        factor = -(tall[:, 1:2] * scale) / (tall[:, 2:3] + root)
        factors[z] = jnp.where(same, factor, 0.0)
    core = lax.axis_index("c")
    mine[...] = blocks[core]
    theirs[...] = blocks[1 - core]


def back_part(cols, slabs, xc, sums, colsums, vectors, values):
    return pl.pallas_call(
        back_kernel,
        in_specs=[ON_CHIP] * 11,
        out_specs=(ON_CHIP,) * 6,
        out_shape=(
            jax.ShapeDtypeStruct((ROWS, D), BF16),
            jax.ShapeDtypeStruct((8, D), F32),
            jax.ShapeDtypeStruct((80, 256), F32),
            jax.ShapeDtypeStruct((80, 256), F32),
            jax.ShapeDtypeStruct((4, 4, 256, 256), BF16),
            jax.ShapeDtypeStruct((4, 256, 256), F32),
        ),
        scratch_shapes=[pltpu.VMEM((2, 80, 256), F32), pltpu.VMEM((8, 256), F32)],
        compiler_params=pltpu.CompilerParams(vmem_limit_bytes=14 << 20),
        name="back_part",
    )(cols, *slabs, xc, sums, *colsums, vectors, values)


def final_kernel(
    dev,
    xc,
    mine,
    theirs,
    own,
    bases,
    factors,
    whiten,
    out,
    fix,
    blocks,
    shift,
    sigma,
    row_vector,
    done,
    sent,
):
    core = lax.axis_index("c")
    blocks[core] = mine[...]
    blocks[1 - core] = theirs[...]
    below = (lax.broadcasted_iota(jnp.int32, (256, 256), 0) & 63) - (
        lax.broadcasted_iota(jnp.int32, (256, 256), 1) & 63
    )
    every = range(4)
    chunk = [slice(256 * z, 256 * z + 256) for z in every]
    total, mean, covs = [], [], []
    for z in every:
        start = 64 + 8 * (z % 2)
        tail = blocks[z // 2, start : start + 8, :]
        total.append(tail[0:1])
        mean.append(tail[1:2] * (1.0 / TOTAL))
        packed = blocks[z // 2, 0:64, :]
        square = jnp.concatenate([packed, packed, packed, packed], axis=0)
        if z % 2 == 0:
            raw = jnp.where(below <= 0, square, square.T)
        else:
            raw = jnp.where(below > 0, square, square.T)
            raw = jnp.where(below == 0, blocks[z // 2, start + 5 : start + 6, :], raw)
        tall = columns_of([total[z], mean[z]])
        covs.append(raw - 0.5 * (tall[:, 1:2] * total[z] + tall[:, 0:1] * mean[z]))
    basis = [(bases[z, 0], bases[z, 1]) for z in every]
    turned = [(bases[z, 2], bases[z, 3]) for z in every]
    grads = [fine(nn, covs[z], basis[z]) for z in every]
    grads = [fine(nn, turned[z], grads[z]) * factors[z] for z in every]
    grads = [fine(nn, grads[z], turned[z]) for z in every]
    grads = [fine(nn, basis[z], grads[z]) for z in every]
    for z in every:
        sigma[z] = (grads[z] * (2.0 / TOTAL)).astype(BF16)
    for z in every:
        lanes = chunk[z]
        moved = own[0:1, lanes] * (1.0 / PIXELS) - total[z] * (1.0 / TOTAL)
        offset = own[1:2, lanes] * (1.0 / PIXELS) - mean[z]
        empty = [jnp.zeros((1, 256), BF16)]
        stacked = jnp.concatenate(pieces(moved, 3) + pieces(mean[z], 3) + empty * 2, axis=0)
        through = nn(stacked, whiten[z])
        stacked = jnp.concatenate(pieces(offset, 3) + empty * 5, axis=0)
        other = nn(stacked, sigma[z])
        row_vector[0:1, lanes] = jnp.sum(through[0:3], axis=0, keepdims=True) + jnp.sum(
            other[0:3], axis=0, keepdims=True
        )
        shift[0:1, lanes] = jnp.sum(through[3:6], axis=0, keepdims=True)
    first = 8 * sum(STRIDE[axis] * lax.axis_index(axis) for axis in ALL)
    lane = lax.broadcasted_iota(jnp.int32, (8, D), 1)
    row = lax.broadcasted_iota(jnp.int32, (8, D), 0)
    chosen = jnp.where(lane == row + first, shift[...], 0.0)
    chosen = jnp.sum(chosen, axis=1, keepdims=True)
    for a in range(3):
        for z in range(3):
            start = 66 + 8 * (z % 2) + a
            fix[a, :, 256 * z : 256 * z + 256] = chosen * blocks[z // 2, start : start + 1, :]
    copies = []
    for b in range(IMAGES):
        rows = slice(H * 16 * b, H * 16 * b + H * 16)
        for z in range(4):
            lanes = slice(256 * z, 256 * z + 256)
            result = nn(dev[rows, lanes], whiten[z]) + nn(xc[rows, lanes], sigma[z])
            result = result + row_vector[0:1, lanes]
            done[b, :, :, lanes] = result.astype(BF16).reshape(H, 16, 256)[:, 0:W, :]
        copies.append(pltpu.make_async_copy(done.at[b], out.at[b], sent.at[b]))
        copies[-1].start()
    for copy in copies:
        copy.wait()


def final_part(dev, xc, mine, theirs, own, bases, factors, whiten):
    return pl.pallas_call(
        final_kernel,
        in_specs=[ON_CHIP] * 8,
        out_specs=(IN_HBM, ON_CHIP),
        out_shape=(
            jax.ShapeDtypeStruct((IMAGES, H, W, D), BF16),
            jax.ShapeDtypeStruct((3, 8, 768), F32),
        ),
        scratch_shapes=[
            pltpu.VMEM((2, 80, 256), F32),
            pltpu.VMEM((1, D), F32),
            pltpu.VMEM((4, 256, 256), BF16),
            pltpu.VMEM((1, D), F32),
            pltpu.VMEM((IMAGES, H, W, D), BF16),
            pltpu.SemaphoreType.DMA((IMAGES,)),
        ],
        compiler_params=pltpu.CompilerParams(vmem_limit_bytes=12 << 20),
        name="final_part",
    )(dev, xc, mine, theirs, own, bases, factors, whiten)


def permutation(move):
    pairs = []
    for device in range(128):
        at = {k: (device // STRIDE[k]) % SIZE[k] for k in ALL}
        move(at)
        pairs.append((device, sum(at[k] * STRIDE[k] for k in ALL)))
    return pairs


def exchange(value, move):
    return lax.ppermute(value, ALL, permutation(move))


def other_core(at):
    at["c"] ^= 1


def ring(axis, step):
    def move(at):
        at[axis] ^= (1, 3)[(step + at["c"] + FLIP[axis]) % 2]

    return move


def halves(value, dim):
    pick = lambda k: lax.index_in_dim(value, k, dim, keepdims=False)
    return pick(0), pick(1)


def local(features, grads, kernel, vectors, values):
    stay = lambda array: pltpu.with_memory_space_constraint(array, pltpu.HBM)
    cols, xc, wht, u, sums, whiten = prep(
        stay(features), stay(grads), stay(vectors), stay(values)
    )
    cols, xc = cols.reshape(ROWS, 9 * O), xc.reshape(ROWS, D)
    kernel = stay(kernel.reshape(9 * O, D))

    parts, colsums, slabs = [], [], []
    for a in range(3):
        keep, send, colsum, slab = weight_part(wht, cols, u, kernel, a)
        colsums.append(colsum)
        slabs.append(slab)
        parts.append((keep + exchange(send, other_core)).reshape(2, 2, 2, 2, 2, 2, 8, 768))
    cols = lax.optimization_barrier((cols, *parts))[0]
    dev, own, mine, theirs, bases, factors = back_part(
        cols, slabs, xc, sums, colsums, vectors, values
    )
    mine = mine + exchange(theirs, other_core)

    names = [["z1", "z2", "y1", "y2", "x1", "x2"] for _ in range(3)]

    def turn(k):
        for a in range(3):
            axis = "xyz"[(a + k) % 3]
            dim = names[a].index(axis + "1")
            names[a].pop(dim)
            keep, send = halves(parts[a], dim)
            parts[a] = keep + exchange(send, ring(axis, 0))

    moves = [ring(axis, step) for axis in "xyz" for step in range(2)]

    def after(value, *others):
        return lax.optimization_barrier((value, *others))[0]

    turn(0)
    mine, *parts = lax.optimization_barrier((mine, *parts))
    one = mine + exchange(mine, moves[0])
    two = one + exchange(one, moves[1])
    turn(1)
    two, *parts = lax.optimization_barrier((two, *parts))
    three = two + exchange(two, moves[2])
    four = three + exchange(three, moves[3])
    turn(2)
    share = after(jnp.stack(parts, axis=3), four)
    five = four + exchange(four, moves[4])
    order = ["z", "y", "x"]
    for axis in "xyz":
        if axis == "y":
            share = after(share, five)
            six = after(five, share)
            six = six + exchange(six, moves[5])
        dim = order.index(axis)
        order.pop(dim)
        keep, send = halves(share, dim)
        share = keep + exchange(send, ring(axis, 1))
    mine, theirs = six, exchange(six, other_core)

    input_grad, fix = final_part(dev, xc, mine, theirs, own, bases, factors, whiten)
    kernel_grad = (share - fix).transpose(1, 0, 2).reshape(8, 3, 3, O)
    return input_grad, kernel_grad


def solution(mesh):
    finer = Mesh(mesh.devices.reshape(4, 4, 2, 4), ALL)
    split_all = P(ALL, None, None, None)
    return jax.shard_map(
        local,
        mesh=finer,
        in_specs=(split_all, split_all, P(), P(), P()),
        out_specs=(split_all, split_all),
        check_vma=False,
    )
```

```python
import functools

import jax
import jax.numpy as jnp
import numpy as np
from jax import lax
from jax.experimental import pallas as pl
from jax.experimental.pallas import tpu as pltpu
from jax.sharding import Mesh
from jax.sharding import PartitionSpec as P

ALL = ("z", "y", "c", "x")
SIZE = {"z": 4, "y": 4, "c": 2, "x": 4}
STRIDE = {"z": 32, "y": 8, "c": 4, "x": 1}
ORDERS = ((0, 3, 1, 2), (0, 1, 3, 2))
FLIP = {"z": 0, "y": 0, "x": 0}
RING = [{axis: ORDERS[(c + FLIP[axis]) % 2] for axis in "zyx"} for c in range(2)]
F32 = jnp.float32
BF16 = jnp.bfloat16
IMAGES, H, W, D, O = 6, 14, 14, 1024, 256
ROWS = IMAGES * H * 16
PIXELS = IMAGES * H * W
TOTAL = 128.0 * PIXELS
ON_CHIP = pl.BlockSpec(memory_space=pltpu.VMEM)
IN_HBM = pl.BlockSpec(memory_space=pltpu.HBM)


def nt(a, b):
    return lax.dot_general(
        a, b, (((1,), (1,)), ((), ())), preferred_element_type=F32
    )


def tn(a, b):
    return lax.dot_general(
        a, b, (((0,), (0,)), ((), ())), preferred_element_type=F32
    )


def nn(a, b):
    return lax.dot_general(
        a, b, (((1,), (0,)), ((), ())), preferred_element_type=F32
    )


def same_group():
    row = lax.broadcasted_iota(jnp.int32, (256, 256), 0)
    col = lax.broadcasted_iota(jnp.int32, (256, 256), 1)
    return (row >> 6) == (col >> 6)


def block_vectors(vectors, z, same):
    four = vectors[4 * z : 4 * z + 4].reshape(256, 64)
    return jnp.where(same, jnp.concatenate([four, four, four, four], axis=1), 0.0)


def value_row(values, z):
    return jnp.concatenate([values[4 * z + g : 4 * z + g + 1, :] for g in range(4)], axis=1)


def columns_of(rows):
    rows = rows + [jnp.zeros((1, 256), F32)] * (8 - len(rows))
    return jnp.concatenate(rows, axis=0).T


def pieces(a, n):
    out = []
    for _ in range(n):
        out.append(a.astype(BF16))
        a = a - out[-1].astype(F32)
    return out


def fine(dot, a, b):
    a_high, a_low = a if isinstance(a, tuple) else pieces(a, 2)
    b_high, b_low = b if isinstance(b, tuple) else pieces(b, 2)
    return dot(a_high, b_high) + (dot(a_high, b_low) + dot(a_low, b_high))


def place():
    core = lax.axis_index("c")
    spots = ([], [])
    for axis in "zyx":
        i = lax.axis_index(axis)
        a, b = (i ^ (i >> 1)) & 1, i >> 1
        for c in range(2):
            spots[c].append(2 * a + b if (c + FLIP[axis]) % 2 == 0 else 2 * b + a)
    return core, spots


def prep_kernel(
    features_hbm,
    grads_hbm,
    vectors_hbm,
    values_hbm,
    cols,
    xc,
    wht,
    u,
    sums,
    whiten,
    wide,
    wp32,
    features,
    grads,
    vectors,
    values,
    arrived,
):
    moves = [(values_hbm, values), (vectors_hbm, vectors), (grads_hbm, grads)]
    moves += [(features_hbm.at[b], features.at[b]) for b in range(IMAGES)]
    copies = [
        pltpu.make_async_copy(source, target, arrived.at[k])
        for k, (source, target) in enumerate(moves)
    ]
    for copy in copies:
        copy.start()
    core, spots = place()
    same = same_group()
    wide[...] = jnp.zeros_like(wide)
    xc[...] = jnp.zeros_like(xc)
    wht[1024:1040, :] = jnp.ones((16, ROWS), BF16)
    copies[0].wait()
    copies[1].wait()
    for z in range(4):
        basis = block_vectors(vectors, z, same)
        scale = lax.rsqrt(value_row(values, z))
        full = fine(nt, basis * scale, basis)
        whiten[z] = full.astype(BF16)
        for c in range(2):
            at_z, at_y, at_x = spots[c]
            order = [(y, x) for y in RING[c]["y"] for x in RING[c]["x"]]
            for row, (y, x) in enumerate(order):
                channel = y * 64 + c * 32 + x * 8
                row = pl.multiple_of(8 * (row ^ (4 * at_y + at_x)), 8)
                wp32[4 * c + z, pl.ds(row, 8), :] = full[channel : channel + 8, :]
    copies[2].wait()
    inside = lax.broadcasted_iota(jnp.int32, (H, 16, O), 1) < W
    for b in range(IMAGES):
        wide[:, 8 : 8 + W, :] = grads[b].astype(F32)
        for c in range(3):
            shifted = wide[:, 9 - c : 25 - c, :]
            if c == 2:
                shifted = jnp.where(inside, shifted, 0.0)
            shifted = shifted.astype(BF16)
            for a in range(3):
                lane = (3 * a + c) * O
                first, last = b * H + max(0, a - 1), b * H + H - max(0, 1 - a)
                start = max(0, 1 - a)
                cols[first:last, :, lane : lane + O] = shifted[start : start + last - first]
                if a == 0:
                    cols[b * H + H - 1, :, lane : lane + O] = jnp.zeros((16, O), BF16)
                if a == 2:
                    cols[b * H, :, lane : lane + O] = jnp.zeros((16, O), BF16)
    total = jnp.zeros((1, D), F32)
    for b in range(IMAGES):
        copies[3 + b].wait()
        total = total + jnp.sum(
            jnp.sum(features[b].astype(F32), axis=0), axis=0, keepdims=True
        )
    sums[...] = total
    mean = total * (1.0 / PIXELS)
    for b in range(IMAGES):
        xc[b * H : b * H + H, 0:W, :] = (features[b].astype(F32) - mean[None]).astype(BF16)
    high, middle, low = pieces(mean, 3)
    pad = lax.broadcasted_iota(jnp.int32, (16, D), 0)
    head = xc[0].astype(F32)
    head = jnp.where(pad == 14, high.astype(F32), jnp.where(pad == 15, middle.astype(F32), head))
    xc[0] = head.astype(BF16)
    head = xc[1].astype(F32)
    xc[1] = jnp.where(pad == 14, low.astype(F32), head).astype(BF16)
    for k in range(8):
        c, z = k // 4, k % 4
        chunk = xc[:, :, 256 * z : 256 * z + 256].reshape(ROWS, 256)
        part = nt(wp32[k].astype(BF16), chunk)
        row = 4 * (c ^ core) + (RING[c]["z"].index(z) ^ spots[c][0])
        row = pl.multiple_of(128 * row, 128)
        wht[pl.ds(row, 128), :] = part.astype(BF16)
        shift = part[:, 14:15] + part[:, 15:16] + part[:, 30:31]
        u[pl.ds(row, 128), :] = jnp.broadcast_to(shift, (128, 128))


def prep(features, grads, vectors, values):
    return pl.pallas_call(
        prep_kernel,
        out_shape=(
            jax.ShapeDtypeStruct((IMAGES * H, 16, 9 * O), BF16),
            jax.ShapeDtypeStruct((IMAGES * H, 16, D), BF16),
            jax.ShapeDtypeStruct((1040, ROWS), BF16),
            jax.ShapeDtypeStruct((1024, 128), F32),
            jax.ShapeDtypeStruct((1, D), F32),
            jax.ShapeDtypeStruct((4, 256, 256), BF16),
        ),
        in_specs=[IN_HBM] * 4,
        out_specs=(ON_CHIP,) * 6,
        scratch_shapes=[
            pltpu.VMEM((H, 32, O), F32),
            pltpu.VMEM((8, 128, 256), F32),
            pltpu.VMEM((IMAGES, H, W, D), BF16),
            pltpu.VMEM((IMAGES, H, W, O), BF16),
            pltpu.VMEM((16, 64, 64), F32),
            pltpu.VMEM((16, 64), F32),
            pltpu.SemaphoreType.DMA((3 + IMAGES,)),
        ],
        compiler_params=pltpu.CompilerParams(vmem_limit_bytes=10 << 20),
        name="prep",
    )(features, grads, vectors, values)


def weight_kernel(a, wht, cols, u, kernel_hbm, keep, send, colsum, slab, arrived):
    copy = pltpu.make_async_copy(kernel_hbm.at[pl.ds(768 * a, 768)], slab, arrived)
    copy.start()
    for n in range(3):
        start = 768 * a + 256 * n
        full = nn(wht[...], cols[:, start : start + 256])
        colsum[:, 256 * n : 256 * n + 256] = full[1024:1032, :]
        for k in range(2):
            ones = full[1024:1025, 128 * k : 128 * k + 128]
            lanes = slice(256 * n + 128 * k, 256 * n + 128 * k + 128)
            part = full[0:1024, 128 * k : 128 * k + 128] + u[...] * ones
            keep[:, lanes] = part[0:512]
            send[:, lanes] = part[512:1024]
    copy.wait()


def weight_part(wht, cols, u, kernel, a):
    return pl.pallas_call(
        functools.partial(weight_kernel, a),
        in_specs=[ON_CHIP] * 3 + [IN_HBM],
        out_specs=(ON_CHIP,) * 4,
        out_shape=(
            jax.ShapeDtypeStruct((512, 768), F32),
            jax.ShapeDtypeStruct((512, 768), F32),
            jax.ShapeDtypeStruct((8, 768), F32),
            jax.ShapeDtypeStruct((768, D), BF16),
        ),
        scratch_shapes=[pltpu.SemaphoreType.DMA],
        compiler_params=pltpu.CompilerParams(vmem_limit_bytes=6 << 20),
        name=f"weight_part_{a}",
    )(wht, cols, u, kernel)


def back_kernel(
    cols,
    slab0,
    slab1,
    slab2,
    xc,
    sums,
    sum0,
    sum1,
    sum2,
    vectors,
    values,
    dev,
    own,
    mine,
    theirs,
    bases,
    factors,
    blocks,
    tails,
):
    same = same_group()
    real = (lax.broadcasted_iota(jnp.int32, (ROWS, 256), 0) & 15) < W
    group = lax.broadcasted_iota(jnp.int32, (64, 256), 1) >> 6
    below = lax.broadcasted_iota(jnp.int32, (64, 256), 0) - (
        lax.broadcasted_iota(jnp.int32, (64, 256), 1) & 63
    )
    row = lax.broadcasted_iota(jnp.int32, (8, 256), 0)
    upper = None
    for z in range(4):
        lanes = slice(256 * z, 256 * z + 256)
        back = nn(cols[:, 0:768], slab0[:, lanes])
        back = back + nn(cols[:, 768:1536], slab1[:, lanes])
        back = back + nn(cols[:, 1536:2304], slab2[:, lanes])
        total = jnp.sum(back, axis=0, keepdims=True)
        low = jnp.where(real, back - total * (1.0 / PIXELS), 0.0).astype(BF16)
        dev[:, lanes] = low
        tails[z : z + 1, :] = total
    for z in range(4):
        lanes = slice(256 * z, 256 * z + 256)
        total = tails[z : z + 1, :]
        value = value_row(values, z)
        scale, root = lax.rsqrt(value), jnp.sqrt(value)
        tall = columns_of([sums[:, lanes] * (1.0 / PIXELS), scale, root])
        cov = tn(xc[:, lanes], dev[:, lanes]) + tall[:, 0:1] * total
        cov = 0.5 * (cov + cov.T)
        packed = cov[0:64]
        for k in range(1, 4):
            packed = jnp.where(group == k, cov[64 * k : 64 * k + 64], packed)
        if z % 2 == 0:
            upper = packed
        else:
            blocks[z // 2, 0:64, :] = jnp.where(below <= 0, upper, packed)
        diagonal = jnp.sum(jnp.where(below == 0, packed, 0.0), axis=0, keepdims=True)
        tail = jnp.where(row == 0, total, jnp.where(row == 1, sums[:, lanes], 0.0))
        tail = jnp.where(row == 5, diagonal, tail)
        if z < 3:
            for a, part in enumerate((sum0, sum1, sum2)):
                tail = jnp.where(row == 2 + a, part[0:1, lanes], tail)
        own[:, lanes] = tail
        blocks[z // 2, 64 + 8 * (z % 2) : 72 + 8 * (z % 2), :] = tail
        basis = block_vectors(vectors, z, same)
        for k, piece in enumerate(pieces(basis, 2) + pieces(basis.T, 2)):
            bases[z, k] = piece
        factor = -(tall[:, 1:2] * scale) / (tall[:, 2:3] + root)
        factors[z] = jnp.where(same, factor, 0.0)
    core = lax.axis_index("c")
    mine[...] = blocks[core]
    theirs[...] = blocks[1 - core]


def back_part(cols, slabs, xc, sums, colsums, vectors, values):
    return pl.pallas_call(
        back_kernel,
        in_specs=[ON_CHIP] * 11,
        out_specs=(ON_CHIP,) * 6,
        out_shape=(
            jax.ShapeDtypeStruct((ROWS, D), BF16),
            jax.ShapeDtypeStruct((8, D), F32),
            jax.ShapeDtypeStruct((80, 256), F32),
            jax.ShapeDtypeStruct((80, 256), F32),
            jax.ShapeDtypeStruct((4, 4, 256, 256), BF16),
            jax.ShapeDtypeStruct((4, 256, 256), F32),
        ),
        scratch_shapes=[pltpu.VMEM((2, 80, 256), F32), pltpu.VMEM((8, 256), F32)],
        compiler_params=pltpu.CompilerParams(vmem_limit_bytes=14 << 20),
        name="back_part",
    )(cols, *slabs, xc, sums, *colsums, vectors, values)


def final_kernel(
    dev,
    xc,
    mine,
    theirs,
    own,
    bases,
    factors,
    whiten,
    out,
    fix,
    blocks,
    shift,
    sigma,
    row_vector,
    done,
    sent,
):
    core = lax.axis_index("c")
    blocks[core] = mine[...]
    blocks[1 - core] = theirs[...]
    below = (lax.broadcasted_iota(jnp.int32, (256, 256), 0) & 63) - (
        lax.broadcasted_iota(jnp.int32, (256, 256), 1) & 63
    )
    every = range(4)
    chunk = [slice(256 * z, 256 * z + 256) for z in every]
    total, mean, covs = [], [], []
    for z in every:
        start = 64 + 8 * (z % 2)
        tail = blocks[z // 2, start : start + 8, :]
        total.append(tail[0:1])
        mean.append(tail[1:2] * (1.0 / TOTAL))
        packed = blocks[z // 2, 0:64, :]
        square = jnp.concatenate([packed, packed, packed, packed], axis=0)
        if z % 2 == 0:
            raw = jnp.where(below <= 0, square, square.T)
        else:
            raw = jnp.where(below > 0, square, square.T)
            raw = jnp.where(below == 0, blocks[z // 2, start + 5 : start + 6, :], raw)
        tall = columns_of([total[z], mean[z]])
        covs.append(raw - 0.5 * (tall[:, 1:2] * total[z] + tall[:, 0:1] * mean[z]))
    basis = [(bases[z, 0], bases[z, 1]) for z in every]
    turned = [(bases[z, 2], bases[z, 3]) for z in every]
    grads = [fine(nn, covs[z], basis[z]) for z in every]
    grads = [fine(nn, turned[z], grads[z]) * factors[z] for z in every]
    grads = [fine(nn, grads[z], turned[z]) for z in every]
    grads = [fine(nn, basis[z], grads[z]) for z in every]
    for z in every:
        sigma[z] = (grads[z] * (2.0 / TOTAL)).astype(BF16)
    for z in every:
        lanes = chunk[z]
        moved = own[0:1, lanes] * (1.0 / PIXELS) - total[z] * (1.0 / TOTAL)
        offset = own[1:2, lanes] * (1.0 / PIXELS) - mean[z]
        empty = [jnp.zeros((1, 256), BF16)]
        stacked = jnp.concatenate(pieces(moved, 3) + pieces(mean[z], 3) + empty * 2, axis=0)
        through = nn(stacked, whiten[z])
        stacked = jnp.concatenate(pieces(offset, 3) + empty * 5, axis=0)
        other = nn(stacked, sigma[z])
        row_vector[0:1, lanes] = jnp.sum(through[0:3], axis=0, keepdims=True) + jnp.sum(
            other[0:3], axis=0, keepdims=True
        )
        shift[0:1, lanes] = jnp.sum(through[3:6], axis=0, keepdims=True)
    first = 8 * sum(STRIDE[axis] * lax.axis_index(axis) for axis in ALL)
    lane = lax.broadcasted_iota(jnp.int32, (8, D), 1)
    row = lax.broadcasted_iota(jnp.int32, (8, D), 0)
    chosen = jnp.where(lane == row + first, shift[...], 0.0)
    chosen = jnp.sum(chosen, axis=1, keepdims=True)
    for a in range(3):
        for z in range(3):
            start = 66 + 8 * (z % 2) + a
            fix[a, :, 256 * z : 256 * z + 256] = chosen * blocks[z // 2, start : start + 1, :]
    copies = []
    for b in range(IMAGES):
        rows = slice(H * 16 * b, H * 16 * b + H * 16)
        for z in range(4):
            lanes = slice(256 * z, 256 * z + 256)
            result = nn(dev[rows, lanes], whiten[z]) + nn(xc[rows, lanes], sigma[z])
            result = result + row_vector[0:1, lanes]
            done[b, :, :, lanes] = result.astype(BF16).reshape(H, 16, 256)[:, 0:W, :]
        copies.append(pltpu.make_async_copy(done.at[b], out.at[b], sent.at[b]))
        copies[-1].start()
    for copy in copies:
        copy.wait()


def final_part(dev, xc, mine, theirs, own, bases, factors, whiten):
    return pl.pallas_call(
        final_kernel,
        in_specs=[ON_CHIP] * 8,
        out_specs=(IN_HBM, ON_CHIP),
        out_shape=(
            jax.ShapeDtypeStruct((IMAGES, H, W, D), BF16),
            jax.ShapeDtypeStruct((3, 8, 768), F32),
        ),
        scratch_shapes=[
            pltpu.VMEM((2, 80, 256), F32),
            pltpu.VMEM((1, D), F32),
            pltpu.VMEM((4, 256, 256), BF16),
            pltpu.VMEM((1, D), F32),
            pltpu.VMEM((IMAGES, H, W, D), BF16),
            pltpu.SemaphoreType.DMA((IMAGES,)),
        ],
        compiler_params=pltpu.CompilerParams(vmem_limit_bytes=12 << 20),
        name="final_part",
    )(dev, xc, mine, theirs, own, bases, factors, whiten)


def permutation(move):
    pairs = []
    for device in range(128):
        at = {k: (device // STRIDE[k]) % SIZE[k] for k in ALL}
        move(at)
        pairs.append((device, sum(at[k] * STRIDE[k] for k in ALL)))
    return pairs


def exchange(value, move):
    return lax.ppermute(value, ALL, permutation(move))


def other_core(at):
    at["c"] ^= 1


def ring(axis, step):
    def move(at):
        at[axis] ^= (1, 3)[(step + at["c"] + FLIP[axis]) % 2]

    return move


def halves(value, dim):
    pick = lambda k: lax.index_in_dim(value, k, dim, keepdims=False)
    return pick(0), pick(1)


def local(features, grads, kernel, vectors, values):
    stay = lambda array: pltpu.with_memory_space_constraint(array, pltpu.HBM)
    cols, xc, wht, u, sums, whiten = prep(
        stay(features), stay(grads), stay(vectors), stay(values)
    )
    cols, xc = cols.reshape(ROWS, 9 * O), xc.reshape(ROWS, D)
    kernel = stay(kernel.reshape(9 * O, D))

    parts, colsums, slabs = [], [], []
    for a in range(3):
        keep, send, colsum, slab = weight_part(wht, cols, u, kernel, a)
        colsums.append(colsum)
        slabs.append(slab)
        parts.append((keep + exchange(send, other_core)).reshape(2, 2, 2, 2, 2, 2, 8, 768))
    cols = lax.optimization_barrier((cols, *parts))[0]
    dev, own, mine, theirs, bases, factors = back_part(
        cols, slabs, xc, sums, colsums, vectors, values
    )
    mine = mine + exchange(theirs, other_core)

    names = [["z1", "z2", "y1", "y2", "x1", "x2"] for _ in range(3)]

    def turn(k):
        for a in range(3):
            axis = "xyz"[(a + k) % 3]
            dim = names[a].index(axis + "1")
            names[a].pop(dim)
            keep, send = halves(parts[a], dim)
            parts[a] = keep + exchange(send, ring(axis, 0))

    moves = [ring(axis, step) for step in (1, 0) for axis in "xyz"]

    def after(value, *others):
        return lax.optimization_barrier((value, *others))[0]

    turn(0)
    mine, *parts = lax.optimization_barrier((mine, *parts))
    one = mine + exchange(mine, moves[0])
    two = one + exchange(one, moves[1])
    turn(1)
    two, *parts = lax.optimization_barrier((two, *parts))
    three = two + exchange(two, moves[2])
    four = three + exchange(three, moves[3])
    turn(2)
    share = after(jnp.stack(parts, axis=3), four)
    five = four + exchange(four, moves[4])
    order = ["z", "y", "x"]
    for axis in "xyz":
        if axis == "y":
            share = after(share, five)
            six = after(five, share)
            six = six + exchange(six, moves[5])
        dim = order.index(axis)
        order.pop(dim)
        keep, send = halves(share, dim)
        share = keep + exchange(send, ring(axis, 1))
    mine, theirs = six, exchange(six, other_core)

    input_grad, fix = final_part(dev, xc, mine, theirs, own, bases, factors, whiten)
    kernel_grad = (share - fix).transpose(1, 0, 2).reshape(8, 3, 3, O)
    return input_grad, kernel_grad


def solution(mesh):
    finer = Mesh(mesh.devices.reshape(4, 4, 2, 4), ALL)
    split_all = P(ALL, None, None, None)
    return jax.shard_map(
        local,
        mesh=finer,
        in_specs=(split_all, split_all, P(), P(), P()),
        out_specs=(split_all, split_all),
        check_vma=False,
    )
```

```python
import functools

import jax
import jax.numpy as jnp
import numpy as np
from jax import lax
from jax.experimental import pallas as pl
from jax.experimental.pallas import tpu as pltpu
from jax.sharding import Mesh
from jax.sharding import PartitionSpec as P

ALL = ("z", "y", "c", "x")
SIZE = {"z": 4, "y": 4, "c": 2, "x": 4}
STRIDE = {"z": 32, "y": 8, "c": 4, "x": 1}
ORDERS = ((0, 3, 1, 2), (0, 1, 3, 2))
FLIP = {"z": 0, "y": 0, "x": 0}
RING = [{axis: ORDERS[(c + FLIP[axis]) % 2] for axis in "zyx"} for c in range(2)]
F32 = jnp.float32
BF16 = jnp.bfloat16
IMAGES, H, W, D, O = 6, 14, 14, 1024, 256
ROWS = IMAGES * H * 16
PIXELS = IMAGES * H * W
TOTAL = 128.0 * PIXELS
ON_CHIP = pl.BlockSpec(memory_space=pltpu.VMEM)
IN_HBM = pl.BlockSpec(memory_space=pltpu.HBM)


def nt(a, b):
    return lax.dot_general(
        a, b, (((1,), (1,)), ((), ())), preferred_element_type=F32
    )


def tn(a, b):
    return lax.dot_general(
        a, b, (((0,), (0,)), ((), ())), preferred_element_type=F32
    )


def nn(a, b):
    return lax.dot_general(
        a, b, (((1,), (0,)), ((), ())), preferred_element_type=F32
    )


def same_group():
    row = lax.broadcasted_iota(jnp.int32, (256, 256), 0)
    col = lax.broadcasted_iota(jnp.int32, (256, 256), 1)
    return (row >> 6) == (col >> 6)


def block_vectors(vectors, z, same):
    four = vectors[4 * z : 4 * z + 4].reshape(256, 64)
    return jnp.where(same, jnp.concatenate([four, four, four, four], axis=1), 0.0)


def value_row(values, z):
    return jnp.concatenate([values[4 * z + g : 4 * z + g + 1, :] for g in range(4)], axis=1)


def columns_of(rows):
    rows = rows + [jnp.zeros((1, 256), F32)] * (8 - len(rows))
    return jnp.concatenate(rows, axis=0).T


def pieces(a, n):
    out = []
    for _ in range(n):
        out.append(a.astype(BF16))
        a = a - out[-1].astype(F32)
    return out


def fine(dot, a, b):
    a_high, a_low = a if isinstance(a, tuple) else pieces(a, 2)
    b_high, b_low = b if isinstance(b, tuple) else pieces(b, 2)
    return dot(a_high, b_high) + (dot(a_high, b_low) + dot(a_low, b_high))


def place():
    core = lax.axis_index("c")
    spots = ([], [])
    for axis in "zyx":
        i = lax.axis_index(axis)
        a, b = (i ^ (i >> 1)) & 1, i >> 1
        for c in range(2):
            spots[c].append(2 * a + b if (c + FLIP[axis]) % 2 == 0 else 2 * b + a)
    return core, spots


def prep_kernel(
    features_hbm,
    grads_hbm,
    vectors_hbm,
    values_hbm,
    cols,
    xc,
    wht,
    u,
    sums,
    whiten,
    wide,
    wp32,
    features,
    grads,
    vectors,
    values,
    arrived,
):
    moves = [(values_hbm, values), (vectors_hbm, vectors), (grads_hbm, grads)]
    moves += [(features_hbm.at[b], features.at[b]) for b in range(IMAGES)]
    copies = [
        pltpu.make_async_copy(source, target, arrived.at[k])
        for k, (source, target) in enumerate(moves)
    ]
    for copy in copies:
        copy.start()
    core, spots = place()
    same = same_group()
    wide[...] = jnp.zeros_like(wide)
    xc[...] = jnp.zeros_like(xc)
    wht[1024:1040, :] = jnp.ones((16, ROWS), BF16)
    copies[0].wait()
    copies[1].wait()
    for z in range(4):
        basis = block_vectors(vectors, z, same)
        scale = lax.rsqrt(value_row(values, z))
        full = fine(nt, basis * scale, basis)
        whiten[z] = full.astype(BF16)
        for c in range(2):
            at_z, at_y, at_x = spots[c]
            order = [(y, x) for y in RING[c]["y"] for x in RING[c]["x"]]
            for row, (y, x) in enumerate(order):
                channel = y * 64 + c * 32 + x * 8
                row = pl.multiple_of(8 * (row ^ (4 * at_y + at_x)), 8)
                wp32[4 * c + z, pl.ds(row, 8), :] = full[channel : channel + 8, :]
    copies[2].wait()
    inside = lax.broadcasted_iota(jnp.int32, (H, 16, O), 1) < W
    for b in range(IMAGES):
        wide[:, 8 : 8 + W, :] = grads[b].astype(F32)
        for c in range(3):
            shifted = wide[:, 9 - c : 25 - c, :]
            if c == 2:
                shifted = jnp.where(inside, shifted, 0.0)
            shifted = shifted.astype(BF16)
            for a in range(3):
                lane = (3 * a + c) * O
                first, last = b * H + max(0, a - 1), b * H + H - max(0, 1 - a)
                start = max(0, 1 - a)
                cols[first:last, :, lane : lane + O] = shifted[start : start + last - first]
                if a == 0:
                    cols[b * H + H - 1, :, lane : lane + O] = jnp.zeros((16, O), BF16)
                if a == 2:
                    cols[b * H, :, lane : lane + O] = jnp.zeros((16, O), BF16)
    total = jnp.zeros((1, D), F32)
    for b in range(IMAGES):
        copies[3 + b].wait()
        total = total + jnp.sum(
            jnp.sum(features[b].astype(F32), axis=0), axis=0, keepdims=True
        )
    sums[...] = total
    mean = total * (1.0 / PIXELS)
    for b in range(IMAGES):
        xc[b * H : b * H + H, 0:W, :] = (features[b].astype(F32) - mean[None]).astype(BF16)
    high, middle, low = pieces(mean, 3)
    pad = lax.broadcasted_iota(jnp.int32, (16, D), 0)
    head = xc[0].astype(F32)
    head = jnp.where(pad == 14, high.astype(F32), jnp.where(pad == 15, middle.astype(F32), head))
    xc[0] = head.astype(BF16)
    head = xc[1].astype(F32)
    xc[1] = jnp.where(pad == 14, low.astype(F32), head).astype(BF16)
    for k in range(8):
        c, z = k // 4, k % 4
        chunk = xc[:, :, 256 * z : 256 * z + 256].reshape(ROWS, 256)
        part = nt(wp32[k].astype(BF16), chunk)
        row = 4 * (c ^ core) + (RING[c]["z"].index(z) ^ spots[c][0])
        row = pl.multiple_of(128 * row, 128)
        wht[pl.ds(row, 128), :] = part.astype(BF16)
        shift = part[:, 14:15] + part[:, 15:16] + part[:, 30:31]
        u[pl.ds(row, 128), :] = jnp.broadcast_to(shift, (128, 128))


def prep(features, grads, vectors, values):
    return pl.pallas_call(
        prep_kernel,
        out_shape=(
            jax.ShapeDtypeStruct((IMAGES * H, 16, 9 * O), BF16),
            jax.ShapeDtypeStruct((IMAGES * H, 16, D), BF16),
            jax.ShapeDtypeStruct((1040, ROWS), BF16),
            jax.ShapeDtypeStruct((1024, 128), F32),
            jax.ShapeDtypeStruct((1, D), F32),
            jax.ShapeDtypeStruct((4, 256, 256), BF16),
        ),
        in_specs=[IN_HBM] * 4,
        out_specs=(ON_CHIP,) * 6,
        scratch_shapes=[
            pltpu.VMEM((H, 32, O), F32),
            pltpu.VMEM((8, 128, 256), F32),
            pltpu.VMEM((IMAGES, H, W, D), BF16),
            pltpu.VMEM((IMAGES, H, W, O), BF16),
            pltpu.VMEM((16, 64, 64), F32),
            pltpu.VMEM((16, 64), F32),
            pltpu.SemaphoreType.DMA((3 + IMAGES,)),
        ],
        compiler_params=pltpu.CompilerParams(vmem_limit_bytes=10 << 20),
        name="prep",
    )(features, grads, vectors, values)


def weight_kernel(a, wht, cols, u, kernel_hbm, keep, send, colsum, slab, arrived):
    copy = pltpu.make_async_copy(kernel_hbm.at[pl.ds(768 * a, 768)], slab, arrived)
    copy.start()
    for n in range(3):
        start = 768 * a + 256 * n
        full = nn(wht[...], cols[:, start : start + 256])
        colsum[:, 256 * n : 256 * n + 256] = full[1024:1032, :]
        for k in range(2):
            ones = full[1024:1025, 128 * k : 128 * k + 128]
            lanes = slice(256 * n + 128 * k, 256 * n + 128 * k + 128)
            part = full[0:1024, 128 * k : 128 * k + 128] + u[...] * ones
            keep[:, lanes] = part[0:512]
            send[:, lanes] = part[512:1024]
    copy.wait()


def weight_part(wht, cols, u, kernel, a):
    return pl.pallas_call(
        functools.partial(weight_kernel, a),
        in_specs=[ON_CHIP] * 3 + [IN_HBM],
        out_specs=(ON_CHIP,) * 4,
        out_shape=(
            jax.ShapeDtypeStruct((512, 768), F32),
            jax.ShapeDtypeStruct((512, 768), F32),
            jax.ShapeDtypeStruct((8, 768), F32),
            jax.ShapeDtypeStruct((768, D), BF16),
        ),
        scratch_shapes=[pltpu.SemaphoreType.DMA],
        compiler_params=pltpu.CompilerParams(vmem_limit_bytes=6 << 20),
        name=f"weight_part_{a}",
    )(wht, cols, u, kernel)


def back_kernel(
    cols,
    slab0,
    slab1,
    slab2,
    xc,
    sums,
    sum0,
    sum1,
    sum2,
    vectors,
    values,
    dev,
    own,
    mine,
    theirs,
    bases,
    factors,
    blocks,
    tails,
):
    same = same_group()
    real = (lax.broadcasted_iota(jnp.int32, (ROWS, 256), 0) & 15) < W
    group = lax.broadcasted_iota(jnp.int32, (64, 256), 1) >> 6
    below = lax.broadcasted_iota(jnp.int32, (64, 256), 0) - (
        lax.broadcasted_iota(jnp.int32, (64, 256), 1) & 63
    )
    row = lax.broadcasted_iota(jnp.int32, (8, 256), 0)
    upper = None
    for z in range(4):
        lanes = slice(256 * z, 256 * z + 256)
        back = nn(cols[:, 0:768], slab0[:, lanes])
        back = back + nn(cols[:, 768:1536], slab1[:, lanes])
        back = back + nn(cols[:, 1536:2304], slab2[:, lanes])
        total = jnp.sum(back, axis=0, keepdims=True)
        low = jnp.where(real, back - total * (1.0 / PIXELS), 0.0).astype(BF16)
        dev[:, lanes] = low
        tails[z : z + 1, :] = total
    for z in range(4):
        lanes = slice(256 * z, 256 * z + 256)
        total = tails[z : z + 1, :]
        value = value_row(values, z)
        scale, root = lax.rsqrt(value), jnp.sqrt(value)
        tall = columns_of([sums[:, lanes] * (1.0 / PIXELS), scale, root])
        cov = tn(xc[:, lanes], dev[:, lanes]) + tall[:, 0:1] * total
        cov = 0.5 * (cov + cov.T)
        packed = cov[0:64]
        for k in range(1, 4):
            packed = jnp.where(group == k, cov[64 * k : 64 * k + 64], packed)
        if z % 2 == 0:
            upper = packed
        else:
            blocks[z // 2, 0:64, :] = jnp.where(below <= 0, upper, packed)
        diagonal = jnp.sum(jnp.where(below == 0, packed, 0.0), axis=0, keepdims=True)
        tail = jnp.where(row == 0, total, jnp.where(row == 1, sums[:, lanes], 0.0))
        tail = jnp.where(row == 5, diagonal, tail)
        if z < 3:
            for a, part in enumerate((sum0, sum1, sum2)):
                tail = jnp.where(row == 2 + a, part[0:1, lanes], tail)
        own[:, lanes] = tail
        blocks[z // 2, 64 + 8 * (z % 2) : 72 + 8 * (z % 2), :] = tail
        basis = block_vectors(vectors, z, same)
        for k, piece in enumerate(pieces(basis, 2) + pieces(basis.T, 2)):
            bases[z, k] = piece
        factor = -(tall[:, 1:2] * scale) / (tall[:, 2:3] + root)
        factors[z] = jnp.where(same, factor, 0.0)
    core = lax.axis_index("c")
    mine[...] = blocks[core]
    theirs[...] = blocks[1 - core]


def back_part(cols, slabs, xc, sums, colsums, vectors, values):
    return pl.pallas_call(
        back_kernel,
        in_specs=[ON_CHIP] * 11,
        out_specs=(ON_CHIP,) * 6,
        out_shape=(
            jax.ShapeDtypeStruct((ROWS, D), BF16),
            jax.ShapeDtypeStruct((8, D), F32),
            jax.ShapeDtypeStruct((80, 256), F32),
            jax.ShapeDtypeStruct((80, 256), F32),
            jax.ShapeDtypeStruct((4, 4, 256, 256), BF16),
            jax.ShapeDtypeStruct((4, 256, 256), F32),
        ),
        scratch_shapes=[pltpu.VMEM((2, 80, 256), F32), pltpu.VMEM((8, 256), F32)],
        compiler_params=pltpu.CompilerParams(vmem_limit_bytes=14 << 20),
        name="back_part",
    )(cols, *slabs, xc, sums, *colsums, vectors, values)


def final_kernel(
    dev,
    xc,
    mine,
    theirs,
    own,
    bases,
    factors,
    whiten,
    out,
    fix,
    blocks,
    shift,
    sigma,
    row_vector,
    done,
    sent,
):
    core = lax.axis_index("c")
    blocks[core] = mine[...]
    blocks[1 - core] = theirs[...]
    below = (lax.broadcasted_iota(jnp.int32, (256, 256), 0) & 63) - (
        lax.broadcasted_iota(jnp.int32, (256, 256), 1) & 63
    )
    every = range(4)
    chunk = [slice(256 * z, 256 * z + 256) for z in every]
    total, mean, covs = [], [], []
    for z in every:
        start = 64 + 8 * (z % 2)
        tail = blocks[z // 2, start : start + 8, :]
        total.append(tail[0:1])
        mean.append(tail[1:2] * (1.0 / TOTAL))
        packed = blocks[z // 2, 0:64, :]
        square = jnp.concatenate([packed, packed, packed, packed], axis=0)
        if z % 2 == 0:
            raw = jnp.where(below <= 0, square, square.T)
        else:
            raw = jnp.where(below > 0, square, square.T)
            raw = jnp.where(below == 0, blocks[z // 2, start + 5 : start + 6, :], raw)
        tall = columns_of([total[z], mean[z]])
        covs.append(raw - 0.5 * (tall[:, 1:2] * total[z] + tall[:, 0:1] * mean[z]))
    basis = [(bases[z, 0], bases[z, 1]) for z in every]
    turned = [(bases[z, 2], bases[z, 3]) for z in every]
    grads = [fine(nn, covs[z], basis[z]) for z in every]
    grads = [fine(nn, turned[z], grads[z]) * factors[z] for z in every]
    grads = [fine(nn, grads[z], turned[z]) for z in every]
    grads = [fine(nn, basis[z], grads[z]) for z in every]
    for z in every:
        sigma[z] = (grads[z] * (2.0 / TOTAL)).astype(BF16)
    for z in every:
        lanes = chunk[z]
        moved = own[0:1, lanes] * (1.0 / PIXELS) - total[z] * (1.0 / TOTAL)
        offset = own[1:2, lanes] * (1.0 / PIXELS) - mean[z]
        empty = [jnp.zeros((1, 256), BF16)]
        stacked = jnp.concatenate(pieces(moved, 3) + pieces(mean[z], 3) + empty * 2, axis=0)
        through = nn(stacked, whiten[z])
        stacked = jnp.concatenate(pieces(offset, 3) + empty * 5, axis=0)
        other = nn(stacked, sigma[z])
        row_vector[0:1, lanes] = jnp.sum(through[0:3], axis=0, keepdims=True) + jnp.sum(
            other[0:3], axis=0, keepdims=True
        )
        shift[0:1, lanes] = jnp.sum(through[3:6], axis=0, keepdims=True)
    first = 8 * sum(STRIDE[axis] * lax.axis_index(axis) for axis in ALL)
    lane = lax.broadcasted_iota(jnp.int32, (8, D), 1)
    row = lax.broadcasted_iota(jnp.int32, (8, D), 0)
    chosen = jnp.where(lane == row + first, shift[...], 0.0)
    chosen = jnp.sum(chosen, axis=1, keepdims=True)
    for a in range(3):
        for z in range(3):
            start = 66 + 8 * (z % 2) + a
            fix[a, :, 256 * z : 256 * z + 256] = chosen * blocks[z // 2, start : start + 1, :]
    copies = []
    for b in range(IMAGES):
        rows = slice(H * 16 * b, H * 16 * b + H * 16)
        for z in range(4):
            lanes = slice(256 * z, 256 * z + 256)
            result = nn(dev[rows, lanes], whiten[z]) + nn(xc[rows, lanes], sigma[z])
            result = result + row_vector[0:1, lanes]
            done[b, :, :, lanes] = result.astype(BF16).reshape(H, 16, 256)[:, 0:W, :]
        copies.append(pltpu.make_async_copy(done.at[b], out.at[b], sent.at[b]))
        copies[-1].start()
    for copy in copies:
        copy.wait()


def final_part(dev, xc, mine, theirs, own, bases, factors, whiten):
    return pl.pallas_call(
        final_kernel,
        in_specs=[ON_CHIP] * 8,
        out_specs=(IN_HBM, ON_CHIP),
        out_shape=(
            jax.ShapeDtypeStruct((IMAGES, H, W, D), BF16),
            jax.ShapeDtypeStruct((3, 8, 768), F32),
        ),
        scratch_shapes=[
            pltpu.VMEM((2, 80, 256), F32),
            pltpu.VMEM((1, D), F32),
            pltpu.VMEM((4, 256, 256), BF16),
            pltpu.VMEM((1, D), F32),
            pltpu.VMEM((IMAGES, H, W, D), BF16),
            pltpu.SemaphoreType.DMA((IMAGES,)),
        ],
        compiler_params=pltpu.CompilerParams(vmem_limit_bytes=12 << 20),
        name="final_part",
    )(dev, xc, mine, theirs, own, bases, factors, whiten)


def permutation(move):
    pairs = []
    for device in range(128):
        at = {k: (device // STRIDE[k]) % SIZE[k] for k in ALL}
        move(at)
        pairs.append((device, sum(at[k] * STRIDE[k] for k in ALL)))
    return pairs


def exchange(value, move):
    return lax.ppermute(value, ALL, permutation(move))


def other_core(at):
    at["c"] ^= 1


def ring(axis, step):
    def move(at):
        at[axis] ^= (1, 3)[(step + at["c"] + FLIP[axis]) % 2]

    return move


def halves(value, dim):
    pick = lambda k: lax.index_in_dim(value, k, dim, keepdims=False)
    return pick(0), pick(1)


def local(features, grads, kernel, vectors, values):
    stay = lambda array: pltpu.with_memory_space_constraint(array, pltpu.HBM)
    cols, xc, wht, u, sums, whiten = prep(
        stay(features), stay(grads), stay(vectors), stay(values)
    )
    cols, xc = cols.reshape(ROWS, 9 * O), xc.reshape(ROWS, D)
    kernel = stay(kernel.reshape(9 * O, D))

    parts, colsums, slabs = [], [], []
    for a in range(3):
        keep, send, colsum, slab = weight_part(wht, cols, u, kernel, a)
        colsums.append(colsum)
        slabs.append(slab)
        parts.append((keep + exchange(send, other_core)).reshape(2, 2, 2, 2, 2, 2, 8, 768))
    cols = lax.optimization_barrier((cols, *parts))[0]
    dev, own, mine, theirs, bases, factors = back_part(
        cols, slabs, xc, sums, colsums, vectors, values
    )
    mine = mine + exchange(theirs, other_core)

    names = [["z1", "z2", "y1", "y2", "x1", "x2"] for _ in range(3)]

    def turn(k):
        for a in range(3):
            axis = "xyz"[(a + k) % 3]
            dim = names[a].index(axis + "1")
            names[a].pop(dim)
            keep, send = halves(parts[a], dim)
            parts[a] = keep + exchange(send, ring(axis, 0))

    moves = [ring(axis, step) for axis in "xyz" for step in range(2)]

    def after(value, *others):
        return lax.optimization_barrier((value, *others))[0]

    turn(0)
    mine, *parts = lax.optimization_barrier((mine, *parts))
    one = mine + exchange(mine, moves[0])
    two = one + exchange(one, moves[1])
    turn(1)
    two, *parts = lax.optimization_barrier((two, *parts))
    three = two + exchange(two, moves[2])
    four = three + exchange(three, moves[3])
    turn(2)
    share = after(jnp.stack(parts, axis=3), four)
    five = four + exchange(four, moves[4])
    order = ["z", "y", "x"]
    for axis in "xyz":
        if axis == "y":
            share = after(share, five)
            six = after(five, share)
            six = six + exchange(six, moves[5])
        dim = order.index(axis)
        order.pop(dim)
        keep, send = halves(share, dim)
        share = keep + exchange(send, ring(axis, 1))
    mine, theirs = six, exchange(six, other_core)

    input_grad, fix = final_part(dev, xc, mine, theirs, own, bases, factors, whiten)
    kernel_grad = (share - fix).transpose(1, 0, 2).reshape(8, 3, 3, O)
    return input_grad, kernel_grad


def solution(mesh):
    finer = Mesh(mesh.devices.reshape(4, 4, 2, 4), ALL)
    split_all = P(ALL, None, None, None)
    return jax.shard_map(
        local,
        mesh=finer,
        in_specs=(split_all, split_all, P(), P(), P()),
        out_specs=(split_all, split_all),
        check_vma=False,
    )
```

```python
import functools

import jax
import jax.numpy as jnp
import numpy as np
from jax import lax
from jax.experimental import pallas as pl
from jax.experimental.pallas import tpu as pltpu
from jax.sharding import Mesh
from jax.sharding import PartitionSpec as P

ALL = ("z", "y", "c", "x")
SIZE = {"z": 4, "y": 4, "c": 2, "x": 4}
STRIDE = {"z": 32, "y": 8, "c": 4, "x": 1}
ORDERS = ((0, 3, 1, 2), (0, 1, 3, 2))
FLIP = {"z": 0, "y": 0, "x": 0}
RING = [{axis: ORDERS[(c + FLIP[axis]) % 2] for axis in "zyx"} for c in range(2)]
F32 = jnp.float32
BF16 = jnp.bfloat16
IMAGES, H, W, D, O = 6, 14, 14, 1024, 256
ROWS = IMAGES * H * 16
PIXELS = IMAGES * H * W
TOTAL = 128.0 * PIXELS
ON_CHIP = pl.BlockSpec(memory_space=pltpu.VMEM)
IN_HBM = pl.BlockSpec(memory_space=pltpu.HBM)


def nt(a, b):
    return lax.dot_general(
        a, b, (((1,), (1,)), ((), ())), preferred_element_type=F32
    )


def tn(a, b):
    return lax.dot_general(
        a, b, (((0,), (0,)), ((), ())), preferred_element_type=F32
    )


def nn(a, b):
    return lax.dot_general(
        a, b, (((1,), (0,)), ((), ())), preferred_element_type=F32
    )


def same_group():
    row = lax.broadcasted_iota(jnp.int32, (256, 256), 0)
    col = lax.broadcasted_iota(jnp.int32, (256, 256), 1)
    return (row >> 6) == (col >> 6)


def block_vectors(vectors, z, same):
    four = vectors[4 * z : 4 * z + 4].reshape(256, 64)
    return jnp.where(same, jnp.concatenate([four, four, four, four], axis=1), 0.0)


def value_row(values, z):
    return jnp.concatenate([values[4 * z + g : 4 * z + g + 1, :] for g in range(4)], axis=1)


def columns_of(rows):
    rows = rows + [jnp.zeros((1, 256), F32)] * (8 - len(rows))
    return jnp.concatenate(rows, axis=0).T


def pieces(a, n):
    out = []
    for _ in range(n):
        out.append(a.astype(BF16))
        a = a - out[-1].astype(F32)
    return out


def fine(dot, a, b):
    a_high, a_low = a if isinstance(a, tuple) else pieces(a, 2)
    b_high, b_low = b if isinstance(b, tuple) else pieces(b, 2)
    return dot(a_high, b_high) + (dot(a_high, b_low) + dot(a_low, b_high))


def place():
    core = lax.axis_index("c")
    spots = ([], [])
    for axis in "zyx":
        i = lax.axis_index(axis)
        a, b = (i ^ (i >> 1)) & 1, i >> 1
        for c in range(2):
            spots[c].append(2 * a + b if (c + FLIP[axis]) % 2 == 0 else 2 * b + a)
    return core, spots


def prep_kernel(
    features_hbm,
    grads_hbm,
    vectors_hbm,
    values_hbm,
    kernel_hbm,
    cols,
    xc,
    wht,
    u,
    sums,
    whiten,
    kernel,
    colsum,
    wide,
    wp32,
    features,
    grads,
    vectors,
    values,
    arrived,
):
    moves = [(values_hbm, values), (vectors_hbm, vectors), (grads_hbm, grads)]
    moves += [(features_hbm.at[b], features.at[b]) for b in range(IMAGES)]
    moves += [(kernel_hbm, kernel)]
    copies = [
        pltpu.make_async_copy(source, target, arrived.at[k])
        for k, (source, target) in enumerate(moves)
    ]
    for copy in copies:
        copy.start()
    core, spots = place()
    same = same_group()
    wide[...] = jnp.zeros_like(wide)
    xc[...] = jnp.zeros_like(xc)
    wht[1024:1040, :] = jnp.ones((16, ROWS), BF16)
    copies[0].wait()
    copies[1].wait()
    for z in range(4):
        basis = block_vectors(vectors, z, same)
        scale = lax.rsqrt(value_row(values, z))
        full = fine(nt, basis * scale, basis)
        whiten[z] = full.astype(BF16)
        for c in range(2):
            at_z, at_y, at_x = spots[c]
            order = [(y, x) for y in RING[c]["y"] for x in RING[c]["x"]]
            for row, (y, x) in enumerate(order):
                channel = y * 64 + c * 32 + x * 8
                row = pl.multiple_of(8 * (row ^ (4 * at_y + at_x)), 8)
                wp32[4 * c + z, pl.ds(row, 8), :] = full[channel : channel + 8, :]
    copies[2].wait()
    inside = lax.broadcasted_iota(jnp.int32, (H, 16, O), 1) < W
    taps = [[jnp.zeros((1, O), F32)] * 3 for _ in range(3)]
    for b in range(IMAGES):
        wide[:, 8 : 8 + W, :] = grads[b].astype(F32)
        for c in range(3):
            shifted = wide[:, 9 - c : 25 - c, :]
            if c == 2:
                shifted = jnp.where(inside, shifted, 0.0)
            lines = jnp.sum(shifted, axis=1)
            every = jnp.sum(lines, axis=0, keepdims=True)
            taps[0][c] = taps[0][c] + (every - lines[0:1])
            taps[1][c] = taps[1][c] + every
            taps[2][c] = taps[2][c] + (every - lines[H - 1 : H])
            shifted = shifted.astype(BF16)
            for a in range(3):
                lane = (3 * a + c) * O
                first, last = b * H + max(0, a - 1), b * H + H - max(0, 1 - a)
                start = max(0, 1 - a)
                cols[first:last, :, lane : lane + O] = shifted[start : start + last - first]
                if a == 0:
                    cols[b * H + H - 1, :, lane : lane + O] = jnp.zeros((16, O), BF16)
                if a == 2:
                    cols[b * H, :, lane : lane + O] = jnp.zeros((16, O), BF16)
    colsum[...] = jnp.zeros_like(colsum)
    for a in range(3):
        for c in range(3):
            colsum[a : a + 1, O * c : O * c + O] = taps[a][c]
    total = jnp.zeros((1, D), F32)
    for b in range(IMAGES):
        copies[3 + b].wait()
        total = total + jnp.sum(
            jnp.sum(features[b].astype(F32), axis=0), axis=0, keepdims=True
        )
    sums[...] = total
    mean = total * (1.0 / PIXELS)
    for b in range(IMAGES):
        xc[b * H : b * H + H, 0:W, :] = (features[b].astype(F32) - mean[None]).astype(BF16)
    high, middle, low = pieces(mean, 3)
    pad = lax.broadcasted_iota(jnp.int32, (16, D), 0)
    head = xc[0].astype(F32)
    head = jnp.where(pad == 14, high.astype(F32), jnp.where(pad == 15, middle.astype(F32), head))
    xc[0] = head.astype(BF16)
    head = xc[1].astype(F32)
    xc[1] = jnp.where(pad == 14, low.astype(F32), head).astype(BF16)
    for k in range(8):
        c, z = k // 4, k % 4
        chunk = xc[:, :, 256 * z : 256 * z + 256].reshape(ROWS, 256)
        part = nt(wp32[k].astype(BF16), chunk)
        row = 4 * (c ^ core) + (RING[c]["z"].index(z) ^ spots[c][0])
        row = pl.multiple_of(128 * row, 128)
        wht[pl.ds(row, 128), :] = part.astype(BF16)
        shift = part[:, 14:15] + part[:, 15:16] + part[:, 30:31]
        u[pl.ds(row, 128), :] = jnp.broadcast_to(shift, (128, 128))
    copies[3 + IMAGES].wait()


def prep(features, grads, vectors, values, kernel):
    return pl.pallas_call(
        prep_kernel,
        out_shape=(
            jax.ShapeDtypeStruct((IMAGES * H, 16, 9 * O), BF16),
            jax.ShapeDtypeStruct((IMAGES * H, 16, D), BF16),
            jax.ShapeDtypeStruct((1040, ROWS), BF16),
            jax.ShapeDtypeStruct((1024, 128), F32),
            jax.ShapeDtypeStruct((1, D), F32),
            jax.ShapeDtypeStruct((4, 256, 256), BF16),
            jax.ShapeDtypeStruct((9 * O, D), BF16),
            jax.ShapeDtypeStruct((8, 768), F32),
        ),
        in_specs=[IN_HBM] * 5,
        out_specs=(ON_CHIP,) * 8,
        scratch_shapes=[
            pltpu.VMEM((H, 32, O), F32),
            pltpu.VMEM((8, 128, 256), F32),
            pltpu.VMEM((IMAGES, H, W, D), BF16),
            pltpu.VMEM((IMAGES, H, W, O), BF16),
            pltpu.VMEM((16, 64, 64), F32),
            pltpu.VMEM((16, 64), F32),
            pltpu.SemaphoreType.DMA((4 + IMAGES,)),
        ],
        compiler_params=pltpu.CompilerParams(vmem_limit_bytes=10 << 20),
        name="prep",
    )(features, grads, vectors, values, kernel)


def weight_kernel(a, wht, cols, u, keep, send):
    for n in range(3):
        start = 768 * a + 256 * n
        full = nn(wht[...], cols[:, start : start + 256])
        for k in range(2):
            ones = full[1024:1025, 128 * k : 128 * k + 128]
            lanes = slice(256 * n + 128 * k, 256 * n + 128 * k + 128)
            part = full[0:1024, 128 * k : 128 * k + 128] + u[...] * ones
            keep[:, lanes] = part[0:512]
            send[:, lanes] = part[512:1024]


def weight_part(wht, cols, u, a):
    return pl.pallas_call(
        functools.partial(weight_kernel, a),
        in_specs=[ON_CHIP] * 3,
        out_specs=(ON_CHIP,) * 2,
        out_shape=(
            jax.ShapeDtypeStruct((512, 768), F32),
            jax.ShapeDtypeStruct((512, 768), F32),
        ),
        compiler_params=pltpu.CompilerParams(vmem_limit_bytes=6 << 20),
        name=f"weight_part_{a}",
    )(wht, cols, u)


def back_kernel(
    cols,
    kernel,
    xc,
    sums,
    colsum,
    vectors,
    values,
    dev,
    own,
    mine,
    theirs,
    bases,
    factors,
    blocks,
    tails,
):
    same = same_group()
    real = (lax.broadcasted_iota(jnp.int32, (ROWS, 256), 0) & 15) < W
    group = lax.broadcasted_iota(jnp.int32, (64, 256), 1) >> 6
    below = lax.broadcasted_iota(jnp.int32, (64, 256), 0) - (
        lax.broadcasted_iota(jnp.int32, (64, 256), 1) & 63
    )
    row = lax.broadcasted_iota(jnp.int32, (8, 256), 0)
    upper = None
    for z in range(4):
        lanes = slice(256 * z, 256 * z + 256)
        back = nn(cols[...], kernel[:, lanes])
        total = jnp.sum(back, axis=0, keepdims=True)
        low = jnp.where(real, back - total * (1.0 / PIXELS), 0.0).astype(BF16)
        dev[:, lanes] = low
        tails[z : z + 1, :] = total
    for z in range(4):
        lanes = slice(256 * z, 256 * z + 256)
        total = tails[z : z + 1, :]
        value = value_row(values, z)
        scale, root = lax.rsqrt(value), jnp.sqrt(value)
        tall = columns_of([sums[:, lanes] * (1.0 / PIXELS), scale, root])
        cov = tn(xc[:, lanes], dev[:, lanes]) + tall[:, 0:1] * total
        cov = 0.5 * (cov + cov.T)
        packed = cov[0:64]
        for k in range(1, 4):
            packed = jnp.where(group == k, cov[64 * k : 64 * k + 64], packed)
        if z % 2 == 0:
            upper = packed
        else:
            blocks[z // 2, 0:64, :] = jnp.where(below <= 0, upper, packed)
        diagonal = jnp.sum(jnp.where(below == 0, packed, 0.0), axis=0, keepdims=True)
        tail = jnp.where(row == 0, total, jnp.where(row == 1, sums[:, lanes], 0.0))
        tail = jnp.where(row == 5, diagonal, tail)
        if z < 3:
            for a in range(3):
                tail = jnp.where(row == 2 + a, colsum[a : a + 1, lanes], tail)
        own[:, lanes] = tail
        blocks[z // 2, 64 + 8 * (z % 2) : 72 + 8 * (z % 2), :] = tail
        basis = block_vectors(vectors, z, same)
        for k, piece in enumerate(pieces(basis, 2) + pieces(basis.T, 2)):
            bases[z, k] = piece
        factor = -(tall[:, 1:2] * scale) / (tall[:, 2:3] + root)
        factors[z] = jnp.where(same, factor, 0.0)
    core = lax.axis_index("c")
    mine[...] = blocks[core]
    theirs[...] = blocks[1 - core]


def back_part(cols, kernel, xc, sums, colsum, vectors, values):
    return pl.pallas_call(
        back_kernel,
        in_specs=[ON_CHIP] * 7,
        out_specs=(ON_CHIP,) * 6,
        out_shape=(
            jax.ShapeDtypeStruct((ROWS, D), BF16),
            jax.ShapeDtypeStruct((8, D), F32),
            jax.ShapeDtypeStruct((80, 256), F32),
            jax.ShapeDtypeStruct((80, 256), F32),
            jax.ShapeDtypeStruct((4, 4, 256, 256), BF16),
            jax.ShapeDtypeStruct((4, 256, 256), F32),
        ),
        scratch_shapes=[pltpu.VMEM((2, 80, 256), F32), pltpu.VMEM((8, 256), F32)],
        compiler_params=pltpu.CompilerParams(vmem_limit_bytes=14 << 20),
        name="back_part",
    )(cols, kernel, xc, sums, colsum, vectors, values)


def final_kernel(
    dev,
    xc,
    mine,
    theirs,
    own,
    bases,
    factors,
    whiten,
    out,
    fix,
    blocks,
    shift,
    sigma,
    row_vector,
    done,
    sent,
):
    core = lax.axis_index("c")
    blocks[core] = mine[...]
    blocks[1 - core] = theirs[...]
    below = (lax.broadcasted_iota(jnp.int32, (256, 256), 0) & 63) - (
        lax.broadcasted_iota(jnp.int32, (256, 256), 1) & 63
    )
    every = range(4)
    chunk = [slice(256 * z, 256 * z + 256) for z in every]
    total, mean, covs = [], [], []
    for z in every:
        start = 64 + 8 * (z % 2)
        tail = blocks[z // 2, start : start + 8, :]
        total.append(tail[0:1])
        mean.append(tail[1:2] * (1.0 / TOTAL))
        packed = blocks[z // 2, 0:64, :]
        square = jnp.concatenate([packed, packed, packed, packed], axis=0)
        if z % 2 == 0:
            raw = jnp.where(below <= 0, square, square.T)
        else:
            raw = jnp.where(below > 0, square, square.T)
            raw = jnp.where(below == 0, blocks[z // 2, start + 5 : start + 6, :], raw)
        tall = columns_of([total[z], mean[z]])
        covs.append(raw - 0.5 * (tall[:, 1:2] * total[z] + tall[:, 0:1] * mean[z]))
    basis = [(bases[z, 0], bases[z, 1]) for z in every]
    turned = [(bases[z, 2], bases[z, 3]) for z in every]
    grads = [fine(nn, covs[z], basis[z]) for z in every]
    grads = [fine(nn, turned[z], grads[z]) * factors[z] for z in every]
    grads = [fine(nn, grads[z], turned[z]) for z in every]
    grads = [fine(nn, basis[z], grads[z]) for z in every]
    for z in every:
        sigma[z] = (grads[z] * (2.0 / TOTAL)).astype(BF16)
    for z in every:
        lanes = chunk[z]
        moved = own[0:1, lanes] * (1.0 / PIXELS) - total[z] * (1.0 / TOTAL)
        offset = own[1:2, lanes] * (1.0 / PIXELS) - mean[z]
        empty = [jnp.zeros((1, 256), BF16)]
        stacked = jnp.concatenate(pieces(moved, 3) + pieces(mean[z], 3) + empty * 2, axis=0)
        through = nn(stacked, whiten[z])
        stacked = jnp.concatenate(pieces(offset, 3) + empty * 5, axis=0)
        other = nn(stacked, sigma[z])
        row_vector[0:1, lanes] = jnp.sum(through[0:3], axis=0, keepdims=True) + jnp.sum(
            other[0:3], axis=0, keepdims=True
        )
        shift[0:1, lanes] = jnp.sum(through[3:6], axis=0, keepdims=True)
    first = 8 * sum(STRIDE[axis] * lax.axis_index(axis) for axis in ALL)
    lane = lax.broadcasted_iota(jnp.int32, (8, D), 1)
    row = lax.broadcasted_iota(jnp.int32, (8, D), 0)
    chosen = jnp.where(lane == row + first, shift[...], 0.0)
    chosen = jnp.sum(chosen, axis=1, keepdims=True)
    for a in range(3):
        for z in range(3):
            start = 66 + 8 * (z % 2) + a
            fix[a, :, 256 * z : 256 * z + 256] = chosen * blocks[z // 2, start : start + 1, :]
    copies = []
    for b in range(IMAGES):
        rows = slice(H * 16 * b, H * 16 * b + H * 16)
        for z in range(4):
            lanes = slice(256 * z, 256 * z + 256)
            result = nn(dev[rows, lanes], whiten[z]) + nn(xc[rows, lanes], sigma[z])
            result = result + row_vector[0:1, lanes]
            done[b, :, :, lanes] = result.astype(BF16).reshape(H, 16, 256)[:, 0:W, :]
        copies.append(pltpu.make_async_copy(done.at[b], out.at[b], sent.at[b]))
        copies[-1].start()
    for copy in copies:
        copy.wait()


def final_part(dev, xc, mine, theirs, own, bases, factors, whiten):
    return pl.pallas_call(
        final_kernel,
        in_specs=[ON_CHIP] * 8,
        out_specs=(IN_HBM, ON_CHIP),
        out_shape=(
            jax.ShapeDtypeStruct((IMAGES, H, W, D), BF16),
            jax.ShapeDtypeStruct((3, 8, 768), F32),
        ),
        scratch_shapes=[
            pltpu.VMEM((2, 80, 256), F32),
            pltpu.VMEM((1, D), F32),
            pltpu.VMEM((4, 256, 256), BF16),
            pltpu.VMEM((1, D), F32),
            pltpu.VMEM((IMAGES, H, W, D), BF16),
            pltpu.SemaphoreType.DMA((IMAGES,)),
        ],
        compiler_params=pltpu.CompilerParams(vmem_limit_bytes=12 << 20),
        name="final_part",
    )(dev, xc, mine, theirs, own, bases, factors, whiten)


def permutation(move):
    pairs = []
    for device in range(128):
        at = {k: (device // STRIDE[k]) % SIZE[k] for k in ALL}
        move(at)
        pairs.append((device, sum(at[k] * STRIDE[k] for k in ALL)))
    return pairs


def exchange(value, move):
    return lax.ppermute(value, ALL, permutation(move))


def other_core(at):
    at["c"] ^= 1


def ring(axis, step):
    def move(at):
        at[axis] ^= (1, 3)[(step + at["c"] + FLIP[axis]) % 2]

    return move


def halves(value, dim):
    pick = lambda k: lax.index_in_dim(value, k, dim, keepdims=False)
    return pick(0), pick(1)


def after(value, *others):
    return lax.optimization_barrier((value, *others))[0]


def local(features, grads, kernel, vectors, values):
    stay = lambda array: pltpu.with_memory_space_constraint(array, pltpu.HBM)
    cols, xc, wht, u, sums, whiten, kernel, colsum = prep(
        stay(features),
        stay(grads),
        stay(vectors),
        stay(values),
        stay(kernel.reshape(9 * O, D)),
    )
    cols, xc = cols.reshape(ROWS, 9 * O), xc.reshape(ROWS, D)
    dev, own, mine, theirs, bases, factors = back_part(
        cols, kernel, xc, sums, colsum, vectors, values
    )

    moves = [ring(axis, step) for axis in "xyz" for step in range(2)]
    names = [["z1", "z2", "y1", "y2", "x1", "x2"] for _ in range(3)]
    parts = []

    def more(k):
        totals.append(totals[-1] + exchange(totals[-1], moves[k]))

    def weights(a, ahead):
        keep, send = weight_part(after(wht, ahead), cols, u, a)
        parts.append((keep + exchange(send, other_core)).reshape(2, 2, 2, 2, 2, 2, 8, 768))

    def turn(k):
        for a in range(3):
            axis = "xyz"[(a + k) % 3]
            dim = names[a].index(axis + "1")
            names[a].pop(dim)
            keep, send = halves(parts[a], dim)
            parts[a] = keep + exchange(send, ring(axis, 0))

    totals = [mine + exchange(theirs, other_core)]
    weights(0, totals[0])
    more(0)
    weights(1, totals[1])
    weights(2, totals[1])
    more(1)
    totals[-1] = after(totals[-1], *parts)
    more(2)
    turn(0)
    totals[-1], *parts = lax.optimization_barrier((totals[-1], *parts))
    more(3)
    more(4)
    turn(1)
    totals[-1], *parts = lax.optimization_barrier((totals[-1], *parts))
    more(5)
    mine, theirs = totals[-1], exchange(totals[-1], other_core)
    turn(2)
    input_grad, fix = final_part(dev, xc, mine, theirs, own, bases, factors, whiten)
    share = after(jnp.stack(parts, axis=3), fix)
    order = ["z", "y", "x"]
    for axis in "xyz":
        dim = order.index(axis)
        order.pop(dim)
        keep, send = halves(share, dim)
        share = keep + exchange(send, ring(axis, 1))

    kernel_grad = (share - fix).transpose(1, 0, 2).reshape(8, 3, 3, O)
    return input_grad, kernel_grad


def solution(mesh):
    finer = Mesh(mesh.devices.reshape(4, 4, 2, 4), ALL)
    split_all = P(ALL, None, None, None)
    return jax.shard_map(
        local,
        mesh=finer,
        in_specs=(split_all, split_all, P(), P(), P()),
        out_specs=(split_all, split_all),
        check_vma=False,
    )
```
